32 devices in a mesh: dp: 8 (over y, x, core), head: 4 (over z).
Axes of the slice: x: 2, y: 2, z: 4, core: 2. Of those that a mesh axis runs over, the one named last changes fastest.
Arguments:
- source_ids: int32 [32, 384], P('dp'), may hold values from 0 to 32127
- target_ids: int32 [32, 128], P('dp'), may hold values from 0 to 32127
- source_lens: int32 [32], P('dp'), may hold values from 96 to 384
- target_lens: int32 [32], P('dp'), may hold values from 0 to 128, as said below
- kl_mask: int32 [32, 128], P('dp'), may hold values 0 or 1
- teacher: bfloat16 [4096, 32128], P('dp', 'head'), may hold values from -10 to 32
- embed: float32 [32128, 512], P('head', 'dp'), may hold values from -12 to 12
- attn_in: float32 [3, 3, 512, 512], P(None, None, 'dp', 'head'), may hold values from -0.25 to 0.25
- attn_out: float32 [3, 512, 512], P(None, 'head', 'dp'), may hold values from -3 to 3
- ff_in: float32 [2, 512, 2048], P(None, 'dp', 'head'), may hold values from -0.25 to 0.25
- ff_out: float32 [2, 2048, 512], P(None, 'head', 'dp'), may hold values from -0.125 to 0.125
- gains: float32 [7, 512], P(None, 'dp'), may hold values from 0.5 to 1.5
- moment_embed: float32 [32128, 512], P('head', 'dp'), may hold values from -1.1920929e-07 to 1.1920929e-07
- moment_attn_in: float32 [3, 3, 512, 512], P(None, None, 'dp', 'head'), may hold values from -2.861023e-06 to 2.861023e-06
- moment_attn_out: float32 [3, 512, 512], P(None, 'head', 'dp'), may hold values from -2.861023e-06 to 2.861023e-06
- moment_ff_in: float32 [2, 512, 2048], P(None, 'dp', 'head'), may hold values from -2.861023e-06 to 2.861023e-06
- moment_ff_out: float32 [2, 2048, 512], P(None, 'head', 'dp'), may hold values from -2.861023e-06 to 2.861023e-06
- moment_gains: float32 [7, 512], P(None, 'dp'), may hold values from -1.335144e-05 to 1.335144e-05
- second_embed: float32 [32128, 512], P('head', 'dp'), may hold values from 6.304335e-17 to 2.521734e-16
- second_attn_in: float32 [3, 3, 512, 512], P(None, None, 'dp', 'head'), may hold values from 1.681156e-14 to 6.724624e-14
- second_attn_out: float32 [3, 512, 512], P(None, 'head', 'dp'), may hold values from 1.681156e-14 to 6.724624e-14
- second_ff_in: float32 [2, 512, 2048], P(None, 'dp', 'head'), may hold values from 1.681156e-14 to 6.724624e-14
- second_ff_out: float32 [2, 2048, 512], P(None, 'head', 'dp'), may hold values from 1.681156e-14 to 6.724624e-14
- second_gains: float32 [7, 512], P(None, 'dp'), may hold values from 4.20289e-13 to 1.681156e-12
Outputs:
- total_loss: float32 [1], replicated
- grad_norm: float32 [1], replicated
- new_embed: float32 [32128, 512], P('head', 'dp')
- new_attn_in: float32 [3, 3, 512, 512], P(None, None, 'dp', 'head')
- new_attn_out: float32 [3, 512, 512], P(None, 'head', 'dp')
- new_ff_in: float32 [2, 512, 2048], P(None, 'dp', 'head')
- new_ff_out: float32 [2, 2048, 512], P(None, 'head', 'dp')
- new_gains: float32 [7, 512], P(None, 'dp')
- new_moment_embed: float32 [32128, 512], P('head', 'dp')
- new_moment_attn_in: float32 [3, 3, 512, 512], P(None, None, 'dp', 'head')
- new_moment_attn_out: float32 [3, 512, 512], P(None, 'head', 'dp')
- new_moment_ff_in: float32 [2, 512, 2048], P(None, 'dp', 'head')
- new_moment_ff_out: float32 [2, 2048, 512], P(None, 'head', 'dp')
- new_moment_gains: float32 [7, 512], P(None, 'dp')
- new_second_embed: float32 [32128, 512], P('head', 'dp')
- new_second_attn_in: float32 [3, 3, 512, 512], P(None, None, 'dp', 'head')
- new_second_attn_out: float32 [3, 512, 512], P(None, 'head', 'dp')
- new_second_ff_in: float32 [2, 512, 2048], P(None, 'dp', 'head')
- new_second_ff_out: float32 [2, 2048, 512], P(None, 'head', 'dp')
- new_second_gains: float32 [7, 512], P(None, 'dp')
The draws below stay inside these ranges and needn't reach their ends.
Inputs may be any that keep to these rules, and one draw needn't show every extreme that they name: `target_lens`: some sequences have no target tokens.
All inputs are finite; a program needn't handle non-finite values. No bound on the sum of `kl_mask` on one device may be relied on, other than what follows from the above.
Results may differ from the reference program's by a relative error of at most 0.012.
Values may be sent and summed in bfloat16 or wider, within the bound.
No kernel may reach another device: no remote copies, remote signals or barrier semaphores. Data moves between devices by JAX's collectives and lax.ppermute only.
A program may use at most 256 MiB of HBM per device.

```python
import math
import jax
import jax.numpy as jnp
import numpy as np
from jax import lax

D = 512
H = 8
DH = 64
FF = 2048
V = 32128
SRC = 384
TGT = 128
NA = 3
NG = 7
STEP_NUM = 10
HD = 512
SEQS = 32
TGT_TOK = 4096
NPARAM = 23793152


def draw_target_lens(key, part):
    first, second = jax.random.split(jax.random.fold_in(key, 7))
    empty = jax.random.randint(first, (SEQS,), 0, 4) == 0
    empty = empty.at[1].set(True)
    lengths = jax.random.randint(second, (SEQS,), TGT // 4, TGT + 1)
    lengths = lengths.at[0].set(TGT)
    empty = empty.at[0].set(False)
    return jnp.where(empty, 0, lengths).astype(jnp.int32)


def draw_teacher(key, part):
    first, second, third = jax.random.split(jax.random.fold_in(key, 11), 3)
    bulk = jnp.clip(2.0 * jax.random.normal(first, (TGT_TOK, V), jnp.float32), -10.0, 10.0)
    chosen = jax.random.randint(second, (TGT_TOK, V), 0, V) < 3
    height = jax.random.uniform(third, (TGT_TOK, V), jnp.float32, 16.0, 22.0)
    return jnp.where(chosen, bulk + height, bulk).astype(jnp.bfloat16)


def touch_ends(drawn, own_key, smallest, high):
    extent = drawn.shape
    index_at = [jax.random.randint(jax.random.fold_in(own_key, axis), (), 0, extent[axis]) for axis in range(len(extent))]
    drawn = drawn.at[tuple(index_at)].set(smallest)
    longest = extent.index(max(extent))
    index_at[longest] = (index_at[longest] + 1) % extent[longest]
    return drawn.at[tuple(index_at)].set(high)


def levels(key, extent, shards, low, top_value):
    def one(dim, shards_of):
        draws = jax.random.uniform(jax.random.fold_in(jax.random.fold_in(key, 6), dim), (shards_of,), jnp.float32, low / len(shards), top_value / len(shards))
        return jnp.repeat(jnp.exp(draws), extent[dim] // shards_of).reshape((-1,) + (1,) * (len(extent) - dim - 1))

    loudness = one(*shards[0])
    for cut in shards[1:]:
        loudness = loudness * one(*cut)
    return loudness


def rank_bounds(count, lean):
    portions = [(1 << 20) // math.isqrt(standing ** lean) + 1 for standing in range(1, count + 1)]
    width = 1 + sum(portions) // (1 << 30)
    return np.cumsum(np.array([max(1, weight // width) for weight in portions]))


def skewed_ids(rng, extent, number_of, skew):
    listing = rank_bounds(number_of, skew)
    lot = jax.random.randint(jax.random.fold_in(rng, 1), extent, 0, int(listing[number_of - 1]))
    grade = jnp.searchsorted(jnp.asarray(listing, jnp.int32), lot, side="right")
    return jax.random.permutation(jax.random.fold_in(rng, 2), number_of)[grade].astype(jnp.int32)


def gaussian(stream_key, dims, scale, reach, shards=(), dtype=jnp.bfloat16):
    entries = scale * jax.random.normal(stream_key, dims, jnp.float32)
    if shards:
        entries = entries * levels(stream_key, dims, shards, -0.22, 0.18)
    return jnp.clip(entries, -reach, reach).astype(dtype)


def setup_inputs(seed: int = 0) -> dict:
    keys = jax.random.split(jax.random.key(seed), 25)
    source_ids = touch_ends(skewed_ids(keys[0], (SEQS, SRC), V, 2), jax.random.fold_in(keys[0], 3), 0, V - 1).astype(jnp.int32)
    target_ids = touch_ends(skewed_ids(keys[1], (SEQS, TGT), V, 2), jax.random.fold_in(keys[1], 3), 0, V - 1).astype(jnp.int32)
    source_lens = touch_ends(jax.random.randint(keys[2], (SEQS,), SRC // 4, SRC + 1), jax.random.fold_in(keys[2], 1), SRC // 4, SRC).astype(jnp.int32)
    target_lens = draw_target_lens(jax.random.fold_in(keys[24], 71), 0)
    kl_mask = touch_ends((jax.random.randint(keys[4], (SEQS, TGT), 0, 4) < 3).astype(jnp.int32), jax.random.fold_in(keys[4], 1), 0, 1)
    teacher = draw_teacher(jax.random.fold_in(keys[24], 71), 0)
    embed = gaussian(keys[6], (V, D), 2.0, 12.0, ((0, 4), (1, 8)), jnp.float32)
    attn_in = gaussian(keys[7], (NA, 3, D, HD), D ** -0.5, 0.25, ((2, 8), (3, 4)), jnp.float32)
    attn_out = gaussian(keys[8], (NA, HD, D), 4 ** -0.5, 3.0, ((1, 4), (2, 8)), jnp.float32)
    ff_in = gaussian(keys[9], (2, D, FF), D ** -0.5, 0.25, ((1, 8), (2, 4)), jnp.float32)
    ff_out = gaussian(keys[10], (2, FF, D), FF ** -0.5, 0.125, ((1, 4), (2, 8)), jnp.float32)
    gains = jnp.clip(1.0 + 0.1 * jax.random.normal(keys[11], (NG, D), jnp.float32), 0.5, 1.5)
    moment_embed = gaussian(keys[12], (V, D), (0.0001 / NPARAM ** 0.5), 1.1920928955078125e-07, ((0, 4), (1, 8)), jnp.float32)
    moment_attn_in = gaussian(keys[13], (NA, 3, D, HD), (0.0022 / NPARAM ** 0.5), 2.86102294921875e-06, ((2, 8), (3, 4)), jnp.float32)
    moment_attn_out = gaussian(keys[14], (NA, HD, D), (0.0022 / NPARAM ** 0.5), 2.86102294921875e-06, ((1, 4), (2, 8)), jnp.float32)
    moment_ff_in = gaussian(keys[15], (2, D, FF), (0.0022 / NPARAM ** 0.5), 2.86102294921875e-06, ((1, 8), (2, 4)), jnp.float32)
    moment_ff_out = gaussian(keys[16], (2, FF, D), (0.0022 / NPARAM ** 0.5), 2.86102294921875e-06, ((1, 4), (2, 8)), jnp.float32)
    moment_gains = gaussian(keys[17], (NG, D), (0.011 / NPARAM ** 0.5), 1.33514404296875e-05, ((1, 8),), jnp.float32)
    second_embed = jnp.clip(jnp.exp(math.log(2.5217340804018916e-16) - 1.3862944 * jax.random.uniform(keys[18], (V, D), jnp.float32) ** levels(keys[18], (V, D), ((0, 4), (1, 8)), -0.2, 0.2)), 6.304335201004729e-17, 2.5217340804018916e-16)
    second_attn_in = jnp.clip(jnp.exp(math.log(6.724623706185276e-14) - 1.3862944 * jax.random.uniform(keys[19], (NA, 3, D, HD), jnp.float32) ** levels(keys[19], (NA, 3, D, HD), ((2, 8), (3, 4)), -0.2, 0.2)), 1.681155926546319e-14, 6.724623706185276e-14)
    second_attn_out = jnp.clip(jnp.exp(math.log(6.724623706185276e-14) - 1.3862944 * jax.random.uniform(keys[20], (NA, HD, D), jnp.float32) ** levels(keys[20], (NA, HD, D), ((1, 4), (2, 8)), -0.2, 0.2)), 1.681155926546319e-14, 6.724623706185276e-14)
    second_ff_in = jnp.clip(jnp.exp(math.log(6.724623706185276e-14) - 1.3862944 * jax.random.uniform(keys[21], (2, D, FF), jnp.float32) ** levels(keys[21], (2, D, FF), ((1, 8), (2, 4)), -0.2, 0.2)), 1.681155926546319e-14, 6.724623706185276e-14)
    second_ff_out = jnp.clip(jnp.exp(math.log(6.724623706185276e-14) - 1.3862944 * jax.random.uniform(keys[22], (2, FF, D), jnp.float32) ** levels(keys[22], (2, FF, D), ((1, 4), (2, 8)), -0.2, 0.2)), 1.681155926546319e-14, 6.724623706185276e-14)
    second_gains = jnp.clip(jnp.exp(math.log(1.681155973980164e-12) - 1.3862944 * jax.random.uniform(keys[23], (NG, D), jnp.float32) ** levels(keys[23], (NG, D), ((1, 8),), -0.2, 0.2)), 4.20288993495041e-13, 1.681155973980164e-12)
    return {"source_ids": source_ids, "target_ids": target_ids, "source_lens": source_lens, "target_lens": target_lens, "kl_mask": kl_mask, "teacher": teacher, "embed": embed, "attn_in": attn_in, "attn_out": attn_out, "ff_in": ff_in, "ff_out": ff_out, "gains": gains, "moment_embed": moment_embed, "moment_attn_in": moment_attn_in, "moment_attn_out": moment_attn_out, "moment_ff_in": moment_ff_in, "moment_ff_out": moment_ff_out, "moment_gains": moment_gains, "second_embed": second_embed, "second_attn_in": second_attn_in, "second_attn_out": second_attn_out, "second_ff_in": second_ff_in, "second_ff_out": second_ff_out, "second_gains": second_gains}


@jax.custom_vjp
def low(v):
    return lax.optimization_barrier(v.astype(jnp.bfloat16)).astype(jnp.float32)

@jax.custom_vjp
def low_back(v):
    return v

def low_keep(v):
    return (low(v), None)

def low_pass(kept, grad):
    return (grad,)

def back_keep(v):
    return (v, None)

def back_low(kept, grad):
    return (low(grad),)
low.defvjp(low_keep, low_pass)
low_back.defvjp(back_keep, back_low)
HIGHEST = lax.Precision.HIGHEST
NORM_EPS = 1e-06
SOFTEN_FACTOR = 2.0
DIVERGENCE_SCALE = 1.0
CLIP_NORM = 0.02
BETA_ONE = 0.9
BETA_TWO = 0.999
ADAM_EPS = 1e-08
WEIGHT_DECAY = 0.01
LEARN_RATE = 0.3
MATRIX_AXES = ((0, 1), (2, 3), (1, 2), (1, 2), (1, 2), (1,))

def rounded(value):
    return low(low_back(value))

def rmsnorm(inputs, gain_row):
    return inputs * lax.rsqrt(lax.optimization_barrier(jnp.mean(inputs * inputs, -1, keepdims=True)) + NORM_EPS) * gain_row

def attend(query_in, source, weights_in, weight_out, allowed):
    batch_size, query_len = (query_in.shape[0], query_in.shape[1])
    key_len = source.shape[1]
    query = rounded(jnp.einsum('bld,dh->blh', query_in, weights_in[0], precision=HIGHEST)).reshape(batch_size, query_len, H, DH)
    keys_all = rounded(jnp.einsum('bld,dh->blh', source, weights_in[1], precision=HIGHEST)).reshape(batch_size, key_len, H, DH)
    values = rounded(jnp.einsum('bld,dh->blh', source, weights_in[2], precision=HIGHEST)).reshape(batch_size, key_len, H, DH)
    scores = low_back(jnp.einsum('bqhe,bkhe->bhqk', query, keys_all, precision=HIGHEST) * DH ** (-0.5))
    scores = jnp.where(allowed[:, None], scores, -1000000000.0)
    probs = jax.nn.softmax(scores, -1)
    mixed = rounded(jnp.einsum('bhqk,bkhe->bqhe', low(probs), values, precision=HIGHEST)).reshape(batch_size, query_len, H * DH)
    return low_back(jnp.einsum('blh,hd->bld', mixed, weight_out, precision=HIGHEST))

def feed(inputs, weight_up, weight_down):
    hidden_pre = low_back(jnp.einsum('bld,df->blf', inputs, weight_up, precision=HIGHEST))
    return low_back(jnp.einsum('blf,fd->bld', low(jax.nn.relu(hidden_pre)), weight_down, precision=HIGHEST))

def forward(params, source_ids, target_ids, source_lens, target_lens, divergence_mask, teacher_share, real_count):
    table = low(params[0])
    w_in = low(params[1])
    w_out = low(params[2])
    w_up = low(params[3])
    w_down = low(params[4])
    gain = low(params[5])
    batch_size = source_ids.shape[0]
    src_keys = jnp.arange(SRC)[None, :] < source_lens[:, None]
    enc_allowed = jnp.broadcast_to(src_keys[:, None, :], (batch_size, SRC, SRC))
    cross_allowed = jnp.broadcast_to(src_keys[:, None, :], (batch_size, TGT, SRC))
    causal = jnp.broadcast_to((jnp.arange(TGT)[:, None] >= jnp.arange(TGT)[None, :])[None], (batch_size, TGT, TGT))
    hidden = jnp.take(table, source_ids, axis=0)
    normed = low(rmsnorm(hidden, gain[0]))
    hidden = hidden + attend(normed, normed, w_in[0], w_out[0], enc_allowed)
    hidden = hidden + feed(low(rmsnorm(hidden, gain[1])), w_up[0], w_down[0])
    encoded = low(rmsnorm(hidden, gain[2]))
    dec_ids = jnp.concatenate([jnp.zeros((batch_size, 1), jnp.int32), target_ids[:, :-1]], 1)
    dec = jnp.take(table, dec_ids, axis=0)
    normed = low(rmsnorm(dec, gain[3]))
    dec = dec + attend(normed, normed, w_in[1], w_out[1], causal)
    dec = dec + attend(low(rmsnorm(dec, gain[4])), encoded, w_in[2], w_out[2], cross_allowed)
    dec = dec + feed(low(rmsnorm(dec, gain[5])), w_up[1], w_down[1])
    final = low(rmsnorm(dec, gain[6]) * D ** (-0.5))
    student_logits = low_back(jnp.einsum('btd,vd->btv', final, table, precision=HIGHEST))
    log_student = jax.nn.log_softmax(student_logits, -1)
    label_logprob = jnp.take_along_axis(log_student, target_ids[..., None], -1)[..., 0]
    student_log_probs = jax.nn.log_softmax(student_logits / SOFTEN_FACTOR, -1)
    teacher_log_probs = jax.nn.log_softmax(teacher_share / SOFTEN_FACTOR, -1)
    divergence_value = lax.optimization_barrier(jnp.sum(jnp.exp(teacher_log_probs) * (teacher_log_probs - student_log_probs), -1))
    valid = (jnp.arange(TGT)[None, :] < target_lens[:, None]).astype(jnp.float32)
    weight_matrix = valid / (jnp.maximum(target_lens, 1).astype(jnp.float32)[:, None] * real_count)
    return jnp.sum(weight_matrix * (-label_logprob + DIVERGENCE_SCALE * SOFTEN_FACTOR * SOFTEN_FACTOR * divergence_value * divergence_mask.astype(jnp.float32)))

def reference(source_ids, target_ids, source_lens, target_lens, kl_mask, teacher, embed, attn_in, attn_out, ff_in, ff_out, gains, moment_embed, moment_attn_in, moment_attn_out, moment_ff_in, moment_ff_out, moment_gains, second_embed, second_attn_in, second_attn_out, second_ff_in, second_ff_out, second_gains):
    params = (embed, attn_in, attn_out, ff_in, ff_out, gains)
    moments = (moment_embed, moment_attn_in, moment_attn_out, moment_ff_in, moment_ff_out, moment_gains)
    seconds = (second_embed, second_attn_in, second_attn_out, second_ff_in, second_ff_out, second_gains)
    real_count = jnp.maximum(jnp.sum((target_lens > 0).astype(jnp.float32)), 1.0)
    groups = SEQS // 8

    def split(array):
        return array.reshape((groups, 8) + array.shape[1:])
    stacked = (split(source_ids), split(target_ids), split(source_lens), split(target_lens), split(kl_mask), teacher.reshape(groups, 8, TGT, V))

    def block(carry, item):
        grads, total = carry
        ids_src, ids_tgt, lens_src, lens_tgt, keep, logits_in = item

        def loss_of(*weights):
            return forward(weights, ids_src, ids_tgt, lens_src, lens_tgt, keep, logits_in.astype(jnp.float32), real_count)
        value, pull = jax.vjp(loss_of, *params)
        fresh = pull(jnp.ones((), jnp.float32))
        return ((tuple((old + new for old, new in zip(grads, fresh))), total + value), None)
    start = (tuple((jnp.zeros_like(weight_matrix) for weight_matrix in params)), jnp.zeros((), jnp.float32))
    (grads, total), unused = lax.scan(block, start, stacked)
    grad_norm = jnp.sqrt(sum((jnp.sum(grad * grad) for grad in grads)))
    clip_scale = jnp.minimum(1.0, CLIP_NORM / grad_norm)
    bias_one = 1.0 - BETA_ONE ** STEP_NUM
    bias_two = 1.0 - BETA_TWO ** STEP_NUM
    outputs = [[], [], []]
    for position in range(6):
        axes = MATRIX_AXES[position]
        weight_matrix = params[position]
        grad_now = grads[position] * clip_scale
        moment_new = BETA_ONE * moments[position] + (1 - BETA_ONE) * grad_now
        second_new = BETA_TWO * seconds[position] + (1 - BETA_TWO) * grad_now * grad_now
        update = moment_new / bias_one / (jnp.sqrt(second_new / bias_two) + ADAM_EPS) + WEIGHT_DECAY * weight_matrix
        weight_size = jnp.sqrt(lax.optimization_barrier(jnp.sum(weight_matrix * weight_matrix, axis=axes, keepdims=True)))
        update_size = jnp.sqrt(lax.optimization_barrier(jnp.sum(update * update, axis=axes, keepdims=True)))
        outputs[0].append(weight_matrix - LEARN_RATE * (weight_size / (update_size + 1e-06)) * update)
        outputs[1].append(moment_new)
        outputs[2].append(second_new)
    fresh_w, fresh_m, fresh_v = outputs
    return (total.reshape(1), grad_norm.reshape(1), fresh_w[0], fresh_w[1], fresh_w[2], fresh_w[3], fresh_w[4], fresh_w[5], fresh_m[0], fresh_m[1], fresh_m[2], fresh_m[3], fresh_m[4], fresh_m[5], fresh_v[0], fresh_v[1], fresh_v[2], fresh_v[3], fresh_v[4], fresh_v[5])
```

```python
import functools

import jax
import jax.numpy as jnp
from jax import lax
from jax.experimental import pallas as pl
from jax.experimental.pallas import tpu as pltpu
from jax.sharding import PartitionSpec as P

D = 512
DH = 64
STEP_NUM = 10

NORM_EPS = 1e-06
SOFTEN_FACTOR = 2.0
DIVERGENCE_SCALE = 1.0
CLIP_NORM = 0.02
BETA_ONE = 0.9
BETA_TWO = 0.999
ADAM_EPS = 1e-08
WEIGHT_DECAY = 0.01
LEARN_RATE = 0.3

BF = jnp.bfloat16
F32 = jnp.float32


def dp_swap(x, bit, dp):
    return lax.ppermute(x, "dp", [(i, i ^ bit) for i in range(dp)])


def head_shift(x, step, heads):
    return lax.ppermute(x, "head", [(i, (i + step) % heads) for i in range(heads)])


def gather_dp(x, dp):
    if dp == 8:
        half = x.shape[-2] // 2
        part_x = dp_swap(x, 2, dp)
        part_y = dp_swap(x, 4, dp)
        diag_a = dp_swap(part_y[..., :half, :], 2, dp)
        diag_b = dp_swap(part_x[..., half:, :], 4, dp)
        near = {0: x, 2: part_x, 4: part_y}
        parts = {}
        for r, value in near.items():
            parts[r] = value
            parts[r + 1] = dp_swap(value, 1, dp)
        parts[6] = jnp.concatenate([diag_a, diag_b], -2)
        parts[7] = jnp.concatenate([dp_swap(diag_a, 1, dp), dp_swap(diag_b, 1, dp)], -2)
        return [parts[r] for r in range(dp)]
    parts = [x]
    bit = 1
    while bit < dp:
        parts = parts + [dp_swap(p, bit, dp) for p in parts]
        bit *= 2
    return parts


def scatter_dp(parts, dp):
    if dp == 8:
        half = parts[0].shape[-2] // 2
        own, to_x, to_y, diag = (
            parts[r] + dp_swap(parts[r + 1].astype(BF), 1, dp).astype(F32) for r in (0, 2, 4, 6)
        )
        diag = diag.astype(BF)
        got_a = dp_swap(diag[..., :half, :], 2, dp).astype(F32)
        got_b = dp_swap(diag[..., half:, :], 4, dp).astype(F32)
        x_low = dp_swap(to_x[..., :half, :].astype(BF), 2, dp).astype(F32)
        y_high = dp_swap(to_y[..., half:, :].astype(BF), 4, dp).astype(F32)
        x_high = dp_swap((to_x[..., half:, :] + got_b).astype(BF), 2, dp).astype(F32)
        y_low = dp_swap((to_y[..., :half, :] + got_a).astype(BF), 4, dp).astype(F32)
        return own + jnp.concatenate([x_low + y_low, x_high + y_high], -2)
    bit = dp // 2
    while bit:
        low, high = parts[:bit], parts[bit:]
        parts = [
            keep + dp_swap(send.astype(BF), bit, dp).astype(F32)
            for keep, send in zip(low, high, strict=True)
        ]
        bit //= 2
    return parts[0]


def gather_head(x, heads):
    return [x] + [head_shift(x, heads - j, heads) for j in range(1, heads)]


def scatter_head(parts, heads):
    total = parts[0].astype(F32)
    for j in range(1, heads):
        total = total + head_shift(parts[j].astype(BF), j, heads).astype(F32)
    return total


def sum_all(x, dp, heads):
    bit = 1
    while bit < dp:
        x = x + dp_swap(x, bit, dp)
        bit *= 2
    total = x
    for j in range(1, heads):
        total = total + head_shift(x, j, heads)
    return total


def lookup_kernel(vocab, tile, ids_ref, table_ref, out_ref, acc_ref):
    step = pl.program_id(0)

    @pl.when(step == 0)
    def _():
        acc_ref[...] = jnp.zeros_like(acc_ref)

    rows = ids_ref.shape[0]
    place = step * tile + lax.broadcasted_iota(jnp.int32, (1, tile), 1)
    block = table_ref[...]
    block = jnp.where(place < vocab, block, jnp.zeros_like(block))
    hit = (ids_ref[...] == place).astype(BF)
    acc_ref[...] += lax.dot_general(
        hit, block, (((1,), (1,)), ((), ())), preferred_element_type=F32
    )

    @pl.when(step == pl.num_programs(0) - 1)
    def _():
        out_ref[...] = acc_ref[...].astype(BF)


def lookup(ids, table_t):
    rows, vocab = ids.shape[0], table_t.shape[1]
    tile = 1024
    return pl.pallas_call(
        functools.partial(lookup_kernel, vocab, tile),
        out_shape=jax.ShapeDtypeStruct((rows, D), BF),
        grid=(pl.cdiv(vocab, tile),),
        in_specs=[
            pl.BlockSpec((rows, 1), lambda i: (0, 0)),
            pl.BlockSpec((D, tile), lambda i: (0, i)),
        ],
        out_specs=pl.BlockSpec((rows, D), lambda i: (0, 0)),
        scratch_shapes=[pltpu.VMEM((rows, D), F32)],
        compiler_params=pltpu.CompilerParams(vmem_limit_bytes=48 * 2**20),
    )(ids.reshape(rows, 1), table_t)


def spread_kernel(tile, ids_ref, rows_ref, base_ref, out_ref):
    place = pl.program_id(0) * tile + lax.broadcasted_iota(jnp.int32, (1, tile), 1)
    hit = (ids_ref[...] == place).astype(BF)
    out_ref[...] = base_ref[...] + lax.dot_general(
        rows_ref[...], hit, (((0,), (0,)), ((), ())), preferred_element_type=F32
    )


def spread(ids, rows_low, base_t):
    rows, vocab = ids.shape[0], base_t.shape[1]
    tile = 512
    return pl.pallas_call(
        functools.partial(spread_kernel, tile),
        out_shape=jax.ShapeDtypeStruct(base_t.shape, F32),
        grid=(pl.cdiv(vocab, tile),),
        in_specs=[
            pl.BlockSpec((rows, 1), lambda i: (0, 0)),
            pl.BlockSpec((rows, D), lambda i: (0, 0)),
            pl.BlockSpec((D, tile), lambda i: (0, i)),
        ],
        out_specs=pl.BlockSpec((D, tile), lambda i: (0, i)),
        compiler_params=pltpu.CompilerParams(vmem_limit_bytes=48 * 2**20),
    )(ids.reshape(rows, 1), rows_low, base_t)


def normed(inputs, gain_row):
    return (
        inputs * lax.rsqrt(jnp.mean(inputs * inputs, -1, keepdims=True) + NORM_EPS) * gain_row
    ).astype(BF)


def norm_back(inputs, gain_row, upstream):
    factor = lax.rsqrt(jnp.mean(inputs * inputs, -1, keepdims=True) + NORM_EPS)
    scaled = upstream * gain_row
    inner = jnp.mean(scaled * inputs, -1, keepdims=True)
    return (
        factor * (scaled - inputs * factor * factor * inner),
        jnp.sum(upstream * inputs * factor, axis=(0, 1)),
    )


def dot(spec, a, b):
    return jnp.einsum(spec, a, b, preferred_element_type=F32)


def split_heads(array):
    return array.reshape(array.shape[0], array.shape[1], -1, DH)


def merge_heads(array):
    return array.reshape(array.shape[0], array.shape[1], -1)


def attn_probs(query, keys_all, allowed):
    scores = dot("bqhe,bkhe->bhqk", query, keys_all) * DH ** (-0.5)
    return jax.nn.softmax(jnp.where(allowed[:, None], scores, -1000000000.0), -1)


def attend_fwd(query_in, source, weights, allowed):
    query = split_heads(dot("bld,dh->blh", query_in, weights[0]).astype(BF))
    keys_all = split_heads(dot("bld,dh->blh", source, weights[1]).astype(BF))
    values = split_heads(dot("bld,dh->blh", source, weights[2]).astype(BF))
    probs = attn_probs(query, keys_all, allowed)
    mixed = merge_heads(dot("bhqk,bkhe->bqhe", probs.astype(BF), values).astype(BF))
    return dot("blh,dh->bld", mixed, weights[3]), (query, keys_all, values, mixed)


def attend_back(upstream, query_in, source, weights, allowed, kept):
    query, keys_all, values, mixed = kept
    up_low = upstream.astype(BF)
    grad_out = dot("bld,blh->dh", up_low, mixed)
    grad_mixed = split_heads(dot("bld,dh->blh", up_low, weights[3]).astype(BF))
    probs = attn_probs(query, keys_all, allowed)
    grad_probs = dot("bqhe,bkhe->bhqk", grad_mixed, values)
    grad_scores = (probs * (grad_probs - jnp.sum(grad_probs * probs, -1, keepdims=True))).astype(BF)
    grad_query = merge_heads(
        (dot("bhqk,bkhe->bqhe", grad_scores, keys_all) * DH ** (-0.5)).astype(BF)
    )
    grad_keys = merge_heads(
        (dot("bhqk,bqhe->bkhe", grad_scores, query) * DH ** (-0.5)).astype(BF)
    )
    grad_values = merge_heads(dot("bhqk,bqhe->bkhe", probs.astype(BF), grad_mixed).astype(BF))
    grads = [
        dot("bld,blh->dh", query_in, grad_query),
        dot("bld,blh->dh", source, grad_keys),
        dot("bld,blh->dh", source, grad_values),
        grad_out,
    ]
    back_query = dot("blh,dh->bld", grad_query, weights[0])
    back_source = dot("blh,dh->bld", grad_keys, weights[1])
    back_source = back_source + dot("blh,dh->bld", grad_values, weights[2])
    return back_query, back_source, grads


def feed_fwd(inputs, weights):
    hidden = jax.nn.relu(dot("bld,df->blf", inputs, weights[0])).astype(BF)
    return dot("blf,df->bld", hidden, weights[1]), hidden


def feed_back(upstream, inputs, weights, hidden):
    up_low = upstream.astype(BF)
    grad_down = dot("bld,blf->df", up_low, hidden)
    grad_hidden = dot("bld,df->blf", up_low, weights[1])
    grad_pre = jnp.where(hidden > 0, grad_hidden, 0.0).astype(BF)
    grad_up = dot("bld,blf->df", inputs, grad_pre)
    back_in = dot("blf,df->bld", grad_pre, weights[0])
    return back_in, [grad_up, grad_down]


def body(
    dp,
    heads,
    source_ids,
    target_ids,
    source_lens,
    target_lens,
    kl_mask,
    teacher,
    *state,
):
    def transposed(group):
        embed, attn_in, attn_out, ff_in, ff_out, gains = group
        swap = functools.partial(jnp.swapaxes, axis1=-1, axis2=-2)
        return (swap(embed), attn_in, swap(attn_out), ff_in, swap(ff_out), gains)

    masters = transposed(state[:6])
    moments = transposed(state[6:12])
    seconds = transposed(state[12:])
    embed_t, attn_in, attn_out_t, ff_in, ff_out_t, gains = masters
    low = embed_t.astype(BF)
    vocab_local = embed_t.shape[1]
    head_pos = lax.axis_index("head")
    lead = (head_pos == 0).astype(F32)
    vocab_start = head_pos * vocab_local
    batch_size, source_len = source_ids.shape
    target_len = target_ids.shape[1]
    token_count = batch_size * target_len
    each = -(-batch_size // heads)
    padded = each * heads

    gain_rows = gains.shape[0]
    width = attn_in.shape[-1]
    gain_block = jnp.pad(gains.T, ((0, 0), (0, width - gain_rows)))
    stacks = [
        jnp.concatenate([attn_in[0], attn_out_t[:1], gain_block[None]], 0),
        jnp.stack([ff_in[0], ff_out_t[0]]),
        jnp.concatenate([attn_in[1], attn_out_t[1:2], attn_in[2], attn_out_t[2:3]], 0),
        jnp.stack([ff_in[1], ff_out_t[1]]),
    ]
    table_t = jnp.stack(gather_dp(low, dp)).reshape(D, vocab_local)
    full = []
    for stack in stacks:
        wide = jnp.concatenate(gather_head(stack.astype(BF), heads), -1)
        full.append(jnp.concatenate(gather_dp(wide, dp), -2))
    w_enc, f_enc, w_dec, f_dec = full
    gain = w_enc[4, :, :gain_rows].T.astype(F32)
    w_self, w_cross = w_dec[:4], w_dec[4:]

    def fill(array):
        return jnp.pad(array, ((0, padded - batch_size),) + ((0, 0),) * (array.ndim - 1))

    dec_ids = jnp.concatenate([jnp.zeros((batch_size, 1), jnp.int32), target_ids[:, :-1]], 1)
    rows_each = each * (source_len + target_len)
    ids_all = jnp.concatenate(
        [
            fill(source_ids).reshape(heads, each * source_len),
            fill(dec_ids).reshape(heads, each * target_len),
        ],
        1,
    )
    ids_rel = jnp.roll(ids_all, -head_pos, 0).reshape(-1) - vocab_start
    looked = lookup(ids_rel, table_t).reshape(heads, rows_each, D)
    mine = scatter_head([looked[j] for j in range(heads)], heads)
    enc_embed = mine[: each * source_len].reshape(each, source_len, D)
    dec_embed = mine[each * source_len :].reshape(each, target_len, D)
    my_lens = lax.dynamic_slice_in_dim(fill(source_lens), head_pos * each, each)

    src_keys = jnp.arange(source_len)[None, :] < my_lens[:, None]
    enc_allowed = jnp.broadcast_to(src_keys[:, None, :], (each, source_len, source_len))
    cross_allowed = jnp.broadcast_to(src_keys[:, None, :], (each, target_len, source_len))
    causal = jnp.broadcast_to(
        (jnp.arange(target_len)[:, None] >= jnp.arange(target_len)[None, :])[None],
        (each, target_len, target_len),
    )
    norm_a = normed(enc_embed, gain[0])
    branch, kept_enc = attend_fwd(norm_a, norm_a, w_enc, enc_allowed)
    enc_mid = enc_embed + branch
    norm_b = normed(enc_mid, gain[1])
    branch, hidden_enc = feed_fwd(norm_b, f_enc)
    enc_last = enc_mid + branch
    encoded = normed(enc_last, gain[2])
    norm_c = normed(dec_embed, gain[3])
    branch, kept_self = attend_fwd(norm_c, norm_c, w_self, causal)
    dec_one = dec_embed + branch
    norm_d = normed(dec_one, gain[4])
    branch, kept_cross = attend_fwd(norm_d, encoded, w_cross, cross_allowed)
    dec_two = dec_one + branch
    norm_e = normed(dec_two, gain[5])
    branch, hidden_dec = feed_fwd(norm_e, f_dec)
    dec_three = dec_two + branch
    head_gain = gain[6] * D ** (-0.5)
    my_final = normed(dec_three, head_gain).reshape(each * target_len, D)

    final = jnp.concatenate(gather_head(my_final, heads), 0)
    final = jnp.roll(final, head_pos * each * target_len, 0)[:token_count]
    student_logits = dot("td,dv->tv", final, table_t)
    counted = jnp.sum((target_lens > 0).astype(F32)).reshape(1, 1)
    real_count = jnp.maximum(lax.psum(counted, "dp")[0, 0], 1.0)
    valid = (jnp.arange(target_len)[None, :] < target_lens[:, None]).astype(F32)
    token_weight = (
        valid / (jnp.maximum(target_lens, 1).astype(F32)[:, None] * real_count)
    ).reshape(token_count)
    divergence_mask = kl_mask.astype(F32).reshape(token_count)
    labels = target_ids.reshape(token_count) - vocab_start
    teacher_full = teacher.astype(F32)
    peak_s = jnp.max(student_logits, -1)
    peak_t = jnp.max(teacher_full, -1)
    shifted = student_logits - peak_s[:, None]
    teacher_exp = jnp.exp((teacher_full - peak_t[:, None]) / SOFTEN_FACTOR)
    local_hit = (labels[:, None] == jnp.arange(vocab_local)[None, :]).astype(F32)
    stats = jnp.stack(
        [
            peak_s,
            peak_t,
            jnp.sum(jnp.exp(shifted), -1),
            jnp.sum(jnp.exp(shifted / SOFTEN_FACTOR), -1),
            jnp.sum(teacher_exp, -1),
            jnp.sum(teacher_exp * (teacher_full - student_logits), -1) / SOFTEN_FACTOR,
            jnp.sum(local_hit * student_logits, -1),
            jnp.zeros_like(peak_s),
        ]
    )
    every = jnp.stack(gather_head(stats, heads))
    peak_student = jnp.max(every[:, 0], 0)
    peak_teacher = jnp.max(every[:, 1], 0)
    off_s = every[:, 0] - peak_student
    off_t = jnp.exp((every[:, 1] - peak_teacher) / SOFTEN_FACTOR)
    sum_one = jnp.sum(every[:, 2] * jnp.exp(off_s), 0)
    sum_half = jnp.sum(every[:, 3] * jnp.exp(off_s / SOFTEN_FACTOR), 0)
    sum_teacher = jnp.sum(every[:, 4] * off_t, 0)
    sum_cross = jnp.sum(every[:, 5] * off_t, 0)
    label_logprob = jnp.sum(every[:, 6], 0)
    lse_one = peak_student + jnp.log(sum_one)
    lse_half = peak_student / SOFTEN_FACTOR + jnp.log(sum_half)
    lse_teacher = peak_teacher / SOFTEN_FACTOR + jnp.log(sum_teacher)
    cross_entropy = lse_one - label_logprob
    divergence_value = sum_cross / sum_teacher - lse_teacher + lse_half
    loss_part = lead * jnp.sum(
        token_weight
        * (
            cross_entropy
            + DIVERGENCE_SCALE * SOFTEN_FACTOR * SOFTEN_FACTOR * divergence_value * divergence_mask
        )
    )
    grad_logits = (
        token_weight[:, None]
        * (
            jnp.exp(student_logits - lse_one[:, None])
            - local_hit
            + DIVERGENCE_SCALE
            * SOFTEN_FACTOR
            * (
                jnp.exp(student_logits / SOFTEN_FACTOR - lse_half[:, None])
                - jnp.exp(teacher_full / SOFTEN_FACTOR - lse_teacher[:, None])
            )
            * divergence_mask[:, None]
        )
    ).astype(BF)
    grad_table_t = dot("td,tv->dv", final, grad_logits)
    part = dot("tv,dv->td", grad_logits, table_t).reshape(batch_size, target_len, D)
    part = jnp.roll(
        fill(part).astype(BF).reshape(heads, each * target_len, D), -head_pos, 0
    )
    grad_final = scatter_head([part[j] for j in range(heads)], heads).reshape(each, target_len, D)

    grad_three, gain_six = norm_back(dec_three, head_gain, grad_final)
    back_in, grads_f_dec = feed_back(grad_three, norm_e, f_dec, hidden_dec)
    grad_norm_in, gain_five = norm_back(dec_two, gain[5], back_in)
    grad_two = grad_three + grad_norm_in
    back_query, grad_encoded, grads_cross = attend_back(
        grad_two, norm_d, encoded, w_cross, cross_allowed, kept_cross
    )
    grad_norm_in, gain_four = norm_back(dec_one, gain[4], back_query)
    grad_one = grad_two + grad_norm_in
    back_query, back_source, grads_self = attend_back(
        grad_one, norm_c, norm_c, w_self, causal, kept_self
    )
    grad_norm_in, gain_three = norm_back(dec_embed, gain[3], back_query + back_source)
    grad_dec_embed = grad_one + grad_norm_in
    grad_last, gain_two = norm_back(enc_last, gain[2], grad_encoded)
    back_in, grads_f_enc = feed_back(grad_last, norm_b, f_enc, hidden_enc)
    grad_norm_in, gain_one = norm_back(enc_mid, gain[1], back_in)
    grad_mid = grad_last + grad_norm_in
    back_query, back_source, grads_enc = attend_back(
        grad_mid, norm_a, norm_a, w_enc, enc_allowed, kept_enc
    )
    grad_norm_in, gain_zero = norm_back(enc_embed, gain[0], back_query + back_source)
    grad_enc_embed = grad_mid + grad_norm_in

    my_rows = jnp.concatenate(
        [grad_enc_embed.reshape(-1, D), grad_dec_embed.reshape(-1, D)], 0
    ).astype(BF)
    all_rows = jnp.concatenate(gather_head(my_rows, heads), 0)
    grad_table_t = spread(ids_rel, all_rows, grad_table_t)
    deep = D // dp
    grad_table_t = scatter_dp(
        [grad_table_t[r * deep : (r + 1) * deep] for r in range(dp)], dp
    )
    gain_grads = jnp.stack(
        [gain_zero, gain_one, gain_two, gain_three, gain_four, gain_five, gain_six * D ** (-0.5)]
    )
    gain_cols = jnp.tile(jnp.pad(gain_grads.T, ((0, 0), (0, width - gain_rows))), (1, heads))
    grad_stacks = [
        grads_f_dec,
        grads_cross,
        grads_self,
        grads_f_enc,
        grads_enc + [gain_cols],
    ]
    reduced = []
    for group in grad_stacks:
        whole = jnp.stack(group)
        shard = scatter_dp([whole[:, r * deep : (r + 1) * deep] for r in range(dp)], dp)
        wide = shard.shape[-1] // heads
        reduced.append(
            scatter_head([shard[..., j * wide : (j + 1) * wide] for j in range(heads)], heads)
        )
    r_fdec, r_cross, r_self, r_fenc, r_enc = reduced
    shards = [
        grad_table_t,
        jnp.stack([r_enc[:3], r_self[:3], r_cross[:3]]),
        jnp.stack([r_enc[3], r_self[3], r_cross[3]]),
        jnp.stack([r_fenc[0], r_fdec[0]]),
        jnp.stack([r_fenc[1], r_fdec[1]]),
        r_enc[4, :, :gain_rows].T,
    ]

    axes = ((0, 1), (2, 3), (1, 2), (1, 2), (1, 2), (1,))
    sizes = (1, 9, 3, 2, 2, gain_rows)

    def squares(arrays):
        out = []
        for position in range(6):
            value = jnp.sum(arrays[position] * arrays[position], axis=axes[position])
            out.append(value.reshape(-1) * (lead if position == 5 else 1.0))
        return out

    lanes = 128
    packed = jnp.concatenate(squares(masters) + squares(shards) + [loss_part.reshape(1)])
    count = packed.shape[0]
    totals = sum_all(jnp.pad(packed, (0, lanes - count)).reshape(1, lanes), dp, heads)[0]
    per = sum(sizes)
    grad_norm = jnp.sqrt(jnp.sum(totals[per : 2 * per]))
    total_loss = totals[2 * per]
    clip_scale = jnp.minimum(1.0, CLIP_NORM / grad_norm)
    bias_one = 1.0 - BETA_ONE**STEP_NUM
    bias_two = 1.0 - BETA_TWO**STEP_NUM
    updates, fresh_m, fresh_v = [], [], []
    for position in range(6):
        grad_now = shards[position] * clip_scale
        moment_new = BETA_ONE * moments[position] + (1 - BETA_ONE) * grad_now
        second_new = BETA_TWO * seconds[position] + (1 - BETA_TWO) * grad_now * grad_now
        update = (
            moment_new / bias_one / (jnp.sqrt(second_new / bias_two) + ADAM_EPS)
            + WEIGHT_DECAY * masters[position]
        )
        updates.append(update)
        fresh_m.append(moment_new)
        fresh_v.append(second_new)
    packed = jnp.concatenate(squares(updates))
    update_tot = sum_all(jnp.pad(packed, (0, lanes - per)).reshape(1, lanes), dp, heads)[0]
    rates = LEARN_RATE * jnp.sqrt(totals[:per]) / (jnp.sqrt(update_tot[:per]) + 1e-06)
    fresh_w = []
    start = 0
    for position in range(6):
        rate = rates[start : start + sizes[position]]
        start += sizes[position]
        shape = [1] * masters[position].ndim
        kept = [d for d in range(masters[position].ndim) if d not in axes[position]]
        for d in kept:
            shape[d] = masters[position].shape[d]
        fresh_w.append(masters[position] - rate.reshape(shape) * updates[position])
    return (
        total_loss.reshape(1),
        grad_norm.reshape(1),
        *transposed(fresh_w),
        *transposed(fresh_m),
        *transposed(fresh_v),
    )


def solution(mesh):
    params = (
        P("head", "dp"),
        P(None, None, "dp", "head"),
        P(None, "head", "dp"),
        P(None, "dp", "head"),
        P(None, "head", "dp"),
        P(None, "dp"),
    )
    return jax.shard_map(
        functools.partial(body, mesh.shape["dp"], mesh.shape["head"]),
        mesh=mesh,
        in_specs=(
            P("dp", None),
            P("dp", None),
            P("dp"),
            P("dp"),
            P("dp", None),
            P("dp", "head"),
            *params,
            *params,
            *params,
        ),
        out_specs=(P(), P(), *params, *params, *params),
        check_vma=False,
    )
```

```python
import functools

import jax
import jax.numpy as jnp
from jax import lax
from jax.experimental import pallas as pl
from jax.experimental.pallas import tpu as pltpu
from jax.sharding import PartitionSpec as P

D = 512
DH = 64
STEP_NUM = 10

NORM_EPS = 1e-06
SOFTEN_FACTOR = 2.0
DIVERGENCE_SCALE = 1.0
CLIP_NORM = 0.02
BETA_ONE = 0.9
BETA_TWO = 0.999
ADAM_EPS = 1e-08
WEIGHT_DECAY = 0.01
LEARN_RATE = 0.3

BF = jnp.bfloat16
F32 = jnp.float32


def dp_swap(x, bit, dp):
    return lax.ppermute(x, "dp", [(i, i ^ bit) for i in range(dp)])


def head_shift(x, step, heads):
    return lax.ppermute(x, "head", [(i, (i + step) % heads) for i in range(heads)])


def after(x, *earlier):
    return lax.optimization_barrier((x, *earlier))[0]


def tie(chain, *arrived):
    return lax.optimization_barrier((chain, *arrived))


class GatherDp:
    def __init__(self, x, dp):
        self.x, self.dp = x, dp
        self.rows = x.shape[0]
        self.near = (dp_swap(x, 4, dp), dp_swap(x, 2, dp)) if dp == 8 else ()
        self.far = ()

    def go_far(self):
        if self.dp == 8:
            half = self.rows // 2
            part_y, part_x = self.near
            self.far = (dp_swap(part_y[:half], 2, self.dp), dp_swap(part_x[half:], 4, self.dp))

    def parts(self):
        dp = self.dp
        if dp == 8:
            here = [self.x, *self.near, *self.far]
            return here + [dp_swap(part, 1, dp) for part in here]
        whole = self.x
        bit = dp // 2
        while bit:
            whole = jnp.concatenate([whole, dp_swap(whole, bit, dp)], 0)
            bit //= 2
        return [whole]


def gather_head(x, heads):
    return [x] + [head_shift(x, heads - j, heads) for j in range(1, heads)]


def scatter_head(parts, heads):
    total = parts[0].astype(F32)
    for j in range(1, heads):
        total = total + head_shift(parts[j].astype(BF), j, heads).astype(F32)
    return total


def sum_head(x, heads):
    total = x
    for j in range(1, heads):
        total = total + head_shift(x, j, heads)
    return total


def sum_all(x, dp, heads):
    return sum_head(sum_dp(x, dp), heads)


def sum_dp(x, dp):
    bit = 1
    while bit < dp:
        x = x + dp_swap(x, bit, dp)
        bit *= 2
    return x


def stacked(refs):
    return refs[0][...] if len(refs) == 1 else jnp.concatenate([ref[...] for ref in refs], 0)


def lookup_kernel(vocab, tile, ids_ref, *refs):
    *table_refs, out_ref, rows_ref, acc_ref = refs
    step = pl.program_id(0)

    @pl.when(step == 0)
    def _():
        acc_ref[...] = jnp.zeros_like(acc_ref)

    place = lax.broadcasted_iota(jnp.int32, (1, tile), 1)
    block = stacked(table_refs)
    block = jnp.where(place < vocab - step * tile, block, jnp.zeros_like(block)).T
    rows_ref[...] = block
    hit = (ids_ref[...] - step * tile == place).astype(BF)
    acc_ref[...] += jnp.dot(hit, block, preferred_element_type=F32)

    @pl.when(step == pl.num_programs(0) - 1)
    def _():
        out_ref[...] = acc_ref[...].astype(BF)


def column_specs(parts, tile):
    return [pl.BlockSpec((part.shape[0], tile), lambda i: (0, i)) for part in parts]


def fixed(shape):
    return pl.BlockSpec(shape, lambda i: (0,) * len(shape))


VMEM_LIMIT = 56 * 2**20


def padded_to(columns, step=128):
    return -(-columns // step) * step


def lookup(ids, table_parts):
    rows, vocab = ids.shape[0], table_parts[0].shape[1]
    tile = 1024
    return pl.pallas_call(
        functools.partial(lookup_kernel, vocab, tile),
        out_shape=[
            jax.ShapeDtypeStruct((rows, D), BF),
            jax.ShapeDtypeStruct((padded_to(vocab), D), BF),
        ],
        grid=(pl.cdiv(vocab, tile),),
        in_specs=[fixed((rows, 1))] + column_specs(table_parts, tile),
        out_specs=[fixed((rows, D)), pl.BlockSpec((tile, D), lambda i: (i, 0))],
        scratch_shapes=[pltpu.VMEM((rows, D), F32)],
        compiler_params=pltpu.CompilerParams(vmem_limit_bytes=VMEM_LIMIT),
    )(ids.reshape(rows, 1), *table_parts)


def spread_kernel(tile, ids_ref, rows_ref, *refs):
    step = pl.program_id(0)
    turned_ref = refs[-1]

    @pl.when(step == 0)
    def _():
        turned_ref[...] = rows_ref[...].T

    place = step * tile + lax.broadcasted_iota(jnp.int32, (1, tile), 1)
    hit = (ids_ref[...] == place).astype(BF)
    total = jnp.dot(turned_ref[...], hit, preferred_element_type=F32)
    if len(refs) == 4:
        final_ref, slope_ref, out_ref, _ = refs
        out_ref[...] = total + lax.dot_general(
            final_ref[...], slope_ref[...], (((1,), (1,)), ((), ())), preferred_element_type=F32
        )
    else:
        base_ref, *keep_refs, send_ref, _ = refs
        total = base_ref[...] + total
        deep = D // 8
        for number, keep_ref in enumerate(keep_refs):
            keep_ref[...] = total[number * deep : (number + 1) * deep]
        send_ref[...] = total[D // 2 :].astype(BF)


def spread(ids, rows_low, columns, final_t=None, slope=None, base=None):
    rows = ids.shape[0]
    tile = 1024
    if base is None:
        shapes = [((D, columns), F32)]
        more = [final_t, slope]
        specs = [fixed(final_t.shape), pl.BlockSpec((tile, slope.shape[1]), lambda i: (i, 0))]
    else:
        shapes = [((D // 8, columns), F32)] * 4 + [((D // 2, columns), BF)]
        more = [base]
        specs = [pl.BlockSpec((D, tile), lambda i: (0, i))]
    return pl.pallas_call(
        functools.partial(spread_kernel, tile),
        out_shape=[jax.ShapeDtypeStruct(*shape) for shape in shapes],
        grid=(pl.cdiv(columns, tile),),
        in_specs=[fixed((rows, 1)), fixed((rows, D))] + specs,
        out_specs=[pl.BlockSpec((shape[0][0], tile), lambda i: (0, i)) for shape in shapes],
        scratch_shapes=[pltpu.VMEM((D, rows), BF)],
        compiler_params=pltpu.CompilerParams(vmem_limit_bytes=VMEM_LIMIT),
    )(ids.reshape(rows, 1), rows_low, *more)


def column_call(kernel, inputs, outputs, tile, sums=(), columns=None):
    columns = columns or inputs[0].shape[1]
    out_shape = [jax.ShapeDtypeStruct((rows, columns), dtype) for rows, dtype in outputs]
    out_specs = [pl.BlockSpec((rows, tile), lambda i: (0, i)) for rows, _ in outputs]
    for shape in sums:
        out_shape.append(jax.ShapeDtypeStruct(shape, F32))
        out_specs.append(fixed(shape))
    return pl.pallas_call(
        kernel,
        out_shape=out_shape,
        grid=(pl.cdiv(columns, tile),),
        in_specs=[
            pl.BlockSpec((array.shape[0], tile), lambda i: (0, i))
            if array.shape[1] >= columns
            else fixed(array.shape)
            for array in inputs
        ],
        out_specs=out_specs,
        compiler_params=pltpu.CompilerParams(vmem_limit_bytes=VMEM_LIMIT),
    )(*inputs)


def first_sums_kernel(y_ref, x_ref, d_ref, got_ref, d_low, d_high, x_low, y_high, y_low, x_high):
    deep = y_ref.shape[0]
    half = deep // 2
    got = got_ref[...].astype(F32)
    y = y_ref[...] + got[deep : 2 * deep]
    x = x_ref[...] + got[2 * deep : 3 * deep]
    d = (d_ref[...] + got[3 * deep :]).astype(BF)
    d_low[...] = d[:half]
    d_high[...] = d[half:]
    x_low[...] = x[:half].astype(BF)
    y_high[...] = y[half:].astype(BF)
    y_low[...] = y[:half]
    x_high[...] = x[half:]


def second_sums_kernel(y_low, got_a, x_high, got_b, y_out, x_out):
    y_out[...] = (y_low[...] + got_a[...].astype(F32)).astype(BF)
    x_out[...] = (x_high[...] + got_b[...].astype(F32)).astype(BF)


def lane_sums(value):
    rows, columns = value.shape
    total = value[:, :128]
    for start in range(128, columns, 128):
        total = total + value[:, start : start + 128]
    out = total[:8]
    for start in range(8, rows, 8):
        out = out + total[start : start + 8]
    return out


def inside(columns, tile, value):
    place = pl.program_id(0) * tile + lax.broadcasted_iota(jnp.int32, (1, tile), 1)
    return jnp.where(place < columns, value, 0.0)


def last_sums_kernel(columns, tile, own, got, x_low, y_high, y_low, x_high, out, squares):
    half = x_low.shape[0]
    low = own[:half] + got[:half].astype(F32) + (x_low[...].astype(F32) + y_low[...].astype(F32))
    high = (
        own[half:]
        + got[half : 2 * half].astype(F32)
        + (x_high[...].astype(F32) + y_high[...].astype(F32))
    )
    whole = jnp.concatenate([low, high], 0)
    out[...] = whole

    @pl.when(pl.program_id(0) == 0)
    def _():
        squares[...] = jnp.zeros_like(squares)

    squares[...] += lane_sums(inside(columns, tile, whole * whole))


class ScatterDp:
    def __init__(self, keeps, send, dp):
        self.keeps, self.dp = keeps, dp
        self.got = dp_swap(send, 1, dp)

    def run(self, columns):
        dp = self.dp
        tile = 4096
        if dp != 8:
            total = jnp.concatenate(self.keeps, 0) + self.got.astype(F32)
            bit = 2
            while bit < dp:
                rows = total.shape[0] // 2
                total = total[:rows] + dp_swap(total[rows:].astype(BF), bit, dp).astype(F32)
                bit *= 2
            total = total[:, :columns]
            squares = jnp.sum(total * total)
            return total, jnp.zeros((8, 128), F32).at[0, 0].set(squares)
        own, y, x, d = self.keeps
        half = own.shape[0] // 2
        d_low, d_high, x_low, y_high, y_low, x_high = column_call(
            first_sums_kernel, [y, x, d, self.got], [(half, BF)] * 4 + [(half, F32)] * 2, tile
        )
        got_a, got_b = dp_swap(d_low, 2, dp), dp_swap(d_high, 4, dp)
        x_low, y_high = dp_swap(x_low, 2, dp), dp_swap(y_high, 4, dp)
        y_low, x_high = column_call(
            second_sums_kernel, [y_low, got_a, x_high, got_b], [(half, BF)] * 2, tile
        )
        y_low, x_high = dp_swap(y_low, 4, dp), dp_swap(x_high, 2, dp)
        return column_call(
            functools.partial(last_sums_kernel, columns, tile),
            [own, self.got, x_low, y_high, y_low, x_high],
            [(2 * half, F32)],
            tile,
            sums=[(8, 128)],
            columns=columns,
        )


def logits_kernel(vocab, tile, final_ref, label_ref, teacher_ref, table_ref, out_ref, *stats):
    top_s, top_t, one, half, teach, cross, label = stats
    step = pl.program_id(0)
    last = pl.num_programs(0) - 1

    @pl.when(step == 0)
    def _():
        top_s[...] = jnp.full_like(top_s, -1e30)
        top_t[...] = jnp.full_like(top_t, -1e30)
        for ref in (one, half, teach, cross, label):
            ref[...] = jnp.zeros_like(ref)

    def work(valid):
        logits = jnp.dot(table_ref[...], final_ref[...], preferred_element_type=F32)
        tokens = logits.shape[1]

        def folded(value):
            return value.reshape(tile // 8, 8, tokens)

        student = folded(logits)
        teacher = folded(teacher_ref[...].astype(F32))
        place = 8 * lax.broadcasted_iota(jnp.int32, (tile // 8, 8, 1), 0)
        place = place + lax.broadcasted_iota(jnp.int32, (tile // 8, 8, 1), 1)
        if valid < tile:
            student = jnp.where(place < valid, student, -1e30)
            teacher = jnp.where(place < valid, teacher, -1e30)
        old_s, old_t = top_s[...], top_t[...]
        new_s = jnp.maximum(old_s, jnp.max(student, 0))
        new_t = jnp.maximum(old_t, jnp.max(teacher, 0))
        top_s[...] = new_s
        top_t[...] = new_t
        scale_s = jnp.exp((old_s - new_s) * 0.5)
        scale_t = jnp.exp((old_t - new_t) * 0.5)
        e = jnp.exp((student - new_s[None]) * 0.5)
        half[...] = half[...] * scale_s + jnp.sum(e, 0)
        one[...] = one[...] * (scale_s * scale_s) + jnp.sum(e * e, 0)
        e = jnp.exp((teacher - new_t[None]) * 0.5)
        teach[...] = teach[...] * scale_t + jnp.sum(e, 0)
        cross[...] = cross[...] * scale_t + jnp.sum(e * (teacher - student), 0)
        labels = (label_ref[...] - step * tile)[None]
        label[...] += jnp.sum(jnp.where(labels == place, student, 0.0), 0)

    rest = vocab - (pl.cdiv(vocab, tile) - 1) * tile
    if rest == tile:
        work(tile)
    else:

        @pl.when(step < last)
        def _():
            work(tile)

        @pl.when(step == last)
        def _():
            work(rest)

    @pl.when(step == last)
    def _():
        peak_s = jnp.max(top_s[...], 0, keepdims=True)
        peak_t = jnp.max(top_t[...], 0, keepdims=True)
        by_s = jnp.exp((top_s[...] - peak_s) * 0.5)
        by_t = jnp.exp((top_t[...] - peak_t) * 0.5)

        def total(value):
            return jnp.sum(value, 0, keepdims=True)

        out_ref[0:1] = peak_s
        out_ref[1:2] = peak_t
        out_ref[2:3] = total(one[...] * (by_s * by_s))
        out_ref[3:4] = total(half[...] * by_s)
        out_ref[4:5] = total(teach[...] * by_t)
        out_ref[5:6] = total(cross[...] * by_t) * 0.5
        out_ref[6:7] = total(label[...])
        out_ref[7:8] = jnp.zeros_like(peak_s)


def logits_stats(final_t, labels, teacher_t, table_rows):
    vocab, tokens = teacher_t.shape
    tile = 1024
    return pl.pallas_call(
        functools.partial(logits_kernel, vocab, tile),
        out_shape=jax.ShapeDtypeStruct((8, tokens), F32),
        grid=(pl.cdiv(vocab, tile),),
        in_specs=[
            fixed(final_t.shape),
            fixed((1, tokens)),
            pl.BlockSpec((tile, tokens), lambda i: (i, 0)),
            pl.BlockSpec((tile, D), lambda i: (i, 0)),
        ],
        out_specs=fixed((8, tokens)),
        scratch_shapes=[pltpu.VMEM((8, tokens), F32)] * 7,
        compiler_params=pltpu.CompilerParams(vmem_limit_bytes=VMEM_LIMIT),
    )(final_t, labels.reshape(1, tokens), teacher_t, table_rows)


def logits_back_kernel(vocab, tile, final_ref, label_ref, scalar_ref, teacher_ref, *refs):
    rows_ref, *table_refs, slope_ref, back_ref, acc_ref = refs
    step = pl.program_id(0)
    last = pl.num_programs(0) - 1

    @pl.when(step == 0)
    def _():
        acc_ref[...] = jnp.zeros_like(acc_ref)

    good = lax.broadcasted_iota(jnp.int32, (1, tile), 1) < vocab - step * tile
    block = stacked(table_refs)
    block = jnp.where(good, block, jnp.zeros_like(block))
    place = lax.broadcasted_iota(jnp.int32, (tile, 1), 0)
    logits = jnp.dot(rows_ref[...], final_ref[...], preferred_element_type=F32)
    lse_half = scalar_ref[0:1]
    lse_teacher = scalar_ref[1:2]
    soft_one = scalar_ref[2:3]
    soft_half = scalar_ref[3:4]
    weight = scalar_ref[4:5]
    student = jnp.exp(logits * 0.5 - lse_half)
    teacher = jnp.exp(teacher_ref[...].astype(F32) * 0.5 - lse_teacher)
    labels = label_ref[...] - step * tile
    slope = student * (soft_one * student + soft_half) - soft_half * teacher
    slope = slope - jnp.where(labels == place, weight, 0.0)
    slope = jnp.where(place < vocab - step * tile, slope, 0.0).astype(BF)
    slope_ref[...] = slope
    acc_ref[...] += jnp.dot(block, slope, preferred_element_type=F32)

    @pl.when(step == last)
    def _():
        back_ref[...] = acc_ref[...].astype(BF)


def logits_back(final_t, labels, scalars, teacher_t, table_rows, table_parts):
    vocab, tokens = teacher_t.shape
    tile = 1024
    return pl.pallas_call(
        functools.partial(logits_back_kernel, vocab, tile),
        out_shape=[
            jax.ShapeDtypeStruct((padded_to(vocab), tokens), BF),
            jax.ShapeDtypeStruct((D, tokens), BF),
        ],
        grid=(pl.cdiv(vocab, tile),),
        in_specs=[
            fixed(final_t.shape),
            fixed((1, tokens)),
            fixed(scalars.shape),
            pl.BlockSpec((tile, tokens), lambda i: (i, 0)),
            pl.BlockSpec((tile, D), lambda i: (i, 0)),
        ]
        + column_specs(table_parts, tile),
        out_specs=[pl.BlockSpec((tile, tokens), lambda i: (i, 0)), fixed((D, tokens))],
        scratch_shapes=[pltpu.VMEM((D, tokens), F32)],
        compiler_params=pltpu.CompilerParams(vmem_limit_bytes=VMEM_LIMIT),
    )(final_t, labels.reshape(1, tokens), scalars, teacher_t, table_rows, *table_parts)


BIAS_ONE = 1.0 - BETA_ONE**STEP_NUM
BIAS_TWO = 1.0 - BETA_TWO**STEP_NUM


def lamb(weight, moment, second, grad, clip):
    grad = grad * clip
    moment = BETA_ONE * moment + (1 - BETA_ONE) * grad
    second = BETA_TWO * second + (1 - BETA_TWO) * grad * grad
    update = (
        moment * (1.0 / BIAS_ONE) / (jnp.sqrt(second * (1.0 / BIAS_TWO)) + ADAM_EPS)
        + WEIGHT_DECAY * weight
    )
    return moment, second, update


def lamb_columns_kernel(columns, tile, w, m, v, g, clip, m_out, v_out, u_out, squares):
    moment, second, update = lamb(w[...], m[...], v[...], g[...], clip[0:1, 0:1])
    m_out[...] = moment
    v_out[...] = second
    u_out[...] = update

    @pl.when(pl.program_id(0) == 0)
    def _():
        squares[...] = jnp.zeros_like(squares)

    squares[...] += lane_sums(inside(columns, tile, update * update))


def lamb_matrices_kernel(places, clip_ref, *refs):
    grads = refs[:2]
    count = len(places)
    states = refs[2 : 2 + 3 * count]
    outs = refs[2 + 3 * count : -1]
    squares = refs[-1]
    squares[...] = jnp.zeros_like(squares)
    clip = clip_ref[0:1, 0:1]
    row = 0
    for group, matrices in enumerate(places):
        w, m, v = states[3 * group : 3 * group + 3]
        m_out, v_out, u_out = outs[3 * group : 3 * group + 3]
        width = w.shape[-1]
        for number, (array, start) in enumerate(matrices):
            grad = grads[array][:, start : start + width]
            moment, second, update = lamb(w[number], m[number], v[number], grad, clip)
            m_out[number] = moment
            v_out[number] = second
            u_out[number] = update
            total = jnp.sum(update * update, 0, keepdims=True)
            lanes = min(128, width)
            line = total[:, :lanes]
            for first in range(lanes, width, lanes):
                line = line + total[:, first : first + lanes]
            squares[row : row + 1, :lanes] = line
            row += 1


def lamb_matrices(clip, grads, groups, places):
    flat = [array for group in groups for array in group]
    shapes = [jax.ShapeDtypeStruct(group[0].shape, F32) for group in groups for _ in range(3)]
    rows = 8 * pl.cdiv(sum(len(matrices) for matrices in places), 8)
    return pl.pallas_call(
        functools.partial(lamb_matrices_kernel, places),
        out_shape=shapes + [jax.ShapeDtypeStruct((rows, 128), F32)],
        compiler_params=pltpu.CompilerParams(vmem_limit_bytes=VMEM_LIMIT),
    )(clip, *grads, *flat)


def pack_kernel(heads_of, *refs):
    *in_refs, out_ref = refs
    start = 0
    for number, index in heads_of:
        value = in_refs[number][...] if index is None else in_refs[number][index]
        out_ref[:, start : start + value.shape[1]] = value.astype(BF)
        start += value.shape[1]


def pack(arrays, plan):
    columns = sum(arrays[number].shape[-1] for number, _ in plan)
    return pl.pallas_call(
        functools.partial(pack_kernel, plan),
        out_shape=jax.ShapeDtypeStruct((arrays[0].shape[-2], columns), BF),
        compiler_params=pltpu.CompilerParams(vmem_limit_bytes=VMEM_LIMIT),
    )(*arrays)


def restack_kernel(split, *refs):
    *in_refs, left_ref, right_ref = refs
    rows = in_refs[0].shape[0]
    for number, ref in enumerate(in_refs):
        left_ref[number * rows : (number + 1) * rows] = ref[:, :split]
        right_ref[number * rows : (number + 1) * rows] = ref[:, split:]


def restack(parts, split):
    rows, columns = parts[0].shape
    total = rows * len(parts)
    return pl.pallas_call(
        functools.partial(restack_kernel, split),
        out_shape=[
            jax.ShapeDtypeStruct((total, split), BF),
            jax.ShapeDtypeStruct((total, columns - split), BF),
        ],
        compiler_params=pltpu.CompilerParams(vmem_limit_bytes=VMEM_LIMIT),
    )(*parts)


def assemble_kernel(widths, heads, order_ref, in_ref, *out_refs):
    deep = in_ref.shape[-2] // heads
    start = 0
    for width, out_ref in zip(widths, out_refs, strict=True):
        shards = out_ref.shape[-1] // width
        for j in range(shards):
            out_ref[:, j * width : (j + 1) * width] = in_ref[
                0, j * deep : (j + 1) * deep, start : start + width
            ]
        start += width


def assemble(order, gathered, widths, heads, single):
    dp, rows, columns = gathered.shape
    deep = rows // heads
    wides = [w * heads for w in widths[: len(widths) - single]] + widths[len(widths) - single :]
    return pl.pallas_call(
        functools.partial(assemble_kernel, widths, heads),
        out_shape=[jax.ShapeDtypeStruct((dp * deep, w), BF) for w in wides],
        grid_spec=pltpu.PrefetchScalarGridSpec(
            num_scalar_prefetch=1,
            grid=(dp,),
            in_specs=[pl.BlockSpec((1, rows, columns), lambda p, order: (order[p], 0, 0))],
            out_specs=[pl.BlockSpec((deep, w), lambda p, order: (p, 0)) for w in wides],
        ),
    )(order, gathered)


def assemble_parts_kernel(widths, heads, deep, *refs):
    outs = refs[len(refs) - len(widths) :]
    row = 0
    for ref in refs[: len(refs) - len(widths)]:
        for first in range(0, ref.shape[0], deep):
            place, j = divmod(row // deep, heads)
            start = 0
            for width, out_ref in zip(widths, outs, strict=True):
                if out_ref.shape[-1] > width:
                    out_ref[place * deep : (place + 1) * deep, j * width : (j + 1) * width] = ref[
                        first : first + deep, start : start + width
                    ]
                elif j == 0:
                    out_ref[place * deep : (place + 1) * deep] = ref[
                        first : first + deep, start : start + width
                    ]
                start += width
            row += deep


def assemble_parts(parts, widths, heads, single, dp):
    deep = D // dp
    wides = [w * heads for w in widths[: len(widths) - single]] + widths[len(widths) - single :]
    return pl.pallas_call(
        functools.partial(assemble_parts_kernel, widths, heads, deep),
        out_shape=[jax.ShapeDtypeStruct((D, w), BF) for w in wides],
        compiler_params=pltpu.CompilerParams(vmem_limit_bytes=VMEM_LIMIT),
    )(*parts)


def weight_grad_kernel(widths, single, order_ref, *refs):
    out_ref = refs[-1]
    dp, heads, deep, _ = out_ref.shape

    def put(j, start, stop, value):
        for place in range(dp):
            out_ref[order_ref[place], j, :, start:stop] = value[place * deep : (place + 1) * deep]

    start = 0
    for number, width in enumerate(widths):
        left = refs[2 * number][...]
        together = max(1, 512 // width)
        for first in range(0, heads, together):
            whole = lax.dot_general(
                left,
                refs[2 * number + 1][:, first * width : (first + together) * width],
                (((0,), (0,)), ((), ())),
                preferred_element_type=F32,
            ).astype(BF)
            for j in range(together):
                put(first + j, start, start + width, whole[:, j * width : (j + 1) * width])
        start += width
    if single:
        value = refs[-2][...].astype(BF)
        for j in range(heads):
            put(j, start, start + value.shape[1], value)


def weight_grads(order, pairs, heads, extra=None):
    dp = order.shape[0]
    flat = []
    for left, right in pairs:
        flat += [left.reshape(-1, left.shape[-1]), right.reshape(-1, right.shape[-1])]
    widths = [right.shape[-1] // heads for _, right in pairs]
    columns = sum(widths)
    if extra is not None:
        flat.append(extra)
        columns += extra.shape[1]
    return pl.pallas_call(
        functools.partial(weight_grad_kernel, widths, extra is not None),
        out_shape=jax.ShapeDtypeStruct((dp, heads, D // dp, columns), BF),
        in_specs=[pl.BlockSpec(memory_space=pltpu.SMEM)]
        + [pl.BlockSpec(memory_space=pltpu.VMEM)] * len(flat),
        out_specs=pl.BlockSpec(memory_space=pltpu.VMEM),
        compiler_params=pltpu.CompilerParams(vmem_limit_bytes=48 * 2**20),
    )(order, *flat)


def normed(inputs, gain_row):
    return (
        inputs * lax.rsqrt(jnp.mean(inputs * inputs, -1, keepdims=True) + NORM_EPS) * gain_row
    ).astype(BF)


def norm_back(inputs, gain_row, upstream):
    factor = lax.rsqrt(jnp.mean(inputs * inputs, -1, keepdims=True) + NORM_EPS)
    scaled = upstream * gain_row
    inner = jnp.mean(scaled * inputs, -1, keepdims=True)
    return (
        factor * (scaled - inputs * factor * factor * inner),
        jnp.sum(upstream * inputs * factor, axis=(0, 1)),
    )


def dot(spec, a, b):
    return jnp.einsum(spec, a, b, preferred_element_type=F32)


def split_heads(array):
    return array.reshape(array.shape[0], array.shape[1], -1, DH)


def merge_heads(array):
    return array.reshape(array.shape[0], array.shape[1], -1)


def attn_probs(query, keys_all, allowed):
    scores = dot("bqhe,bkhe->bhqk", query, keys_all) * DH ** (-0.5)
    return jax.nn.softmax(jnp.where(allowed[:, None], scores, -1000000000.0), -1)


def attend_fwd(query_in, source, weights, allowed):
    query = split_heads(dot("bld,dh->blh", query_in, weights[0]).astype(BF))
    keys_all = split_heads(dot("bld,dh->blh", source, weights[1]).astype(BF))
    values = split_heads(dot("bld,dh->blh", source, weights[2]).astype(BF))
    probs = attn_probs(query, keys_all, allowed)
    mixed = merge_heads(dot("bhqk,bkhe->bqhe", probs.astype(BF), values).astype(BF))
    return dot("blh,dh->bld", mixed, weights[3]), (query, keys_all, values, mixed)


def attend_back(upstream, query_in, source, weights, allowed, kept):
    query, keys_all, values, mixed = kept
    up_low = upstream.astype(BF)
    grad_mixed = split_heads(dot("bld,dh->blh", up_low, weights[3]).astype(BF))
    probs = attn_probs(query, keys_all, allowed)
    grad_probs = dot("bqhe,bkhe->bhqk", grad_mixed, values)
    grad_scores = (probs * (grad_probs - jnp.sum(grad_probs * probs, -1, keepdims=True))).astype(BF)
    grad_query = merge_heads(
        (dot("bhqk,bkhe->bqhe", grad_scores, keys_all) * DH ** (-0.5)).astype(BF)
    )
    grad_keys = merge_heads(
        (dot("bhqk,bqhe->bkhe", grad_scores, query) * DH ** (-0.5)).astype(BF)
    )
    grad_values = merge_heads(dot("bhqk,bqhe->bkhe", probs.astype(BF), grad_mixed).astype(BF))
    pairs = [(query_in, grad_query), (source, grad_keys), (source, grad_values), (up_low, mixed)]
    back_query = dot("blh,dh->bld", grad_query, weights[0])
    back_source = dot("blh,dh->bld", grad_keys, weights[1])
    back_source = back_source + dot("blh,dh->bld", grad_values, weights[2])
    return back_query, back_source, pairs


def feed_fwd(inputs, weights):
    hidden = jax.nn.relu(dot("bld,df->blf", inputs, weights[0])).astype(BF)
    return dot("blf,df->bld", hidden, weights[1]), hidden


def feed_back(upstream, inputs, weights, hidden):
    up_low = upstream.astype(BF)
    grad_hidden = dot("bld,df->blf", up_low, weights[1])
    grad_pre = jnp.where(hidden > 0, grad_hidden, 0.0).astype(BF)
    back_in = dot("blf,df->bld", grad_pre, weights[0])
    return back_in, [(inputs, grad_pre), (up_low, hidden)]


def body(
    dp,
    heads,
    source_ids,
    target_ids,
    source_lens,
    target_lens,
    kl_mask,
    teacher,
    *state,
):
    def transposed(group):
        embed, attn_in, attn_out, ff_in, ff_out, gains = group
        swap = functools.partial(jnp.swapaxes, axis1=-1, axis2=-2)
        return (swap(embed), attn_in, swap(attn_out), ff_in, swap(ff_out), gains)

    masters = transposed(state[:6])
    moments = transposed(state[6:12])
    seconds = transposed(state[12:])
    embed_t, attn_in, attn_out_t, ff_in, ff_out_t, gains = masters
    low = embed_t.astype(BF)
    vocab_local = embed_t.shape[1]
    head_pos = lax.axis_index("head")
    lead = (head_pos == 0).astype(F32)
    vocab_start = head_pos * vocab_local
    batch_size, source_len = source_ids.shape
    target_len = target_ids.shape[1]
    token_count = batch_size * target_len
    each = -(-batch_size // heads)
    padded = each * heads

    sides = [
        [attn_in[0, 0], attn_in[0, 1], attn_in[0, 2], attn_out_t[0], ff_in[0], ff_out_t[0]],
        [attn_in[1, 0], attn_in[1, 1], attn_in[1, 2], attn_out_t[1]]
        + [attn_in[2, 0], attn_in[2, 1], attn_in[2, 2], attn_out_t[2], ff_in[1], ff_out_t[1]],
    ]
    widths = [[matrix.shape[-1] for matrix in side] for side in sides]
    lanes = 128
    gain_rows = gains.shape[0]
    counted = jnp.full((1, gains.shape[1]), jnp.sum((target_lens > 0).astype(F32)))
    gain_block = jnp.pad(
        jnp.concatenate([gains, counted], 0).T, ((0, 0), (0, lanes - gain_rows - 1))
    )
    places = [0]
    bit = dp // 2
    while bit:
        places = places + [place ^ bit for place in places]
        bit //= 2
    order = lax.axis_index("dp") ^ jnp.array(places, jnp.int32)
    flat_in = attn_in.reshape((9,) + attn_in.shape[2:])
    arrays = [flat_in, attn_out_t, ff_in, ff_out_t, gain_block]
    plan = [(0, 0), (0, 1), (0, 2), (1, 0), (2, 0), (3, 0), (4, None)]
    plan += [(0, 3), (0, 4), (0, 5), (1, 1), (0, 6), (0, 7), (0, 8), (1, 2), (2, 1), (3, 1)]
    split = sum(widths[0]) + lanes
    packed = pack(arrays, plan)
    low, packed = tie(low, packed)
    came = gather_head(packed, heads)
    table = GatherDp(low, dp)
    table.go_far()
    came = tie(came[0], *came[1:], *table.far)[:heads]
    enc_wide, dec_wide = restack(came, split)
    enc_gather = GatherDp(enc_wide, dp)
    dec_gathered = lax.all_gather(dec_wide, "dp", axis=0)
    table_parts = table.parts()

    def fill(array):
        return jnp.pad(array, ((0, padded - batch_size),) + ((0, 0),) * (array.ndim - 1))

    dec_ids = jnp.concatenate([jnp.zeros((batch_size, 1), jnp.int32), target_ids[:, :-1]], 1)
    enc_ids = jnp.roll(fill(source_ids).reshape(heads, -1), -head_pos, 0) - vocab_start
    dec_ids = jnp.roll(fill(dec_ids).reshape(heads, -1), -head_pos, 0) - vocab_start
    enc_rows_count = heads * each * source_len
    looked, table_rows = lookup(
        jnp.concatenate([enc_ids.reshape(-1), dec_ids.reshape(-1)]), table_parts
    )
    enc_looked = looked[:enc_rows_count].reshape(heads, -1, D)
    dec_looked = looked[enc_rows_count:]
    came = [enc_looked[0]] + [head_shift(enc_looked[j], j, heads) for j in range(1, heads)]
    dec_looked, *enc_gather.near = tie(dec_looked, *enc_gather.near)
    enc_gather.go_far()
    *enc_list, gain = assemble_parts(enc_gather.parts(), widths[0] + [lanes], heads, 1, dp)
    w_enc, f_enc = enc_list[:4], enc_list[4:]
    gain = gain[:, : gain_rows + 1].astype(F32).T
    real_count = jnp.maximum(jnp.sum(gain[gain_rows].reshape(dp, -1)[:, 0]), 1.0)
    enc_embed = functools.reduce(jnp.add, came).astype(F32).reshape(each, source_len, D)
    my_lens = lax.dynamic_slice_in_dim(fill(source_lens), head_pos * each, each)

    src_keys = jnp.arange(source_len)[None, :] < my_lens[:, None]
    enc_allowed = jnp.broadcast_to(src_keys[:, None, :], (each, source_len, source_len))
    cross_allowed = jnp.broadcast_to(src_keys[:, None, :], (each, target_len, source_len))
    causal = jnp.broadcast_to(
        (jnp.arange(target_len)[:, None] >= jnp.arange(target_len)[None, :])[None],
        (each, target_len, target_len),
    )
    norm_a = normed(enc_embed, gain[0])
    branch, kept_enc = attend_fwd(norm_a, norm_a, w_enc, enc_allowed)
    enc_mid = enc_embed + branch
    enc_mid, dec_looked = tie(enc_mid, dec_looked)
    looked = dec_looked.reshape(heads, -1, D)
    dec_came = [looked[0]] + [head_shift(looked[j], j, heads) for j in range(1, heads)]
    norm_b = normed(enc_mid, gain[1])
    branch, hidden_enc = feed_fwd(norm_b, f_enc)
    enc_last = enc_mid + branch
    encoded = normed(enc_last, gain[2])
    dec_list = assemble(order, dec_gathered, widths[1], heads, 0)
    w_self, w_cross, f_dec = dec_list[:4], dec_list[4:8], dec_list[8:]
    dec_embed = functools.reduce(jnp.add, dec_came).astype(F32).reshape(each, target_len, D)
    norm_c = normed(dec_embed, gain[3])
    branch, kept_self = attend_fwd(norm_c, norm_c, w_self, causal)
    dec_one = dec_embed + branch
    norm_d = normed(dec_one, gain[4])
    branch, kept_cross = attend_fwd(norm_d, encoded, w_cross, cross_allowed)
    dec_two = dec_one + branch
    norm_e = normed(dec_two, gain[5])
    branch, hidden_dec = feed_fwd(norm_e, f_dec)
    dec_three = dec_two + branch
    head_gain = gain[6] * D ** (-0.5)
    my_final = normed(dec_three, head_gain).reshape(each * target_len, D)

    final = jnp.concatenate(gather_head(my_final, heads), 0)
    final = jnp.roll(final, head_pos * each * target_len, 0)[:token_count]
    valid = (jnp.arange(target_len)[None, :] < target_lens[:, None]).astype(F32)
    token_weight = (
        valid / (jnp.maximum(target_lens, 1).astype(F32)[:, None] * real_count)
    ).reshape(token_count)
    divergence_mask = kl_mask.astype(F32).reshape(token_count)
    labels = target_ids.reshape(token_count) - vocab_start
    labels = jnp.where((labels >= 0) & (labels < vocab_local), labels, -1)
    final_t = final.T
    teacher_t = teacher.T
    stats = logits_stats(final_t, labels, teacher_t, table_rows)
    every = jnp.stack(gather_head(stats, heads))
    peak_student = jnp.max(every[:, 0], 0)
    peak_teacher = jnp.max(every[:, 1], 0)
    off_s = every[:, 0] - peak_student
    off_t = jnp.exp((every[:, 1] - peak_teacher) / SOFTEN_FACTOR)
    sum_one = jnp.sum(every[:, 2] * jnp.exp(off_s), 0)
    sum_half = jnp.sum(every[:, 3] * jnp.exp(off_s / SOFTEN_FACTOR), 0)
    sum_teacher = jnp.sum(every[:, 4] * off_t, 0)
    sum_cross = jnp.sum(every[:, 5] * off_t, 0)
    label_logprob = jnp.sum(every[:, 6], 0)
    lse_one = peak_student + jnp.log(sum_one)
    lse_half = peak_student / SOFTEN_FACTOR + jnp.log(sum_half)
    lse_teacher = peak_teacher / SOFTEN_FACTOR + jnp.log(sum_teacher)
    cross_entropy = lse_one - label_logprob
    divergence_value = sum_cross / sum_teacher - lse_teacher + lse_half
    loss_part = lead * jnp.sum(
        token_weight
        * (
            cross_entropy
            + DIVERGENCE_SCALE * SOFTEN_FACTOR * SOFTEN_FACTOR * divergence_value * divergence_mask
        )
    )
    soft_half = DIVERGENCE_SCALE * SOFTEN_FACTOR * divergence_mask * token_weight
    soft_one = token_weight * jnp.exp(SOFTEN_FACTOR * lse_half - lse_one)
    nothing = jnp.zeros_like(lse_half)
    scalars = jnp.stack(
        [lse_half, lse_teacher, soft_one, soft_half, token_weight, nothing, nothing, nothing]
    )
    slope, part = logits_back(final_t, labels, scalars, teacher_t, table_rows, table_parts)
    part = part.T.reshape(batch_size, target_len, D)
    part = jnp.roll(fill(part).reshape(heads, each * target_len, D), -head_pos, 0)
    grad_final = scatter_head([part[j] for j in range(heads)], heads).reshape(each, target_len, D)

    grad_three, gain_six = norm_back(dec_three, head_gain, grad_final)
    back_in, pairs_f_dec = feed_back(grad_three, norm_e, f_dec, hidden_dec)
    grad_norm_in, gain_five = norm_back(dec_two, gain[5], back_in)
    grad_two = grad_three + grad_norm_in
    back_query, grad_encoded, pairs_cross = attend_back(
        grad_two, norm_d, encoded, w_cross, cross_allowed, kept_cross
    )
    grad_norm_in, gain_four = norm_back(dec_one, gain[4], back_query)
    grad_one = grad_two + grad_norm_in
    back_query, back_source, pairs_self = attend_back(
        grad_one, norm_c, norm_c, w_self, causal, kept_self
    )
    grad_norm_in, gain_three = norm_back(dec_embed, gain[3], back_query + back_source)
    grad_dec_embed = grad_one + grad_norm_in
    dec_rows = gather_head(grad_dec_embed.reshape(-1, D).astype(BF), heads)
    dec_grads = weight_grads(order, pairs_self + pairs_cross + pairs_f_dec, heads)
    grad_encoded, dec_grads = tie(grad_encoded, dec_grads)
    dec_shard = lax.psum_scatter(dec_grads, "dp", scatter_dimension=0)
    grad_last, gain_two = norm_back(enc_last, gain[2], grad_encoded)
    back_in, pairs_f_enc = feed_back(grad_last, norm_b, f_enc, hidden_enc)
    back_in, *dec_rows = tie(back_in, *dec_rows)
    grad_norm_in, gain_one = norm_back(enc_mid, gain[1], back_in)
    grad_mid = grad_last + grad_norm_in
    back_query, back_source, pairs_enc = attend_back(
        grad_mid, norm_a, norm_a, w_enc, enc_allowed, kept_enc
    )
    grad_norm_in, gain_zero = norm_back(enc_embed, gain[0], back_query + back_source)
    grad_enc_embed = grad_mid + grad_norm_in

    gain_grads = jnp.stack(
        [gain_zero, gain_one, gain_two, gain_three, gain_four, gain_five, gain_six * D ** (-0.5)]
    )
    gain_cols = jnp.pad(gain_grads.T, ((0, 0), (0, lanes - gain_rows)))
    enc_low = grad_enc_embed.reshape(-1, D).astype(BF)
    enc_rows = gather_head(enc_low, heads)
    enc_grads = weight_grads(order, pairs_enc + pairs_f_enc, heads, gain_cols)
    enc_low, enc_grads = tie(enc_low, enc_grads)
    enc_shard = lax.psum_scatter(enc_grads, "dp", scatter_dimension=0)
    near_ids = jnp.concatenate([dec_ids.reshape(-1), enc_ids[0]])
    near_rows = jnp.concatenate(dec_rows + [enc_low], 0)
    columns = padded_to(vocab_local)
    (grad_table_t,) = spread(near_ids, near_rows, columns, final_t=final_t, slope=slope)

    def send_heads(shard):
        return [shard[0]] + [head_shift(shard[j], j, heads) for j in range(1, heads)]

    far_ids = enc_ids[1:].reshape(-1)
    far_rows = jnp.concatenate(enc_rows[1:], 0)
    dec_sums = send_heads(dec_shard)
    *keeps, send = spread(far_ids, far_rows, columns, base=grad_table_t)
    g_table, table_squares = ScatterDp(keeps, send, dp).run(vocab_local)
    enc_sums = send_heads(enc_shard)
    g_dec = functools.reduce(jnp.add, [value.astype(F32) for value in dec_sums])
    g_enc = functools.reduce(jnp.add, [value.astype(F32) for value in enc_sums])

    def squares(array, axes):
        return jnp.sum(array * array, axis=axes).reshape(-1)

    weight_squares = jnp.concatenate(
        [
            squares(embed_t, (0, 1)),
            squares(attn_in, (2, 3)),
            squares(attn_out_t, (1, 2)),
            squares(ff_in, (1, 2)),
            squares(ff_out_t, (1, 2)),
            squares(gains, (1,)) * lead,
        ]
    )
    matrix_count = weight_squares.shape[0]
    gain_at = sum(widths[0])
    g_gain = g_enc[:, gain_at : gain_at + gain_rows]
    grad_squares = (
        jnp.sum(g_dec * g_dec)
        + jnp.sum(g_enc[:, :gain_at] * g_enc[:, :gain_at])
        + lead * jnp.sum(g_gain * g_gain)
    )
    first_line = jnp.pad(
        jnp.concatenate([weight_squares, loss_part.reshape(1), grad_squares.reshape(1)]),
        (0, lanes - matrix_count - 2),
    ).reshape(1, lanes)
    totals = sum_all(jnp.concatenate([first_line, table_squares], 0), dp, heads)
    grad_norm = jnp.sqrt(totals[0, matrix_count + 1] + jnp.sum(totals[1:]))
    total_loss = totals[0, matrix_count]
    clip = jnp.full((8, 128), jnp.minimum(1.0, CLIP_NORM / grad_norm))
    m_table, v_table, u_table, squares_table = column_call(
        functools.partial(lamb_columns_kernel, vocab_local, 1024),
        [masters[0], moments[0], seconds[0], g_table, clip],
        [(embed_t.shape[0], F32)] * 3,
        1024,
        sums=[(8, 128)],
    )

    def flat9(array):
        return array.reshape((9,) + array.shape[2:])

    def starts(width):
        out = [0]
        for columns in width:
            out.append(out[-1] + columns)
        return out

    at_enc, at_dec = starts(widths[0]), starts(widths[1])
    places = [
        [(0, at_enc[k]) for k in range(3)]
        + [(1, at_dec[k]) for k in range(3)]
        + [(1, at_dec[k]) for k in range(4, 7)],
        [(0, at_enc[3]), (1, at_dec[3]), (1, at_dec[7])],
        [(0, at_enc[4]), (1, at_dec[8])],
        [(0, at_enc[5]), (1, at_dec[9])],
    ]
    groups = [
        tuple(flat9(stack[1]) if k == 1 else stack[k] for stack in (masters, moments, seconds))
        for k in range(1, 5)
    ]
    *fresh, squares_small = lamb_matrices(clip, [g_enc, g_dec], groups, places)
    m_gain, v_gain, u_gain = lamb(gains, moments[5], seconds[5], g_gain.T, clip[0, 0])
    gain_squares = jnp.pad(squares(u_gain, (1,)) * lead, (0, lanes - gain_rows)).reshape(1, lanes)
    small_count = sum(len(matrices) for matrices in places)
    update_totals = sum_all(
        jnp.concatenate([squares_table, squares_small, gain_squares], 0), dp, heads
    )
    update_squares = jnp.concatenate(
        [
            jnp.sum(update_totals[:8]).reshape(1),
            jnp.sum(update_totals[8 : 8 + small_count], 1),
            update_totals[-1, :gain_rows],
        ]
    )
    rates = LEARN_RATE * jnp.sqrt(totals[0, :matrix_count]) / (jnp.sqrt(update_squares) + 1e-06)
    fresh_m = [m_table] + list(fresh[0::3]) + [m_gain]
    fresh_v = [v_table] + list(fresh[1::3]) + [v_gain]
    updates = [u_table] + list(fresh[2::3]) + [u_gain]
    for stack in (fresh_m, fresh_v, updates):
        stack[1] = stack[1].reshape(attn_in.shape)
    shapes = [(1, 1), (3, 3, 1, 1), (3, 1, 1), (2, 1, 1), (2, 1, 1), (gain_rows, 1)]
    fresh_w, start = [], 0
    for master, update, shape in zip(masters, updates, shapes, strict=True):
        count = 1
        for extent in shape:
            count *= extent
        fresh_w.append(master - rates[start : start + count].reshape(shape) * update)
        start += count
    return (
        total_loss.reshape(1),
        grad_norm.reshape(1),
        *transposed(fresh_w),
        *transposed(fresh_m),
        *transposed(fresh_v),
    )


def solution(mesh):
    params = (
        P("head", "dp"),
        P(None, None, "dp", "head"),
        P(None, "head", "dp"),
        P(None, "dp", "head"),
        P(None, "head", "dp"),
        P(None, "dp"),
    )
    return jax.shard_map(
        functools.partial(body, mesh.shape["dp"], mesh.shape["head"]),
        mesh=mesh,
        in_specs=(
            P("dp", None),
            P("dp", None),
            P("dp"),
            P("dp"),
            P("dp", None),
            P("dp", "head"),
            *params,
            *params,
            *params,
        ),
        out_specs=(P(), P(), *params, *params, *params),
        check_vma=False,
    )
```

```python
import functools

import jax
import jax.numpy as jnp
from jax import lax
from jax.experimental import pallas as pl
from jax.experimental.pallas import tpu as pltpu
from jax.sharding import PartitionSpec as P

D = 512
DH = 64
STEP_NUM = 10

NORM_EPS = 1e-06
SOFTEN_FACTOR = 2.0
DIVERGENCE_SCALE = 1.0
CLIP_NORM = 0.02
BETA_ONE = 0.9
BETA_TWO = 0.999
ADAM_EPS = 1e-08
WEIGHT_DECAY = 0.01
LEARN_RATE = 0.3

BF = jnp.bfloat16
F32 = jnp.float32


def dp_swap(x, bit, dp):
    return lax.ppermute(x, "dp", [(i, i ^ bit) for i in range(dp)])


def head_shift(x, step, heads):
    return lax.ppermute(x, "head", [(i, (i + step) % heads) for i in range(heads)])


def after(x, *earlier):
    return lax.optimization_barrier((x, *earlier))[0]


def tie(chain, *arrived):
    return lax.optimization_barrier((chain, *arrived))


class GatherDp:
    def __init__(self, x, dp):
        self.x, self.dp = x, dp
        self.rows = x.shape[0]
        self.near = (dp_swap(x, 4, dp), dp_swap(x, 2, dp)) if dp == 8 else ()
        self.far = ()

    def go_far(self):
        if self.dp == 8:
            half = self.rows // 2
            part_y, part_x = self.near
            self.far = (dp_swap(part_y[:half], 2, self.dp), dp_swap(part_x[half:], 4, self.dp))

    def parts(self):
        dp = self.dp
        if dp == 8:
            here = [self.x, *self.near, *self.far]
            return here + [dp_swap(part, 1, dp) for part in here]
        whole = self.x
        bit = dp // 2
        while bit:
            whole = jnp.concatenate([whole, dp_swap(whole, bit, dp)], 0)
            bit //= 2
        return [whole]


def gather_head(x, heads):
    return [x] + [head_shift(x, heads - j, heads) for j in range(1, heads)]


def scatter_head(parts, heads):
    total = parts[0].astype(F32)
    for j in range(1, heads):
        total = total + head_shift(parts[j].astype(BF), j, heads).astype(F32)
    return total


def sum_head(x, heads):
    total = x
    for j in range(1, heads):
        total = total + head_shift(x, j, heads)
    return total


def sum_all(x, dp, heads):
    return sum_head(sum_dp(x, dp), heads)


def sum_dp(x, dp):
    bit = 1
    while bit < dp:
        x = x + dp_swap(x, bit, dp)
        bit *= 2
    return x


def stacked(refs):
    return refs[0][...] if len(refs) == 1 else jnp.concatenate([ref[...] for ref in refs], 0)


def lookup_kernel(vocab, tile, ids_ref, *refs):
    *table_refs, out_ref, rows_ref, acc_ref = refs
    step = pl.program_id(0)

    @pl.when(step == 0)
    def _():
        acc_ref[...] = jnp.zeros_like(acc_ref)

    place = lax.broadcasted_iota(jnp.int32, (1, tile), 1)
    block = stacked(table_refs)
    block = jnp.where(place < vocab - step * tile, block, jnp.zeros_like(block)).T
    rows_ref[...] = block
    hit = (ids_ref[...] - step * tile == place).astype(BF)
    acc_ref[...] += jnp.dot(hit, block, preferred_element_type=F32)

    @pl.when(step == pl.num_programs(0) - 1)
    def _():
        out_ref[...] = acc_ref[...].astype(BF)


def column_specs(parts, tile):
    return [pl.BlockSpec((part.shape[0], tile), lambda i: (0, i)) for part in parts]


def fixed(shape):
    return pl.BlockSpec(shape, lambda i: (0,) * len(shape))


VMEM_LIMIT = 56 * 2**20


def padded_to(columns, step=128):
    return -(-columns // step) * step


def lookup(ids, table_parts):
    rows, vocab = ids.shape[0], table_parts[0].shape[1]
    tile = 1024
    return pl.pallas_call(
        functools.partial(lookup_kernel, vocab, tile),
        out_shape=[
            jax.ShapeDtypeStruct((rows, D), BF),
            jax.ShapeDtypeStruct((padded_to(vocab), D), BF),
        ],
        grid=(pl.cdiv(vocab, tile),),
        in_specs=[fixed((rows, 1))] + column_specs(table_parts, tile),
        out_specs=[fixed((rows, D)), pl.BlockSpec((tile, D), lambda i: (i, 0))],
        scratch_shapes=[pltpu.VMEM((rows, D), F32)],
        compiler_params=pltpu.CompilerParams(vmem_limit_bytes=VMEM_LIMIT),
    )(ids.reshape(rows, 1), *table_parts)


def spread_kernel(tile, ids_ref, rows_ref, *refs):
    step = pl.program_id(0)
    turned_ref = refs[-1]

    @pl.when(step == 0)
    def _():
        turned_ref[...] = rows_ref[...].T

    place = step * tile + lax.broadcasted_iota(jnp.int32, (1, tile), 1)
    hit = (ids_ref[...] == place).astype(BF)
    total = jnp.dot(turned_ref[...], hit, preferred_element_type=F32)
    if len(refs) == 4:
        final_ref, slope_ref, out_ref, _ = refs
        out_ref[...] = total + lax.dot_general(
            final_ref[...], slope_ref[...], (((1,), (1,)), ((), ())), preferred_element_type=F32
        )
    else:
        base_ref, *keep_refs, send_ref, _ = refs
        total = base_ref[...] + total
        deep = D // 8
        for number, keep_ref in enumerate(keep_refs):
            keep_ref[...] = total[number * deep : (number + 1) * deep]
        send_ref[...] = total[D // 2 :].astype(BF)


def spread(ids, rows_low, columns, final_t=None, slope=None, base=None):
    rows = ids.shape[0]
    tile = 1024
    if base is None:
        shapes = [((D, columns), F32)]
        more = [final_t, slope]
        specs = [fixed(final_t.shape), pl.BlockSpec((tile, slope.shape[1]), lambda i: (i, 0))]
    else:
        shapes = [((D // 8, columns), F32)] * 4 + [((D // 2, columns), BF)]
        more = [base]
        specs = [pl.BlockSpec((D, tile), lambda i: (0, i))]
    return pl.pallas_call(
        functools.partial(spread_kernel, tile),
        out_shape=[jax.ShapeDtypeStruct(*shape) for shape in shapes],
        grid=(pl.cdiv(columns, tile),),
        in_specs=[fixed((rows, 1)), fixed((rows, D))] + specs,
        out_specs=[pl.BlockSpec((shape[0][0], tile), lambda i: (0, i)) for shape in shapes],
        scratch_shapes=[pltpu.VMEM((D, rows), BF)],
        compiler_params=pltpu.CompilerParams(vmem_limit_bytes=VMEM_LIMIT),
    )(ids.reshape(rows, 1), rows_low, *more)


def column_call(kernel, inputs, outputs, tile, sums=(), columns=None):
    columns = columns or inputs[0].shape[1]
    out_shape = [jax.ShapeDtypeStruct((rows, columns), dtype) for rows, dtype in outputs]
    out_specs = [pl.BlockSpec((rows, tile), lambda i: (0, i)) for rows, _ in outputs]
    for shape in sums:
        out_shape.append(jax.ShapeDtypeStruct(shape, F32))
        out_specs.append(fixed(shape))
    return pl.pallas_call(
        kernel,
        out_shape=out_shape,
        grid=(pl.cdiv(columns, tile),),
        in_specs=[
            pl.BlockSpec((array.shape[0], tile), lambda i: (0, i))
            if array.shape[1] >= columns
            else fixed(array.shape)
            for array in inputs
        ],
        out_specs=out_specs,
        compiler_params=pltpu.CompilerParams(vmem_limit_bytes=VMEM_LIMIT),
    )(*inputs)


def first_sums_kernel(y_ref, x_ref, d_ref, got_ref, d_low, d_high, x_low, y_high, y_low, x_high):
    deep = y_ref.shape[0]
    half = deep // 2
    got = got_ref[...].astype(F32)
    y = y_ref[...] + got[deep : 2 * deep]
    x = x_ref[...] + got[2 * deep : 3 * deep]
    d = (d_ref[...] + got[3 * deep :]).astype(BF)
    d_low[...] = d[:half]
    d_high[...] = d[half:]
    x_low[...] = x[:half].astype(BF)
    y_high[...] = y[half:].astype(BF)
    y_low[...] = y[:half]
    x_high[...] = x[half:]


def second_sums_kernel(y_low, got_a, x_high, got_b, y_out, x_out):
    y_out[...] = (y_low[...] + got_a[...].astype(F32)).astype(BF)
    x_out[...] = (x_high[...] + got_b[...].astype(F32)).astype(BF)


def lane_sums(value):
    rows, columns = value.shape
    total = value[:, :128]
    for start in range(128, columns, 128):
        total = total + value[:, start : start + 128]
    out = total[:8]
    for start in range(8, rows, 8):
        out = out + total[start : start + 8]
    return out


def inside(columns, tile, value):
    place = pl.program_id(0) * tile + lax.broadcasted_iota(jnp.int32, (1, tile), 1)
    return jnp.where(place < columns, value, 0.0)


def last_sums_kernel(columns, tile, own, got, x_low, y_high, y_low, x_high, out, squares):
    half = x_low.shape[0]
    low = own[:half] + got[:half].astype(F32) + (x_low[...].astype(F32) + y_low[...].astype(F32))
    high = (
        own[half:]
        + got[half : 2 * half].astype(F32)
        + (x_high[...].astype(F32) + y_high[...].astype(F32))
    )
    whole = jnp.concatenate([low, high], 0)
    out[...] = whole

    @pl.when(pl.program_id(0) == 0)
    def _():
        squares[...] = jnp.zeros_like(squares)

    squares[...] += lane_sums(inside(columns, tile, whole * whole))


class ScatterDp:
    def __init__(self, keeps, send, dp):
        self.keeps, self.dp = keeps, dp
        self.got = dp_swap(send, 1, dp)

    def run(self, columns, middle, late):
        dp = self.dp
        tile = 4096
        if dp != 8:
            total = jnp.concatenate(self.keeps, 0) + self.got.astype(F32)
            bit = 2
            while bit < dp:
                rows = total.shape[0] // 2
                total = total[:rows] + dp_swap(total[rows:].astype(BF), bit, dp).astype(F32)
                bit *= 2
            total = total[:, :columns]
            squares = jnp.sum(total * total)
            return total, jnp.zeros((8, 128), F32).at[0, 0].set(squares)
        own, y, x, d = self.keeps
        half = own.shape[0] // 2
        d_low, d_high, x_low, y_high, y_low, x_high = column_call(
            first_sums_kernel, [y, x, d, self.got], [(half, BF)] * 4 + [(half, F32)] * 2, tile
        )
        got_a, got_b = dp_swap(d_low, 2, dp), dp_swap(d_high, 4, dp)
        x_low, y_high = dp_swap(x_low, 2, dp), dp_swap(y_high, 4, dp)
        got_a, *middle[:] = tie(got_a, *middle)
        y_low, x_high = column_call(
            second_sums_kernel, [y_low, got_a, x_high, got_b], [(half, BF)] * 2, tile
        )
        y_low, x_high = dp_swap(y_low, 4, dp), dp_swap(x_high, 2, dp)
        y_low, *late[:] = tie(y_low, *late)
        return column_call(
            functools.partial(last_sums_kernel, columns, tile),
            [own, self.got, x_low, y_high, y_low, x_high],
            [(2 * half, F32)],
            tile,
            sums=[(8, 128)],
            columns=columns,
        )


def logits_kernel(vocab, tile, final_ref, label_ref, teacher_ref, table_ref, out_ref, *stats):
    top_s, top_t, one, half, teach, cross, label = stats
    step = pl.program_id(0)
    last = pl.num_programs(0) - 1

    @pl.when(step == 0)
    def _():
        top_s[...] = jnp.full_like(top_s, -1e30)
        top_t[...] = jnp.full_like(top_t, -1e30)
        for ref in (one, half, teach, cross, label):
            ref[...] = jnp.zeros_like(ref)

    def work(valid):
        logits = jnp.dot(table_ref[...], final_ref[...], preferred_element_type=F32)
        tokens = logits.shape[1]

        def folded(value):
            return value.reshape(tile // 8, 8, tokens)

        student = folded(logits)
        teacher = folded(teacher_ref[...].astype(F32))
        place = 8 * lax.broadcasted_iota(jnp.int32, (tile // 8, 8, 1), 0)
        place = place + lax.broadcasted_iota(jnp.int32, (tile // 8, 8, 1), 1)
        if valid < tile:
            student = jnp.where(place < valid, student, -1e30)
            teacher = jnp.where(place < valid, teacher, -1e30)
        old_s, old_t = top_s[...], top_t[...]
        new_s = jnp.maximum(old_s, jnp.max(student, 0))
        new_t = jnp.maximum(old_t, jnp.max(teacher, 0))
        top_s[...] = new_s
        top_t[...] = new_t
        scale_s = jnp.exp((old_s - new_s) * 0.5)
        scale_t = jnp.exp((old_t - new_t) * 0.5)
        e = jnp.exp((student - new_s[None]) * 0.5)
        half[...] = half[...] * scale_s + jnp.sum(e, 0)
        one[...] = one[...] * (scale_s * scale_s) + jnp.sum(e * e, 0)
        e = jnp.exp((teacher - new_t[None]) * 0.5)
        teach[...] = teach[...] * scale_t + jnp.sum(e, 0)
        cross[...] = cross[...] * scale_t + jnp.sum(e * (teacher - student), 0)
        labels = (label_ref[...] - step * tile)[None]
        label[...] += jnp.sum(jnp.where(labels == place, student, 0.0), 0)

    rest = vocab - (pl.cdiv(vocab, tile) - 1) * tile
    if rest == tile:
        work(tile)
    else:

        @pl.when(step < last)
        def _():
            work(tile)

        @pl.when(step == last)
        def _():
            work(rest)

    @pl.when(step == last)
    def _():
        peak_s = jnp.max(top_s[...], 0, keepdims=True)
        peak_t = jnp.max(top_t[...], 0, keepdims=True)
        by_s = jnp.exp((top_s[...] - peak_s) * 0.5)
        by_t = jnp.exp((top_t[...] - peak_t) * 0.5)

        def total(value):
            return jnp.sum(value, 0, keepdims=True)

        out_ref[0:1] = peak_s
        out_ref[1:2] = peak_t
        out_ref[2:3] = total(one[...] * (by_s * by_s))
        out_ref[3:4] = total(half[...] * by_s)
        out_ref[4:5] = total(teach[...] * by_t)
        out_ref[5:6] = total(cross[...] * by_t) * 0.5
        out_ref[6:7] = total(label[...])
        out_ref[7:8] = jnp.zeros_like(peak_s)


def logits_stats(final_t, labels, teacher_t, table_rows):
    vocab, tokens = teacher_t.shape
    tile = 1024
    return pl.pallas_call(
        functools.partial(logits_kernel, vocab, tile),
        out_shape=jax.ShapeDtypeStruct((8, tokens), F32),
        grid=(pl.cdiv(vocab, tile),),
        in_specs=[
            fixed(final_t.shape),
            fixed((1, tokens)),
            pl.BlockSpec((tile, tokens), lambda i: (i, 0)),
            pl.BlockSpec((tile, D), lambda i: (i, 0)),
        ],
        out_specs=fixed((8, tokens)),
        scratch_shapes=[pltpu.VMEM((8, tokens), F32)] * 7,
        compiler_params=pltpu.CompilerParams(vmem_limit_bytes=VMEM_LIMIT),
    )(final_t, labels.reshape(1, tokens), teacher_t, table_rows)


def logits_back_kernel(vocab, tile, final_ref, label_ref, scalar_ref, teacher_ref, *refs):
    rows_ref, *table_refs, slope_ref, back_ref, acc_ref = refs
    step = pl.program_id(0)
    last = pl.num_programs(0) - 1

    @pl.when(step == 0)
    def _():
        acc_ref[...] = jnp.zeros_like(acc_ref)

    good = lax.broadcasted_iota(jnp.int32, (1, tile), 1) < vocab - step * tile
    block = stacked(table_refs)
    block = jnp.where(good, block, jnp.zeros_like(block))
    place = lax.broadcasted_iota(jnp.int32, (tile, 1), 0)
    logits = jnp.dot(rows_ref[...], final_ref[...], preferred_element_type=F32)
    lse_half = scalar_ref[0:1]
    lse_teacher = scalar_ref[1:2]
    soft_one = scalar_ref[2:3]
    soft_half = scalar_ref[3:4]
    weight = scalar_ref[4:5]
    student = jnp.exp(logits * 0.5 - lse_half)
    teacher = jnp.exp(teacher_ref[...].astype(F32) * 0.5 - lse_teacher)
    labels = label_ref[...] - step * tile
    slope = student * (soft_one * student + soft_half) - soft_half * teacher
    slope = slope - jnp.where(labels == place, weight, 0.0)
    slope = jnp.where(place < vocab - step * tile, slope, 0.0).astype(BF)
    slope_ref[...] = slope
    acc_ref[...] += jnp.dot(block, slope, preferred_element_type=F32)

    @pl.when(step == last)
    def _():
        back_ref[...] = acc_ref[...].astype(BF)


def logits_back(final_t, labels, scalars, teacher_t, table_rows, table_parts):
    vocab, tokens = teacher_t.shape
    tile = 1024
    return pl.pallas_call(
        functools.partial(logits_back_kernel, vocab, tile),
        out_shape=[
            jax.ShapeDtypeStruct((padded_to(vocab), tokens), BF),
            jax.ShapeDtypeStruct((D, tokens), BF),
        ],
        grid=(pl.cdiv(vocab, tile),),
        in_specs=[
            fixed(final_t.shape),
            fixed((1, tokens)),
            fixed(scalars.shape),
            pl.BlockSpec((tile, tokens), lambda i: (i, 0)),
            pl.BlockSpec((tile, D), lambda i: (i, 0)),
        ]
        + column_specs(table_parts, tile),
        out_specs=[pl.BlockSpec((tile, tokens), lambda i: (i, 0)), fixed((D, tokens))],
        scratch_shapes=[pltpu.VMEM((D, tokens), F32)],
        compiler_params=pltpu.CompilerParams(vmem_limit_bytes=VMEM_LIMIT),
    )(final_t, labels.reshape(1, tokens), scalars, teacher_t, table_rows, *table_parts)


BIAS_ONE = 1.0 - BETA_ONE**STEP_NUM
BIAS_TWO = 1.0 - BETA_TWO**STEP_NUM


def lamb(weight, moment, second, grad, clip):
    grad = grad * clip
    moment = BETA_ONE * moment + (1 - BETA_ONE) * grad
    second = BETA_TWO * second + (1 - BETA_TWO) * grad * grad
    update = (
        moment * (1.0 / BIAS_ONE) / (jnp.sqrt(second * (1.0 / BIAS_TWO)) + ADAM_EPS)
        + WEIGHT_DECAY * weight
    )
    return moment, second, update


def lamb_columns_kernel(columns, tile, w, m, v, g, clip, m_out, v_out, u_out, squares):
    moment, second, update = lamb(w[...], m[...], v[...], g[...], clip[0:1, 0:1])
    m_out[...] = moment
    v_out[...] = second
    u_out[...] = update

    @pl.when(pl.program_id(0) == 0)
    def _():
        squares[...] = jnp.zeros_like(squares)

    squares[...] += lane_sums(inside(columns, tile, update * update))


def lamb_matrices_kernel(places, clip_ref, *refs):
    grads = refs[:2]
    count = len(places)
    states = refs[2 : 2 + 3 * count]
    outs = refs[2 + 3 * count : -1]
    squares = refs[-1]
    squares[...] = jnp.zeros_like(squares)
    clip = clip_ref[0:1, 0:1]
    row = 0
    for group, matrices in enumerate(places):
        w, m, v = states[3 * group : 3 * group + 3]
        m_out, v_out, u_out = outs[3 * group : 3 * group + 3]
        width = w.shape[-1]
        for number, (array, start) in enumerate(matrices):
            grad = grads[array][:, start : start + width]
            moment, second, update = lamb(w[number], m[number], v[number], grad, clip)
            m_out[number] = moment
            v_out[number] = second
            u_out[number] = update
            total = jnp.sum(update * update, 0, keepdims=True)
            lanes = min(128, width)
            line = total[:, :lanes]
            for first in range(lanes, width, lanes):
                line = line + total[:, first : first + lanes]
            squares[row : row + 1, :lanes] = line
            row += 1


def lamb_matrices(clip, grads, groups, places):
    flat = [array for group in groups for array in group]
    shapes = [jax.ShapeDtypeStruct(group[0].shape, F32) for group in groups for _ in range(3)]
    rows = 8 * pl.cdiv(sum(len(matrices) for matrices in places), 8)
    return pl.pallas_call(
        functools.partial(lamb_matrices_kernel, places),
        out_shape=shapes + [jax.ShapeDtypeStruct((rows, 128), F32)],
        compiler_params=pltpu.CompilerParams(vmem_limit_bytes=VMEM_LIMIT),
    )(clip, *grads, *flat)


def pack_kernel(heads_of, *refs):
    *in_refs, out_ref = refs
    start = 0
    for number, index in heads_of:
        value = in_refs[number][...] if index is None else in_refs[number][index]
        out_ref[:, start : start + value.shape[1]] = value.astype(BF)
        start += value.shape[1]


def pack(arrays, plan):
    columns = sum(arrays[number].shape[-1] for number, _ in plan)
    return pl.pallas_call(
        functools.partial(pack_kernel, plan),
        out_shape=jax.ShapeDtypeStruct((arrays[0].shape[-2], columns), BF),
        compiler_params=pltpu.CompilerParams(vmem_limit_bytes=VMEM_LIMIT),
    )(*arrays)


def dot(a, b):
    return jnp.dot(a, b, preferred_element_type=F32)


def dot_nt(a, b):
    return lax.dot_general(a, b, (((1,), (1,)), ((), ())), preferred_element_type=F32)


def dot_tn(a, b):
    return lax.dot_general(a, b, (((0,), (0,)), ((), ())), preferred_element_type=F32)


def root(inputs):
    return lax.rsqrt(jnp.mean(inputs * inputs, -1, keepdims=True) + NORM_EPS)


def normed(inputs, gain_row):
    return (inputs * root(inputs) * gain_row).astype(BF)


def norm_back(inputs, gain_row, upstream):
    factor = root(inputs)
    scaled = upstream * gain_row
    inner = jnp.mean(scaled * inputs, -1, keepdims=True)
    return (
        factor * (scaled - inputs * factor * factor * inner),
        jnp.sum(upstream * inputs * factor, axis=0, keepdims=True),
    )


def attn_probs(query, keys_all, allowed):
    scores = jnp.where(allowed, dot_nt(query, keys_all) * DH ** (-0.5), -1000000000.0)
    grown = jnp.exp(scores - jnp.max(scores, -1, keepdims=True))
    return grown * (1.0 / jnp.sum(grown, -1, keepdims=True))


def key_mask(count, keys):
    return lax.broadcasted_iota(jnp.int32, (1, keys), 1) < count


def causal_mask(rows):
    return lax.broadcasted_iota(jnp.int32, (rows, rows), 0) >= lax.broadcasted_iota(
        jnp.int32, (rows, rows), 1
    )


def weights_of(ref, order_ref, start, stop):
    return jnp.concatenate(
        [ref[order_ref[place], 0, :, start:stop] for place in range(ref.shape[0])], 0
    )


def attend_heads(query, keys_all, values, each, mask_of):
    rows, source = query.shape[0] // each, keys_all.shape[0] // each
    out = []
    for number in range(each):
        a, b = number * rows, number * source
        line = []
        for first in range(0, query.shape[1], DH):
            probs = attn_probs(
                query[a : a + rows, first : first + DH],
                keys_all[b : b + source, first : first + DH],
                mask_of(number),
            ).astype(BF)
            line.append(dot(probs, values[b : b + source, first : first + DH]).astype(BF))
        out.append(jnp.concatenate(line, 1) if len(line) > 1 else line[0])
    return jnp.concatenate(out, 0) if each > 1 else out[0]


def attend_heads_back(query, keys_all, values, grad_mixed, each, mask_of):
    rows, source = query.shape[0] // each, keys_all.shape[0] // each
    outs = ([], [], [])
    for number in range(each):
        a, b = number * rows, number * source
        lines = ([], [], [])
        for first in range(0, query.shape[1], DH):
            q = query[a : a + rows, first : first + DH]
            k = keys_all[b : b + source, first : first + DH]
            v = values[b : b + source, first : first + DH]
            g = grad_mixed[a : a + rows, first : first + DH]
            probs = attn_probs(q, k, mask_of(number))
            grad_probs = dot_nt(g, v)
            slope = probs * (grad_probs - jnp.sum(grad_probs * probs, -1, keepdims=True))
            slope = slope.astype(BF)
            lines[0].append((dot(slope, k) * DH ** (-0.5)).astype(BF))
            lines[1].append((dot_tn(slope, q) * DH ** (-0.5)).astype(BF))
            lines[2].append(dot_tn(probs.astype(BF), g).astype(BF))
        for out, line in zip(outs, lines, strict=True):
            out.append(jnp.concatenate(line, 1) if len(line) > 1 else line[0])
    return [jnp.concatenate(out, 0) if each > 1 else out[0] for out in outs]


def at_phase(step, phase, heads):
    return jnp.clip(step - phase * heads, 0, heads - 1)


class Layers:
    def __init__(self, order, head_pos, lens, weights, gain, each):
        self.prefetch = (order, head_pos.reshape(1), lens)
        self.weights, self.gain, self.each = weights, gain, each
        self.dp, self.heads, self.deep, _ = weights.shape
        self.width = 4 * D // self.heads
        self.unit = self.width // 4

    def weight_spec(self, block, phase):
        heads = self.heads

        def index(step, order, head, lens):
            return (0, lax.rem(head[0] + at_phase(step, phase, heads), heads), 0, block)

        return pl.BlockSpec((self.dp, 1, self.deep, self.width), index)

    def kept_spec(self, shape, phase):
        heads = self.heads
        return pl.BlockSpec(
            (1,) + shape[1:], lambda step, *_: (at_phase(step, phase, heads), 0, 0)
        )

    @staticmethod
    def whole(shape):
        return pl.BlockSpec(shape, lambda *_: (0,) * len(shape))

    def call(self, kernel, phases, arrays, outs, scratch):
        return pl.pallas_call(
            kernel,
            out_shape=[jax.ShapeDtypeStruct(shape, dtype) for shape, dtype, _ in outs],
            grid_spec=pltpu.PrefetchScalarGridSpec(
                num_scalar_prefetch=3,
                grid=(phases * self.heads,),
                in_specs=[spec or self.whole(array.shape) for array, spec in arrays],
                out_specs=[spec or self.whole(shape) for shape, _, spec in outs],
                scratch_shapes=[pltpu.VMEM(shape, dtype) for shape, dtype in scratch],
            ),
            compiler_params=pltpu.CompilerParams(vmem_limit_bytes=VMEM_LIMIT),
        )(*self.prefetch, *[array for array, _ in arrays])

    def encoder(self, x):
        heads, each, unit, width = self.heads, self.each, self.unit, self.width
        rows = x.shape[0]

        def kernel(order, head, lens, x_ref, gain, a_ref, u_ref, d_ref, *refs):
            kept, mid, hidden, last, encoded, low, acc = refs
            step = pl.program_id(0)

            @pl.when(step == 0)
            def _():
                acc[...] = x_ref[...]
                low[...] = normed(x_ref[...], gain[0:1])

            @pl.when(step < heads)
            def _():
                w = weights_of(a_ref, order, 0, width)
                qkv = dot(low[...], w[:, : 3 * unit]).astype(BF)
                mixed = attend_heads(
                    qkv[:, :unit],
                    qkv[:, unit : 2 * unit],
                    qkv[:, 2 * unit :],
                    each,
                    lambda n: key_mask(lens[n], rows // each),
                )
                kept[0, :, : 3 * unit] = qkv
                kept[0, :, 3 * unit :] = mixed
                acc[...] += dot_nt(mixed, w[:, 3 * unit :])

            @pl.when(step == heads)
            def _():
                mid[...] = acc[...]
                low[...] = normed(acc[...], gain[1:2])

            @pl.when(step >= heads)
            def _():
                grown = jax.nn.relu(dot(low[...], weights_of(u_ref, order, 0, width))).astype(BF)
                hidden[0] = grown
                acc[...] += dot_nt(grown, weights_of(d_ref, order, 0, width))

            @pl.when(step == 2 * heads - 1)
            def _():
                last[...] = acc[...]
                encoded[...] = normed(acc[...], gain[2:3])

        shape = (heads, rows, width)
        return self.call(
            kernel,
            2,
            [(x, None), (self.gain, None)]
            + [(self.weights, self.weight_spec(*at)) for at in ((0, 0), (1, 1), (2, 1))],
            [
                (shape, BF, self.kept_spec(shape, 0)),
                ((rows, D), F32, None),
                (shape, BF, self.kept_spec(shape, 1)),
                ((rows, D), F32, None),
                ((rows, D), BF, None),
            ],
            [((rows, D), BF), ((rows, D), F32)],
        )

    def decoder(self, x, encoded):
        heads, each, unit, width = self.heads, self.each, self.unit, self.width
        rows, source = x.shape[0], encoded.shape[0]

        def kernel(order, head, lens, x_ref, enc_ref, gain, s_ref, c_ref, u_ref, d_ref, *refs):
            kept, one, kept_q, kept_k, two, hidden, three, final, low, acc = refs
            step = pl.program_id(0)

            @pl.when(step == 0)
            def _():
                acc[...] = x_ref[...]
                low[...] = normed(x_ref[...], gain[3:4])

            @pl.when(step < heads)
            def _():
                w = weights_of(s_ref, order, 0, width)
                qkv = dot(low[...], w[:, : 3 * unit]).astype(BF)
                mixed = attend_heads(
                    qkv[:, :unit],
                    qkv[:, unit : 2 * unit],
                    qkv[:, 2 * unit :],
                    each,
                    lambda n: causal_mask(rows // each),
                )
                kept[0, :, : 3 * unit] = qkv
                kept[0, :, 3 * unit :] = mixed
                acc[...] += dot_nt(mixed, w[:, 3 * unit :])

            @pl.when(step == heads)
            def _():
                one[...] = acc[...]
                low[...] = normed(acc[...], gain[4:5])

            @pl.when((step >= heads) & (step < 2 * heads))
            def _():
                w = weights_of(c_ref, order, 0, width)
                query = dot(low[...], w[:, :unit]).astype(BF)
                both = dot(enc_ref[...], w[:, unit : 3 * unit]).astype(BF)
                mixed = attend_heads(
                    query,
                    both[:, :unit],
                    both[:, unit:],
                    each,
                    lambda n: key_mask(lens[n], source // each),
                )
                kept_q[0, :, :unit] = query
                kept_q[0, :, unit:] = mixed
                kept_k[0] = both
                acc[...] += dot_nt(mixed, w[:, 3 * unit :])

            @pl.when(step == 2 * heads)
            def _():
                two[...] = acc[...]
                low[...] = normed(acc[...], gain[5:6])

            @pl.when(step >= 2 * heads)
            def _():
                grown = jax.nn.relu(dot(low[...], weights_of(u_ref, order, 0, width))).astype(BF)
                hidden[0] = grown
                acc[...] += dot_nt(grown, weights_of(d_ref, order, 0, width))

            @pl.when(step == 3 * heads - 1)
            def _():
                three[...] = acc[...]
                final[...] = normed(acc[...], gain[6:7] * D ** (-0.5))

        shape = (heads, rows, width)
        shape_q, shape_k = (heads, rows, 2 * unit), (heads, source, 2 * unit)
        return self.call(
            kernel,
            3,
            [(x, None), (encoded, None), (self.gain, None)]
            + [(self.weights, self.weight_spec(*at)) for at in ((3, 0), (4, 1), (5, 2), (6, 2))],
            [
                (shape, BF, self.kept_spec(shape, 0)),
                ((rows, D), F32, None),
                (shape_q, BF, self.kept_spec(shape_q, 1)),
                (shape_k, BF, self.kept_spec(shape_k, 1)),
                ((rows, D), F32, None),
                (shape, BF, self.kept_spec(shape, 2)),
                ((rows, D), F32, None),
                ((rows, D), BF, None),
            ],
            [((rows, D), BF), ((rows, D), F32)],
        )

    def put(self, out_ref, order, j, start, value):
        low = value.astype(BF)
        for place in range(self.dp):
            out_ref[order[place], j, :, start : start + value.shape[1]] = low[
                place * self.deep : (place + 1) * self.deep
            ]

    def feed_step(self, order, j, u_ref, d_ref, hidden, out, at, low, up_t, in_t, back):
        width = self.width
        up, down = weights_of(u_ref, order, 0, width), weights_of(d_ref, order, 0, width)
        grad_pre = jnp.where(hidden > 0, dot(low[...], down), 0.0).astype(BF)
        self.put(out, order, j, at, dot(in_t[...], grad_pre))
        self.put(out, order, j, at + width, dot(up_t[...], hidden))
        back[...] += dot_nt(grad_pre, up)

    def decoder_back(self, grad_final, x, encoded, kept_all):
        heads, each, unit, width = self.heads, self.each, self.unit, self.width
        kept, one, kept_q, kept_k, two, hidden, three = kept_all
        rows, source = x.shape[0], encoded.shape[0]

        def kernel(order, head, lens, *refs):
            g_ref, x_ref, enc_ref, gain, one, two, three, kept, kept_q, kept_k, hid = refs[:11]
            s_ref, c_ref, u_ref, d_ref = refs[11:15]
            out, gains_out, grad_enc, grad_x = refs[15:19]
            grad, low, up_t, in_t, enc_t, back = refs[19:]
            step = pl.program_id(0)

            def enter(value, inputs, gain_row):
                grad[...] = value
                low[...] = value.astype(BF)
                up_t[...] = low[...].T
                in_t[...] = normed(inputs, gain_row).T
                back[...] = jnp.zeros_like(back)

            @pl.when(step == 0)
            def _():
                gains_out[...] = jnp.zeros_like(gains_out)
                value, slope = norm_back(three[...], gain[6:7] * D ** (-0.5), g_ref[...])
                gains_out[6:7] = slope * D ** (-0.5)
                enter(value, two[...], gain[5:6])

            @pl.when(step < heads)
            def _():
                self.feed_step(
                    order, step, u_ref, d_ref, hid[0], out, 2 * width, low, up_t, in_t, back
                )

            @pl.when(step == heads)
            def _():
                value, slope = norm_back(two[...], gain[5:6], back[...])
                gains_out[5:6] = slope
                enter(grad[...] + value, one[...], gain[4:5])
                enc_t[...] = enc_ref[...].T
                grad_enc[...] = jnp.zeros_like(grad_enc)

            @pl.when((step >= heads) & (step < 2 * heads))
            def _():
                j = step - heads
                w = weights_of(c_ref, order, 0, width)
                grad_mixed = dot(low[...], w[:, 3 * unit :]).astype(BF)
                query, mixed = kept_q[0, :, :unit], kept_q[0, :, unit:]
                dq, dk, dv = attend_heads_back(
                    query,
                    kept_k[0, :, :unit],
                    kept_k[0, :, unit:],
                    grad_mixed,
                    each,
                    lambda n: key_mask(lens[n], source // each),
                )
                both = jnp.concatenate([dk, dv], 1)
                self.put(out, order, j, width, dot(in_t[...], dq))
                self.put(out, order, j, width + unit, dot(enc_t[...], both))
                self.put(out, order, j, width + 3 * unit, dot(up_t[...], mixed))
                back[...] += dot_nt(dq, w[:, :unit])
                grad_enc[...] += dot_nt(both, w[:, unit : 3 * unit])

            @pl.when(step == 2 * heads)
            def _():
                value, slope = norm_back(one[...], gain[4:5], back[...])
                gains_out[4:5] = slope
                enter(grad[...] + value, x_ref[...], gain[3:4])

            @pl.when(step >= 2 * heads)
            def _():
                self.self_step(
                    order, step - 2 * heads, s_ref, kept, out, 0, low, up_t, in_t, back,
                    lambda n: causal_mask(rows // each),
                )

            @pl.when(step == 3 * heads - 1)
            def _():
                value, slope = norm_back(x_ref[...], gain[3:4], back[...])
                gains_out[3:4] = slope
                grad_x[...] = (grad[...] + value).astype(BF)

        return self.call(
            kernel,
            3,
            [
                (grad_final, None),
                (x, None),
                (encoded, None),
                (self.gain, None),
                (one, None),
                (two, None),
                (three, None),
                (kept, self.kept_spec(kept.shape, 2)),
                (kept_q, self.kept_spec(kept_q.shape, 1)),
                (kept_k, self.kept_spec(kept_k.shape, 1)),
                (hidden, self.kept_spec(hidden.shape, 0)),
            ]
            + [(self.weights, self.weight_spec(*at)) for at in ((3, 2), (4, 1), (5, 0), (6, 0))],
            [
                ((self.dp, heads, self.deep, 4 * width), BF, None),
                ((8, D), F32, None),
                ((source, D), F32, None),
                ((rows, D), BF, None),
            ],
            [
                ((rows, D), F32),
                ((rows, D), BF),
                ((D, rows), BF),
                ((D, rows), BF),
                ((D, source), BF),
                ((rows, D), F32),
            ],
        )

    def self_step(self, order, j, a_ref, kept, out, at, low, up_t, in_t, back, mask_of):
        unit, width = self.unit, self.width
        w = weights_of(a_ref, order, 0, width)
        grad_mixed = dot(low[...], w[:, 3 * unit :]).astype(BF)
        slopes = attend_heads_back(
            kept[0, :, :unit],
            kept[0, :, unit : 2 * unit],
            kept[0, :, 2 * unit : 3 * unit],
            grad_mixed,
            self.each,
            mask_of,
        )
        three = jnp.concatenate(slopes, 1)
        self.put(out, order, j, at, dot(in_t[...], three))
        self.put(out, order, j, at + 3 * unit, dot(up_t[...], kept[0, :, 3 * unit :]))
        back[...] += dot_nt(three, w[:, : 3 * unit])

    def encoder_back(self, grad_encoded, gain_grads, x, kept_all, lanes):
        heads, each, width = self.heads, self.each, self.width
        kept, mid, hidden, last = kept_all
        rows = x.shape[0]

        def kernel(order, head, lens, *refs):
            g_ref, more_ref, x_ref, gain, mid, last, kept, hid, a_ref, u_ref, d_ref = refs[:11]
            out, grad_x = refs[11:13]
            grad, low, up_t, in_t, back, gains = refs[13:]
            step = pl.program_id(0)

            def enter(value, inputs, gain_row):
                grad[...] = value
                low[...] = value.astype(BF)
                up_t[...] = low[...].T
                in_t[...] = normed(inputs, gain_row).T
                back[...] = jnp.zeros_like(back)

            @pl.when(step == 0)
            def _():
                gains[...] = jnp.zeros_like(gains)
                gains[0:8] = more_ref[...]
                value, slope = norm_back(last[...], gain[2:3], g_ref[...])
                gains[2:3] = slope
                enter(value, mid[...], gain[1:2])

            @pl.when(step < heads)
            def _():
                self.feed_step(
                    order, step, u_ref, d_ref, hid[0], out, width, low, up_t, in_t, back
                )

            @pl.when(step == heads)
            def _():
                value, slope = norm_back(mid[...], gain[1:2], back[...])
                gains[1:2] = slope
                enter(grad[...] + value, x_ref[...], gain[0:1])

            @pl.when(step >= heads)
            def _():
                self.self_step(
                    order, step - heads, a_ref, kept, out, 0, low, up_t, in_t, back,
                    lambda n: key_mask(lens[n], rows // each),
                )

            @pl.when(step == 2 * heads - 1)
            def _():
                value, slope = norm_back(x_ref[...], gain[0:1], back[...])
                gains[0:1] = slope
                grad_x[...] = (grad[...] + value).astype(BF)
                turned = gains[...].T
                for j in range(heads):
                    self.put(out, order, j, 3 * width, turned)

        return self.call(
            kernel,
            2,
            [
                (grad_encoded, None),
                (gain_grads, None),
                (x, None),
                (self.gain, None),
                (mid, None),
                (last, None),
                (kept, self.kept_spec(kept.shape, 1)),
                (hidden, self.kept_spec(hidden.shape, 0)),
            ]
            + [(self.weights, self.weight_spec(*at)) for at in ((0, 1), (1, 0), (2, 0))],
            [
                ((self.dp, heads, self.deep, 3 * width + lanes), BF, None),
                ((rows, D), BF, None),
            ],
            [
                ((rows, D), F32),
                ((rows, D), BF),
                ((D, rows), BF),
                ((D, rows), BF),
                ((rows, D), F32),
                ((lanes, D), F32),
            ],
        )


def body(
    dp,
    heads,
    source_ids,
    target_ids,
    source_lens,
    target_lens,
    kl_mask,
    teacher,
    *state,
):
    def transposed(group):
        embed, attn_in, attn_out, ff_in, ff_out, gains = group
        swap = functools.partial(jnp.swapaxes, axis1=-1, axis2=-2)
        return (swap(embed), attn_in, swap(attn_out), ff_in, swap(ff_out), gains)

    masters = transposed(state[:6])
    moments = transposed(state[6:12])
    seconds = transposed(state[12:])
    embed_t, attn_in, attn_out_t, ff_in, ff_out_t, gains = masters
    low = embed_t.astype(BF)
    vocab_local = embed_t.shape[1]
    head_pos = lax.axis_index("head")
    lead = (head_pos == 0).astype(F32)
    vocab_start = head_pos * vocab_local
    batch_size, source_len = source_ids.shape
    target_len = target_ids.shape[1]
    token_count = batch_size * target_len
    each = -(-batch_size // heads)
    padded = each * heads

    sides = [
        [attn_in[0, 0], attn_in[0, 1], attn_in[0, 2], attn_out_t[0], ff_in[0], ff_out_t[0]],
        [attn_in[1, 0], attn_in[1, 1], attn_in[1, 2], attn_out_t[1]]
        + [attn_in[2, 0], attn_in[2, 1], attn_in[2, 2], attn_out_t[2], ff_in[1], ff_out_t[1]],
    ]
    widths = [[matrix.shape[-1] for matrix in side] for side in sides]
    lanes = 128
    gain_rows = gains.shape[0]
    counted = jnp.full((1, gains.shape[1]), jnp.sum((target_lens > 0).astype(F32)))
    gain_block = jnp.pad(
        jnp.concatenate([gains, counted], 0).T, ((0, 0), (0, lanes - gain_rows - 1))
    )
    places = [0]
    bit = dp // 2
    while bit:
        places = places + [place ^ bit for place in places]
        bit //= 2
    order = lax.axis_index("dp") ^ jnp.array(places, jnp.int32)
    flat_in = attn_in.reshape((9,) + attn_in.shape[2:])
    arrays = [flat_in, attn_out_t, ff_in, ff_out_t, gain_block]
    plan = [(0, 0), (0, 1), (0, 2), (1, 0), (2, 0), (3, 0)]
    plan += [(0, 3), (0, 4), (0, 5), (1, 1), (0, 6), (0, 7), (0, 8), (1, 2), (2, 1), (3, 1)]
    packed = pack(arrays, plan + [(4, None)])
    low, packed = tie(low, packed)
    weights = lax.all_gather(packed, ("dp", "head"), axis=0)
    weights = weights.reshape((dp, heads) + packed.shape)
    table = GatherDp(low, dp)
    table.go_far()
    table_parts = table.parts()

    def fill(array):
        return jnp.pad(array, ((0, padded - batch_size),) + ((0, 0),) * (array.ndim - 1))

    dec_ids = jnp.concatenate([jnp.zeros((batch_size, 1), jnp.int32), target_ids[:, :-1]], 1)
    enc_ids = jnp.roll(fill(source_ids).reshape(heads, -1), -head_pos, 0) - vocab_start
    dec_ids = jnp.roll(fill(dec_ids).reshape(heads, -1), -head_pos, 0) - vocab_start
    enc_rows_count = heads * each * source_len
    looked, table_rows = lookup(
        jnp.concatenate([enc_ids.reshape(-1), dec_ids.reshape(-1)]), table_parts
    )
    enc_looked = looked[:enc_rows_count].reshape(heads, -1, D)
    dec_looked = looked[enc_rows_count:]
    came = [enc_looked[0]] + [head_shift(enc_looked[j], j, heads) for j in range(1, heads)]
    gain = jnp.take(weights[:, 0, :, sum(widths[0]) + sum(widths[1]) :], order, axis=0)
    gain = gain[..., :8].astype(F32).reshape(D, 8).T
    real_count = jnp.maximum(jnp.sum(gain[gain_rows].reshape(dp, -1)[:, 0]), 1.0)
    my_lens = lax.dynamic_slice_in_dim(fill(source_lens), head_pos * each, each)
    layers = Layers(order, head_pos, my_lens, weights, gain, each)
    enc_embed = functools.reduce(jnp.add, came).astype(F32)
    *kept_enc, encoded = layers.encoder(enc_embed)
    looked, encoded = tie(dec_looked, encoded)
    looked = looked.reshape(heads, -1, D)
    dec_came = [looked[0]] + [head_shift(looked[j], j, heads) for j in range(1, heads)]
    dec_embed = functools.reduce(jnp.add, dec_came).astype(F32)
    *kept_dec, my_final = layers.decoder(dec_embed, encoded)

    final = jnp.concatenate(gather_head(my_final, heads), 0)
    final = jnp.roll(final, head_pos * each * target_len, 0)[:token_count]
    valid = (jnp.arange(target_len)[None, :] < target_lens[:, None]).astype(F32)
    token_weight = (
        valid / (jnp.maximum(target_lens, 1).astype(F32)[:, None] * real_count)
    ).reshape(token_count)
    divergence_mask = kl_mask.astype(F32).reshape(token_count)
    labels = target_ids.reshape(token_count) - vocab_start
    labels = jnp.where((labels >= 0) & (labels < vocab_local), labels, -1)
    final_t = final.T
    teacher_t = teacher.T
    stats = logits_stats(final_t, labels, teacher_t, table_rows)
    every = jnp.stack(gather_head(stats, heads))
    peak_student = jnp.max(every[:, 0], 0)
    peak_teacher = jnp.max(every[:, 1], 0)
    off_s = every[:, 0] - peak_student
    off_t = jnp.exp((every[:, 1] - peak_teacher) / SOFTEN_FACTOR)
    sum_one = jnp.sum(every[:, 2] * jnp.exp(off_s), 0)
    sum_half = jnp.sum(every[:, 3] * jnp.exp(off_s / SOFTEN_FACTOR), 0)
    sum_teacher = jnp.sum(every[:, 4] * off_t, 0)
    sum_cross = jnp.sum(every[:, 5] * off_t, 0)
    label_logprob = jnp.sum(every[:, 6], 0)
    lse_one = peak_student + jnp.log(sum_one)
    lse_half = peak_student / SOFTEN_FACTOR + jnp.log(sum_half)
    lse_teacher = peak_teacher / SOFTEN_FACTOR + jnp.log(sum_teacher)
    cross_entropy = lse_one - label_logprob
    divergence_value = sum_cross / sum_teacher - lse_teacher + lse_half
    loss_part = lead * jnp.sum(
        token_weight
        * (
            cross_entropy
            + DIVERGENCE_SCALE * SOFTEN_FACTOR * SOFTEN_FACTOR * divergence_value * divergence_mask
        )
    )
    soft_half = DIVERGENCE_SCALE * SOFTEN_FACTOR * divergence_mask * token_weight
    soft_one = token_weight * jnp.exp(SOFTEN_FACTOR * lse_half - lse_one)
    nothing = jnp.zeros_like(lse_half)
    scalars = jnp.stack(
        [lse_half, lse_teacher, soft_one, soft_half, token_weight, nothing, nothing, nothing]
    )
    slope, part = logits_back(final_t, labels, scalars, teacher_t, table_rows, table_parts)
    part = part.T.reshape(batch_size, target_len, D)
    part = jnp.roll(fill(part).reshape(heads, each * target_len, D), -head_pos, 0)
    grad_final = scatter_head([part[j] for j in range(heads)], heads)

    dec_grads, gain_grads, grad_encoded, dec_low = layers.decoder_back(
        grad_final, dec_embed, encoded, kept_dec
    )
    dec_shard = lax.psum_scatter(dec_grads, "dp", scatter_dimension=0)
    dec_rows = gather_head(dec_low, heads)
    enc_grads, enc_low = layers.encoder_back(grad_encoded, gain_grads, enc_embed, kept_enc, lanes)
    enc_low, *dec_rows = tie(enc_low, *dec_rows)

    enc_rows = gather_head(enc_low, heads)
    enc_shard = lax.psum_scatter(after(enc_grads, dec_shard), "dp", scatter_dimension=0)
    near_ids = jnp.concatenate([dec_ids.reshape(-1), enc_ids[0]])
    near_rows = jnp.concatenate(dec_rows + [enc_low], 0)
    columns = padded_to(vocab_local)
    (grad_table_t,) = spread(near_ids, near_rows, columns, final_t=final_t, slope=slope)

    def send_heads(shard):
        return [shard[0]] + [head_shift(shard[j], j, heads) for j in range(1, heads)]

    far_ids = enc_ids[1:].reshape(-1)
    far_rows = jnp.concatenate(enc_rows[1:], 0)
    dec_sums = send_heads(dec_shard)
    *keeps, send = spread(far_ids, far_rows, columns, base=grad_table_t)
    enc_sums = send_heads(enc_shard)
    g_table, table_squares = ScatterDp(keeps, send, dp).run(vocab_local, dec_sums, enc_sums)
    g_dec = functools.reduce(jnp.add, [value.astype(F32) for value in dec_sums])
    g_enc = functools.reduce(jnp.add, [value.astype(F32) for value in enc_sums])

    def squares(array, axes):
        return jnp.sum(array * array, axis=axes).reshape(-1)

    weight_squares = jnp.concatenate(
        [
            squares(embed_t, (0, 1)),
            squares(attn_in, (2, 3)),
            squares(attn_out_t, (1, 2)),
            squares(ff_in, (1, 2)),
            squares(ff_out_t, (1, 2)),
            squares(gains, (1,)) * lead,
        ]
    )
    matrix_count = weight_squares.shape[0]
    gain_at = sum(widths[0])
    g_gain = g_enc[:, gain_at : gain_at + gain_rows]
    grad_squares = (
        jnp.sum(g_dec * g_dec)
        + jnp.sum(g_enc[:, :gain_at] * g_enc[:, :gain_at])
        + lead * jnp.sum(g_gain * g_gain)
    )
    first_line = jnp.pad(
        jnp.concatenate([weight_squares, loss_part.reshape(1), grad_squares.reshape(1)]),
        (0, lanes - matrix_count - 2),
    ).reshape(1, lanes)
    totals = sum_all(jnp.concatenate([first_line, table_squares], 0), dp, heads)
    grad_norm = jnp.sqrt(totals[0, matrix_count + 1] + jnp.sum(totals[1:]))
    total_loss = totals[0, matrix_count]
    clip = jnp.full((8, 128), jnp.minimum(1.0, CLIP_NORM / grad_norm))
    m_table, v_table, u_table, squares_table = column_call(
        functools.partial(lamb_columns_kernel, vocab_local, 1024),
        [masters[0], moments[0], seconds[0], g_table, clip],
        [(embed_t.shape[0], F32)] * 3,
        1024,
        sums=[(8, 128)],
    )

    def flat9(array):
        return array.reshape((9,) + array.shape[2:])

    def starts(width):
        out = [0]
        for columns in width:
            out.append(out[-1] + columns)
        return out

    at_enc, at_dec = starts(widths[0]), starts(widths[1])
    places = [
        [(0, at_enc[k]) for k in range(3)]
        + [(1, at_dec[k]) for k in range(3)]
        + [(1, at_dec[k]) for k in range(4, 7)],
        [(0, at_enc[3]), (1, at_dec[3]), (1, at_dec[7])],
        [(0, at_enc[4]), (1, at_dec[8])],
        [(0, at_enc[5]), (1, at_dec[9])],
    ]
    groups = [
        tuple(flat9(stack[1]) if k == 1 else stack[k] for stack in (masters, moments, seconds))
        for k in range(1, 5)
    ]
    *fresh, squares_small = lamb_matrices(clip, [g_enc, g_dec], groups, places)
    m_gain, v_gain, u_gain = lamb(gains, moments[5], seconds[5], g_gain.T, clip[0, 0])
    gain_squares = jnp.pad(squares(u_gain, (1,)) * lead, (0, lanes - gain_rows)).reshape(1, lanes)
    small_count = sum(len(matrices) for matrices in places)
    update_totals = sum_all(
        jnp.concatenate([squares_table, squares_small, gain_squares], 0), dp, heads
    )
    update_squares = jnp.concatenate(
        [
            jnp.sum(update_totals[:8]).reshape(1),
            jnp.sum(update_totals[8 : 8 + small_count], 1),
            update_totals[-1, :gain_rows],
        ]
    )
    rates = LEARN_RATE * jnp.sqrt(totals[0, :matrix_count]) / (jnp.sqrt(update_squares) + 1e-06)
    fresh_m = [m_table] + list(fresh[0::3]) + [m_gain]
    fresh_v = [v_table] + list(fresh[1::3]) + [v_gain]
    updates = [u_table] + list(fresh[2::3]) + [u_gain]
    for stack in (fresh_m, fresh_v, updates):
        stack[1] = stack[1].reshape(attn_in.shape)
    shapes = [(1, 1), (3, 3, 1, 1), (3, 1, 1), (2, 1, 1), (2, 1, 1), (gain_rows, 1)]
    fresh_w, start = [], 0
    for master, update, shape in zip(masters, updates, shapes, strict=True):
        count = 1
        for extent in shape:
            count *= extent
        fresh_w.append(master - rates[start : start + count].reshape(shape) * update)
        start += count
    return (
        total_loss.reshape(1),
        grad_norm.reshape(1),
        *transposed(fresh_w),
        *transposed(fresh_m),
        *transposed(fresh_v),
    )


def solution(mesh):
    params = (
        P("head", "dp"),
        P(None, None, "dp", "head"),
        P(None, "head", "dp"),
        P(None, "dp", "head"),
        P(None, "head", "dp"),
        P(None, "dp"),
    )
    return jax.shard_map(
        functools.partial(body, mesh.shape["dp"], mesh.shape["head"]),
        mesh=mesh,
        in_specs=(
            P("dp", None),
            P("dp", None),
            P("dp"),
            P("dp"),
            P("dp", None),
            P("dp", "head"),
            *params,
            *params,
            *params,
        ),
        out_specs=(P(), P(), *params, *params, *params),
        check_vma=False,
    )
```

```python
import functools

import jax
import jax.numpy as jnp
from jax import lax
from jax.experimental import pallas as pl
from jax.experimental.pallas import tpu as pltpu
from jax.sharding import PartitionSpec as P

D = 512
DH = 64
STEP_NUM = 10

NORM_EPS = 1e-06
SOFTEN_FACTOR = 2.0
DIVERGENCE_SCALE = 1.0
CLIP_NORM = 0.02
BETA_ONE = 0.9
BETA_TWO = 0.999
ADAM_EPS = 1e-08
WEIGHT_DECAY = 0.01
LEARN_RATE = 0.3

BF = jnp.bfloat16
F32 = jnp.float32


def dp_swap(x, bit, dp):
    return lax.ppermute(x, "dp", [(i, i ^ bit) for i in range(dp)])


def head_shift(x, step, heads):
    return lax.ppermute(x, "head", [(i, (i + step) % heads) for i in range(heads)])


def after(x, *earlier):
    return lax.optimization_barrier((x, *earlier))[0]


def tie(chain, *arrived):
    return lax.optimization_barrier((chain, *arrived))


class GatherDp:
    def __init__(self, x, dp):
        self.x, self.dp = x, dp
        self.rows = x.shape[0]
        self.near = (dp_swap(x, 4, dp), dp_swap(x, 2, dp)) if dp == 8 else ()
        self.far = ()

    def go_far(self):
        if self.dp == 8:
            half = self.rows // 2
            part_y, part_x = self.near
            self.far = (dp_swap(part_y[:half], 2, self.dp), dp_swap(part_x[half:], 4, self.dp))

    def parts(self):
        dp = self.dp
        if dp == 8:
            here = [self.x, *self.near, *self.far]
            return here + [dp_swap(part, 1, dp) for part in here]
        whole = self.x
        bit = dp // 2
        while bit:
            whole = jnp.concatenate([whole, dp_swap(whole, bit, dp)], 0)
            bit //= 2
        return [whole]


def gather_head(x, heads):
    return [x] + [head_shift(x, heads - j, heads) for j in range(1, heads)]


def scatter_head(parts, heads):
    total = parts[0].astype(F32)
    for j in range(1, heads):
        total = total + head_shift(parts[j].astype(BF), j, heads).astype(F32)
    return total


def sum_head(x, heads):
    total = x
    for j in range(1, heads):
        total = total + head_shift(x, j, heads)
    return total


def sum_all(x, dp, heads):
    return sum_head(sum_dp(x, dp), heads)


def sum_dp(x, dp):
    bit = 1
    while bit < dp:
        x = x + dp_swap(x, bit, dp)
        bit *= 2
    return x


def ordered(kernel, count, waits):
    if not waits:
        return kernel

    def body(*refs):
        kernel(*refs[:count], *refs[count + len(waits) :])

    return body


ANYWHERE = pl.BlockSpec(memory_space=pl.ANY)


def stacked(refs):
    return refs[0][...] if len(refs) == 1 else jnp.concatenate([ref[...] for ref in refs], 0)


def lookup_kernel(vocab, tile, ids_ref, *refs):
    *table_refs, out_ref, rows_ref, acc_ref = refs
    step = pl.program_id(0)

    @pl.when(step == 0)
    def _():
        acc_ref[...] = jnp.zeros_like(acc_ref)

    place = lax.broadcasted_iota(jnp.int32, (1, tile), 1)
    block = stacked(table_refs)
    block = jnp.where(place < vocab - step * tile, block, jnp.zeros_like(block)).T
    rows_ref[...] = block
    hit = (ids_ref[...] - step * tile == place).astype(BF)
    acc_ref[...] += jnp.dot(hit, block, preferred_element_type=F32)

    @pl.when(step == pl.num_programs(0) - 1)
    def _():
        out_ref[...] = acc_ref[...].astype(BF)


def column_specs(parts, tile):
    return [pl.BlockSpec((part.shape[0], tile), lambda i: (0, i)) for part in parts]


def fixed(shape):
    return pl.BlockSpec(shape, lambda i: (0,) * len(shape))


VMEM_LIMIT = 56 * 2**20


def cost(microseconds):
    return pl.CostEstimate(
        flops=int(1.15e9 * microseconds),
        bytes_accessed=int(3.7e6 * microseconds),
        transcendentals=0,
    )


def padded_to(columns, step=128):
    return -(-columns // step) * step


def lookup(ids, table_parts):
    rows, vocab = ids.shape[0], table_parts[0].shape[1]
    tile = 1024
    return pl.pallas_call(
        functools.partial(lookup_kernel, vocab, tile),
        out_shape=[
            jax.ShapeDtypeStruct((rows, D), BF),
            jax.ShapeDtypeStruct((padded_to(vocab), D), BF),
        ],
        grid=(pl.cdiv(vocab, tile),),
        in_specs=[fixed((rows, 1))] + column_specs(table_parts, tile),
        out_specs=[fixed((rows, D)), pl.BlockSpec((tile, D), lambda i: (i, 0))],
        scratch_shapes=[pltpu.VMEM((rows, D), F32)],
        cost_estimate=cost(26),
        compiler_params=pltpu.CompilerParams(vmem_limit_bytes=VMEM_LIMIT),
    )(ids.reshape(rows, 1), *table_parts)


def pick(ids, table_rows, waits):
    rows, vocab = ids.shape[0], table_rows.shape[0]
    tile = 1024
    return pl.pallas_call(
        ordered(functools.partial(pick_kernel, vocab, tile), 2, waits),
        out_shape=jax.ShapeDtypeStruct((rows, D), BF),
        grid=(pl.cdiv(vocab, tile),),
        in_specs=[fixed((rows, 1)), pl.BlockSpec((tile, D), lambda i: (i, 0))]
        + [ANYWHERE] * len(waits),
        out_specs=fixed((rows, D)),
        scratch_shapes=[pltpu.VMEM((rows, D), F32)],
        cost_estimate=cost(12),
        compiler_params=pltpu.CompilerParams(vmem_limit_bytes=VMEM_LIMIT),
    )(ids.reshape(rows, 1), table_rows, *waits)


def pick_kernel(vocab, tile, ids_ref, rows_ref, out_ref, acc_ref):
    step = pl.program_id(0)

    @pl.when(step == 0)
    def _():
        acc_ref[...] = jnp.zeros_like(acc_ref)

    place = lax.broadcasted_iota(jnp.int32, (1, tile), 1)
    below = lax.broadcasted_iota(jnp.int32, (tile, 1), 0)
    block = rows_ref[...]
    block = jnp.where(below < vocab - step * tile, block, jnp.zeros_like(block))
    hit = (ids_ref[...] - step * tile == place).astype(BF)
    acc_ref[...] += jnp.dot(hit, block, preferred_element_type=F32)

    @pl.when(step == pl.num_programs(0) - 1)
    def _():
        out_ref[...] = acc_ref[...].astype(BF)


def spread_kernel(tile, ids_ref, rows_ref, *refs):
    step = pl.program_id(0)
    turned_ref = refs[-1]

    @pl.when(step == 0)
    def _():
        turned_ref[...] = rows_ref[...].T

    place = step * tile + lax.broadcasted_iota(jnp.int32, (1, tile), 1)
    hit = (ids_ref[...] == place).astype(BF)
    total = jnp.dot(turned_ref[...], hit, preferred_element_type=F32)
    if len(refs) == 4:
        final_ref, slope_ref, out_ref, _ = refs
        out_ref[...] = total + lax.dot_general(
            final_ref[...], slope_ref[...], (((1,), (1,)), ((), ())), preferred_element_type=F32
        )
    else:
        base_ref, *keep_refs, send_ref, _ = refs
        total = base_ref[...] + total
        deep = D // 8
        for number, keep_ref in enumerate(keep_refs):
            keep_ref[...] = total[number * deep : (number + 1) * deep]
        send_ref[...] = total[D // 2 :].astype(BF)


def spread(ids, rows_low, columns, final_t=None, slope=None, base=None, waits=()):
    rows = ids.shape[0]
    tile = 1024
    if base is None:
        shapes = [((D, columns), F32)]
        more = [final_t, slope]
        specs = [fixed(final_t.shape), pl.BlockSpec((tile, slope.shape[1]), lambda i: (i, 0))]
    else:
        shapes = [((D // 8, columns), F32)] * 4 + [((D // 2, columns), BF)]
        more = [base]
        specs = [pl.BlockSpec((D, tile), lambda i: (0, i))]
    return pl.pallas_call(
        ordered(functools.partial(spread_kernel, tile), 2 + len(more), waits),
        out_shape=[jax.ShapeDtypeStruct(*shape) for shape in shapes],
        grid=(pl.cdiv(columns, tile),),
        in_specs=[fixed((rows, 1)), fixed((rows, D))] + specs + [ANYWHERE] * len(waits),
        out_specs=[pl.BlockSpec((shape[0][0], tile), lambda i: (0, i)) for shape in shapes],
        scratch_shapes=[pltpu.VMEM((D, rows), BF)],
        cost_estimate=cost(18),
        compiler_params=pltpu.CompilerParams(vmem_limit_bytes=VMEM_LIMIT),
    )(ids.reshape(rows, 1), rows_low, *more, *waits)


def column_call(kernel, inputs, outputs, tile, sums=(), columns=None, waits=()):
    columns = columns or inputs[0].shape[1]
    out_shape = [jax.ShapeDtypeStruct((rows, columns), dtype) for rows, dtype in outputs]
    out_specs = [pl.BlockSpec((rows, tile), lambda i: (0, i)) for rows, _ in outputs]
    for shape in sums:
        out_shape.append(jax.ShapeDtypeStruct(shape, F32))
        out_specs.append(fixed(shape))
    return pl.pallas_call(
        ordered(kernel, len(inputs), waits),
        out_shape=out_shape,
        grid=(pl.cdiv(columns, tile),),
        in_specs=[
            pl.BlockSpec((array.shape[0], tile), lambda i: (0, i))
            if array.shape[1] >= columns
            else fixed(array.shape)
            for array in inputs
        ]
        + [ANYWHERE] * len(waits),
        out_specs=out_specs,
        cost_estimate=cost(5),
        compiler_params=pltpu.CompilerParams(vmem_limit_bytes=VMEM_LIMIT),
    )(*inputs, *waits)


def first_sums_kernel(groups, *refs):
    d_low, d_high, x_sum, y_sum = refs[4 * groups :]
    start = 0
    for group in range(groups):
        y_ref, x_ref, d_ref, got_ref = refs[4 * group : 4 * group + 4]
        deep, columns = y_ref.shape
        half, stop = deep // 2, start + columns
        y_sum[:, start:stop] = y_ref[...] + got_ref[deep : 2 * deep].astype(F32)
        x_sum[:, start:stop] = x_ref[...] + got_ref[2 * deep : 3 * deep].astype(F32)
        d = (d_ref[...] + got_ref[3 * deep :].astype(F32)).astype(BF)
        d_low[:, start:stop] = d[:half]
        d_high[:, start:stop] = d[half:]
        start = stop


def second_sums_kernel(y_sum, got_a, x_sum, got_b, y_out, x_out):
    half = got_a.shape[0]
    y_out[:half] = (y_sum[:half] + got_a[...].astype(F32)).astype(BF)
    y_out[half:] = y_sum[half:].astype(BF)
    x_out[:half] = x_sum[:half].astype(BF)
    x_out[half:] = (x_sum[half:] + got_b[...].astype(F32)).astype(BF)


def lane_sums(value):
    rows, columns = value.shape
    total = value[:, :128]
    for start in range(128, columns, 128):
        total = total + value[:, start : start + 128]
    out = total[:8]
    for start in range(8, rows, 8):
        out = out + total[start : start + 8]
    return out


def inside(columns, tile, value):
    place = pl.program_id(0) * tile + lax.broadcasted_iota(jnp.int32, (1, tile), 1)
    return jnp.where(place < columns, value, 0.0)


def last_sums_kernel(groups, columns, tile, *refs):
    y_ref, x_ref, out = refs[2 * groups : 2 * groups + 3]
    more = x_ref[...].astype(F32) + y_ref[...].astype(F32)
    start = 0
    for group in range(groups):
        own, got = refs[2 * group : 2 * group + 2]
        deep, stop = own.shape[0], start + own.shape[1]
        out[:, start:stop] = own[...] + got[:deep].astype(F32) + more[:, start:stop]
        start = stop
    if columns is not None:
        squares = refs[-1]

        @pl.when(pl.program_id(0) == 0)
        def _():
            squares[...] = jnp.zeros_like(squares)

        squares[...] += lane_sums(inside(columns, tile, out[...] * out[...]))


class ScatterDp:
    def __init__(self, dp):
        self.dp, self.groups = dp, []

    def add(self, keeps, send):
        self.groups.append((*keeps, dp_swap(send, 1, self.dp)))

    def far(self, tile, waits=()):
        dp = self.dp
        self.pieces = ()
        if dp == 8:
            rows = self.groups[0][0].shape[0]
            inputs, columns = [], 0
            for own, y, x, d, got in self.groups:
                inputs += [y, x, d, got]
                columns += own.shape[1]
            outputs = [(rows // 2, BF)] * 2 + [(rows, F32)] * 2
            kernel = functools.partial(first_sums_kernel, len(self.groups))
            d_low, d_high, *self.later = sums_call(
                kernel, inputs, outputs, columns, tile, waits=waits
            )
            self.pieces = [dp_swap(d_low, 2, dp), dp_swap(d_high, 4, dp)]

    def near(self, tile):
        dp = self.dp
        self.last = self.ready = ()
        if dp == 8:
            x_sum, y_sum = self.later
            rows, columns = y_sum.shape
            y_sum, x_sum = sums_call(
                second_sums_kernel,
                [y_sum, self.pieces[0], x_sum, self.pieces[1]],
                [(rows, BF)] * 2,
                columns,
                tile,
            )
            self.ready = [y_sum, x_sum]
            self.last = [dp_swap(y_sum, 4, dp), dp_swap(x_sum, 2, dp)]

    def result(self, tile, columns=None):
        dp = self.dp
        if dp != 8:
            total = jnp.concatenate(
                [
                    jnp.concatenate(group[:4], 0) + group[4].astype(F32)
                    for group in self.groups
                ],
                1,
            )
            bit = 2
            while bit < dp:
                rows = total.shape[0] // 2
                total = total[:rows] + dp_swap(total[rows:].astype(BF), bit, dp).astype(F32)
                bit *= 2
            total = total[:, :columns]
            if columns is None:
                return [total]
            return [total, jnp.zeros((8, 128), F32).at[0, 0].set(jnp.sum(total * total))]
        inputs, wide = [], 0
        for own, _, _, _, got in self.groups:
            inputs += [own, got]
            wide += own.shape[1]
        inputs += self.last
        kernel = functools.partial(last_sums_kernel, len(self.groups), columns, tile)
        sums = [] if columns is None else [(8, 128)]
        rows = self.groups[0][0].shape[0]
        return sums_call(kernel, inputs, [(rows, F32)], columns or wide, tile, sums)


def sums_call(kernel, inputs, outputs, columns, tile, sums=(), waits=()):
    if tile is not None:
        return column_call(kernel, inputs, outputs, tile, sums, columns, waits)
    return pl.pallas_call(
        kernel,
        out_shape=[jax.ShapeDtypeStruct((rows, columns), dtype) for rows, dtype in outputs],
        cost_estimate=cost(5),
        compiler_params=pltpu.CompilerParams(vmem_limit_bytes=VMEM_LIMIT),
    )(*inputs)


def logits_kernel(vocab, tile, final_ref, label_ref, teacher_ref, table_ref, out_ref, *stats):
    top_s, top_t, one, half, teach, cross, label = stats
    step = pl.program_id(0)
    last = pl.num_programs(0) - 1

    @pl.when(step == 0)
    def _():
        top_s[...] = jnp.full_like(top_s, -1e30)
        top_t[...] = jnp.full_like(top_t, -1e30)
        for ref in (one, half, teach, cross, label):
            ref[...] = jnp.zeros_like(ref)

    def work(valid):
        logits = jnp.dot(table_ref[...], final_ref[...], preferred_element_type=F32)
        tokens = logits.shape[1]

        def folded(value):
            return value.reshape(tile // 8, 8, tokens)

        student = folded(logits)
        teacher = folded(teacher_ref[...].astype(F32))
        place = 8 * lax.broadcasted_iota(jnp.int32, (tile // 8, 8, 1), 0)
        place = place + lax.broadcasted_iota(jnp.int32, (tile // 8, 8, 1), 1)
        if valid < tile:
            student = jnp.where(place < valid, student, -1e30)
            teacher = jnp.where(place < valid, teacher, -1e30)
        old_s, old_t = top_s[...], top_t[...]
        new_s = jnp.maximum(old_s, jnp.max(student, 0))
        new_t = jnp.maximum(old_t, jnp.max(teacher, 0))
        top_s[...] = new_s
        top_t[...] = new_t
        scale_s = jnp.exp((old_s - new_s) * 0.5)
        scale_t = jnp.exp((old_t - new_t) * 0.5)
        e = jnp.exp((student - new_s[None]) * 0.5)
        half[...] = half[...] * scale_s + jnp.sum(e, 0)
        one[...] = one[...] * (scale_s * scale_s) + jnp.sum(e * e, 0)
        e = jnp.exp((teacher - new_t[None]) * 0.5)
        teach[...] = teach[...] * scale_t + jnp.sum(e, 0)
        cross[...] = cross[...] * scale_t + jnp.sum(e * (teacher - student), 0)
        labels = (label_ref[...] - step * tile)[None]
        label[...] += jnp.sum(jnp.where(labels == place, student, 0.0), 0)

    rest = vocab - (pl.cdiv(vocab, tile) - 1) * tile
    if rest == tile:
        work(tile)
    else:

        @pl.when(step < last)
        def _():
            work(tile)

        @pl.when(step == last)
        def _():
            work(rest)

    @pl.when(step == last)
    def _():
        peak_s = jnp.max(top_s[...], 0, keepdims=True)
        peak_t = jnp.max(top_t[...], 0, keepdims=True)
        by_s = jnp.exp((top_s[...] - peak_s) * 0.5)
        by_t = jnp.exp((top_t[...] - peak_t) * 0.5)

        def total(value):
            return jnp.sum(value, 0, keepdims=True)

        out_ref[0:1] = peak_s
        out_ref[1:2] = peak_t
        out_ref[2:3] = total(one[...] * (by_s * by_s))
        out_ref[3:4] = total(half[...] * by_s)
        out_ref[4:5] = total(teach[...] * by_t)
        out_ref[5:6] = total(cross[...] * by_t) * 0.5
        out_ref[6:7] = total(label[...])
        out_ref[7:8] = jnp.zeros_like(peak_s)


def logits_stats(final_t, labels, teacher_t, table_rows):
    vocab, tokens = teacher_t.shape
    tile = 1024
    return pl.pallas_call(
        functools.partial(logits_kernel, vocab, tile),
        out_shape=jax.ShapeDtypeStruct((8, tokens), F32),
        grid=(pl.cdiv(vocab, tile),),
        in_specs=[
            fixed(final_t.shape),
            fixed((1, tokens)),
            pl.BlockSpec((tile, tokens), lambda i: (i, 0)),
            pl.BlockSpec((tile, D), lambda i: (i, 0)),
        ],
        out_specs=fixed((8, tokens)),
        scratch_shapes=[pltpu.VMEM((8, tokens), F32)] * 7,
        cost_estimate=cost(17),
        compiler_params=pltpu.CompilerParams(vmem_limit_bytes=VMEM_LIMIT),
    )(final_t, labels.reshape(1, tokens), teacher_t, table_rows)


def logits_back_kernel(vocab, tile, final_ref, label_ref, scalar_ref, teacher_ref, *refs):
    rows_ref, *table_refs, slope_ref, back_ref, acc_ref = refs
    step = pl.program_id(0)
    last = pl.num_programs(0) - 1

    @pl.when(step == 0)
    def _():
        acc_ref[...] = jnp.zeros_like(acc_ref)

    good = lax.broadcasted_iota(jnp.int32, (1, tile), 1) < vocab - step * tile
    block = stacked(table_refs)
    block = jnp.where(good, block, jnp.zeros_like(block))
    place = lax.broadcasted_iota(jnp.int32, (tile, 1), 0)
    logits = jnp.dot(rows_ref[...], final_ref[...], preferred_element_type=F32)
    lse_half = scalar_ref[0:1]
    lse_teacher = scalar_ref[1:2]
    soft_one = scalar_ref[2:3]
    soft_half = scalar_ref[3:4]
    weight = scalar_ref[4:5]
    student = jnp.exp(logits * 0.5 - lse_half)
    teacher = jnp.exp(teacher_ref[...].astype(F32) * 0.5 - lse_teacher)
    labels = label_ref[...] - step * tile
    slope = student * (soft_one * student + soft_half) - soft_half * teacher
    slope = slope - jnp.where(labels == place, weight, 0.0)
    slope = jnp.where(place < vocab - step * tile, slope, 0.0).astype(BF)
    slope_ref[...] = slope
    acc_ref[...] += jnp.dot(block, slope, preferred_element_type=F32)

    @pl.when(step == last)
    def _():
        back_ref[...] = acc_ref[...].astype(BF)


def logits_back(final_t, labels, scalars, teacher_t, table_rows, table_parts):
    vocab, tokens = teacher_t.shape
    tile = 1024
    return pl.pallas_call(
        functools.partial(logits_back_kernel, vocab, tile),
        out_shape=[
            jax.ShapeDtypeStruct((padded_to(vocab), tokens), BF),
            jax.ShapeDtypeStruct((D, tokens), BF),
        ],
        grid=(pl.cdiv(vocab, tile),),
        in_specs=[
            fixed(final_t.shape),
            fixed((1, tokens)),
            fixed(scalars.shape),
            pl.BlockSpec((tile, tokens), lambda i: (i, 0)),
            pl.BlockSpec((tile, D), lambda i: (i, 0)),
        ]
        + column_specs(table_parts, tile),
        out_specs=[pl.BlockSpec((tile, tokens), lambda i: (i, 0)), fixed((D, tokens))],
        scratch_shapes=[pltpu.VMEM((D, tokens), F32)],
        cost_estimate=cost(22),
        compiler_params=pltpu.CompilerParams(vmem_limit_bytes=VMEM_LIMIT),
    )(final_t, labels.reshape(1, tokens), scalars, teacher_t, table_rows, *table_parts)


BIAS_ONE = 1.0 - BETA_ONE**STEP_NUM
BIAS_TWO = 1.0 - BETA_TWO**STEP_NUM


def lamb(weight, moment, second, grad, clip):
    grad = grad * clip
    moment = BETA_ONE * moment + (1 - BETA_ONE) * grad
    second = BETA_TWO * second + (1 - BETA_TWO) * grad * grad
    update = (
        moment * (1.0 / BIAS_ONE) / (jnp.sqrt(second * (1.0 / BIAS_TWO)) + ADAM_EPS)
        + WEIGHT_DECAY * weight
    )
    return moment, second, update


def lamb_columns_kernel(columns, tile, w, m, v, g, clip, m_out, v_out, u_out, squares):
    moment, second, update = lamb(w[...], m[...], v[...], g[...], clip[0:1, 0:1])
    m_out[...] = moment
    v_out[...] = second
    u_out[...] = update

    @pl.when(pl.program_id(0) == 0)
    def _():
        squares[...] = jnp.zeros_like(squares)

    squares[...] += lane_sums(inside(columns, tile, update * update))


def lamb_matrices_kernel(places, clip_ref, *refs):
    grads = refs[:2]
    count = len(places)
    states = refs[2 : 2 + 3 * count]
    outs = refs[2 + 3 * count : -1]
    squares = refs[-1]
    squares[...] = jnp.zeros_like(squares)
    clip = clip_ref[0:1, 0:1]
    row = 0
    for group, matrices in enumerate(places):
        w, m, v = states[3 * group : 3 * group + 3]
        m_out, v_out, u_out = outs[3 * group : 3 * group + 3]
        width = w.shape[-1]
        for number, (array, start) in enumerate(matrices):
            grad = grads[array][:, start : start + width]
            moment, second, update = lamb(w[number], m[number], v[number], grad, clip)
            m_out[number] = moment
            v_out[number] = second
            u_out[number] = update
            total = jnp.sum(update * update, 0, keepdims=True)
            lanes = min(128, width)
            line = total[:, :lanes]
            for first in range(lanes, width, lanes):
                line = line + total[:, first : first + lanes]
            squares[row : row + 1, :lanes] = line
            row += 1


def lamb_matrices(clip, grads, groups, places):
    flat = [array for group in groups for array in group]
    shapes = [jax.ShapeDtypeStruct(group[0].shape, F32) for group in groups for _ in range(3)]
    rows = 8 * pl.cdiv(sum(len(matrices) for matrices in places), 8)
    return pl.pallas_call(
        functools.partial(lamb_matrices_kernel, places),
        out_shape=shapes + [jax.ShapeDtypeStruct((rows, 128), F32)],
        cost_estimate=cost(4),
        compiler_params=pltpu.CompilerParams(vmem_limit_bytes=VMEM_LIMIT),
    )(clip, *grads, *flat)


def pack_kernel(heads_of, *refs):
    *in_refs, out_ref = refs
    start = 0
    for number, index in heads_of:
        value = in_refs[number][...] if index is None else in_refs[number][index]
        out_ref[:, start : start + value.shape[1]] = value.astype(BF)
        start += value.shape[1]


def pack(arrays, plan):
    columns = sum(arrays[number].shape[-1] for number, _ in plan)
    return pl.pallas_call(
        functools.partial(pack_kernel, plan),
        out_shape=jax.ShapeDtypeStruct((arrays[0].shape[-2], columns), BF),
        cost_estimate=cost(2),
        compiler_params=pltpu.CompilerParams(vmem_limit_bytes=VMEM_LIMIT),
    )(*arrays)


def dot(a, b):
    return jnp.dot(a, b, preferred_element_type=F32)


def dot_nt(a, b):
    return lax.dot_general(a, b, (((1,), (1,)), ((), ())), preferred_element_type=F32)


def dot_tn(a, b):
    return lax.dot_general(a, b, (((0,), (0,)), ((), ())), preferred_element_type=F32)


def root(inputs):
    return lax.rsqrt(jnp.mean(inputs * inputs, -1, keepdims=True) + NORM_EPS)


def normed(inputs, gain_row):
    return (inputs * root(inputs) * gain_row).astype(BF)


def norm_back(inputs, gain_row, upstream):
    factor = root(inputs)
    scaled = upstream * gain_row
    inner = jnp.mean(scaled * inputs, -1, keepdims=True)
    return (
        factor * (scaled - inputs * factor * factor * inner),
        jnp.sum(upstream * inputs * factor, axis=0, keepdims=True),
    )


def attn_probs(query, keys_all, allowed):
    scores = jnp.where(allowed, dot_nt(query, keys_all) * DH ** (-0.5), -1000000000.0)
    grown = jnp.exp(scores - jnp.max(scores, -1, keepdims=True))
    return grown * (1.0 / jnp.sum(grown, -1, keepdims=True))


def key_mask(count, keys):
    return lax.broadcasted_iota(jnp.int32, (1, keys), 1) < count


def causal_mask(rows):
    return lax.broadcasted_iota(jnp.int32, (rows, rows), 0) >= lax.broadcasted_iota(
        jnp.int32, (rows, rows), 1
    )


def weights_of(ref, order_ref, j):
    return jnp.concatenate([ref[order_ref[place], j] for place in range(ref.shape[0])], 0)


def attend_heads(query, keys_all, values, each, mask_of):
    rows, source = query.shape[0] // each, keys_all.shape[0] // each
    out = []
    for number in range(each):
        a, b = number * rows, number * source
        line = []
        for first in range(0, query.shape[1], DH):
            probs = attn_probs(
                query[a : a + rows, first : first + DH],
                keys_all[b : b + source, first : first + DH],
                mask_of(number),
            ).astype(BF)
            line.append(dot(probs, values[b : b + source, first : first + DH]).astype(BF))
        out.append(jnp.concatenate(line, 1) if len(line) > 1 else line[0])
    return jnp.concatenate(out, 0) if each > 1 else out[0]


def attend_heads_back(query, keys_all, values, grad_mixed, each, mask_of):
    rows, source = query.shape[0] // each, keys_all.shape[0] // each
    outs = ([], [], [])
    for number in range(each):
        a, b = number * rows, number * source
        lines = ([], [], [])
        for first in range(0, query.shape[1], DH):
            q = query[a : a + rows, first : first + DH]
            k = keys_all[b : b + source, first : first + DH]
            v = values[b : b + source, first : first + DH]
            g = grad_mixed[a : a + rows, first : first + DH]
            probs = attn_probs(q, k, mask_of(number))
            grad_probs = dot_nt(g, v)
            slope = probs * (grad_probs - jnp.sum(grad_probs * probs, -1, keepdims=True))
            slope = slope.astype(BF)
            lines[0].append((dot(slope, k) * DH ** (-0.5)).astype(BF))
            lines[1].append((dot_tn(slope, q) * DH ** (-0.5)).astype(BF))
            lines[2].append(dot_tn(probs.astype(BF), g).astype(BF))
        for out, line in zip(outs, lines, strict=True):
            out.append(jnp.concatenate(line, 1) if len(line) > 1 else line[0])
    return [jnp.concatenate(out, 0) if each > 1 else out[0] for out in outs]


class Layers:
    def __init__(self, order, head_pos, lens, enc_weights, dec_weights, gain, each):
        self.prefetch = (order, head_pos.reshape(1), lens)
        self.sides, self.gain, self.each = (enc_weights, dec_weights), gain, each
        self.dp, self.heads, self.deep, _ = enc_weights.shape
        self.width = 4 * D // self.heads
        self.unit = self.width // 4

    def weight_specs(self, side, first, stride, fixed_block=None):
        shape = (self.dp, self.heads, self.deep, self.width)
        weights = self.sides[side]
        out = [
            (
                weights,
                pl.BlockSpec(shape, lambda step, *_: (0, 0, 0, first + stride * step)),
            )
        ]
        if fixed_block is not None:
            out.append(
                (weights, pl.BlockSpec(shape, lambda step, *_: (0, 0, 0, fixed_block)))
            )
        return out

    @staticmethod
    def whole(shape):
        return pl.BlockSpec(shape, lambda *_: (0,) * len(shape))

    def call(self, kernel, phases, arrays, outs, scratch, time):
        arrays = [a if isinstance(a, tuple) else (a, self.whole(a.shape)) for a in arrays]
        return pl.pallas_call(
            kernel,
            out_shape=[jax.ShapeDtypeStruct(shape, dtype) for shape, dtype in outs],
            grid_spec=pltpu.PrefetchScalarGridSpec(
                num_scalar_prefetch=3,
                grid=(phases,),
                in_specs=[spec for _, spec in arrays],
                out_specs=[self.whole(shape) for shape, _ in outs],
                scratch_shapes=[pltpu.VMEM(shape, dtype) for shape, dtype in scratch],
            ),
            cost_estimate=cost(time),
            compiler_params=pltpu.CompilerParams(vmem_limit_bytes=VMEM_LIMIT),
        )(*self.prefetch, *[array for array, _ in arrays])

    def self_attention(self, low, w_of, kept, mask_of):
        unit = self.unit
        total = None
        for j in range(self.heads):
            w = w_of(j)
            qkv = dot(low, w[:, : 3 * unit]).astype(BF)
            mixed = attend_heads(
                qkv[:, :unit], qkv[:, unit : 2 * unit], qkv[:, 2 * unit :], self.each, mask_of
            )
            kept[j, :, : 3 * unit] = qkv
            kept[j, :, 3 * unit :] = mixed
            part = dot_nt(mixed, w[:, 3 * unit :])
            total = part if total is None else total + part
        return total

    def feed(self, low, up_of, down_of, hidden):
        total = None
        for j in range(self.heads):
            grown = jax.nn.relu(dot(low, up_of(j))).astype(BF)
            hidden[j] = grown
            part = dot_nt(grown, down_of(j))
            total = part if total is None else total + part
        return total

    def encoder(self, x):
        heads, each, width = self.heads, self.each, self.width
        rows = x.shape[0]

        def kernel(order, head, lens, x_ref, gain, w_ref, d_ref, kept, mid, hidden, last, encoded):
            step = pl.program_id(0)
            w_of = functools.partial(weights_of, w_ref, order)

            @pl.when(step == 0)
            def _():
                low = normed(x_ref[...], gain[0:1])
                mid[...] = x_ref[...] + self.self_attention(
                    low, w_of, kept, lambda n: key_mask(lens[n], rows // each)
                )

            @pl.when(step == 1)
            def _():
                low = normed(mid[...], gain[1:2])
                d_of = functools.partial(weights_of, d_ref, order)
                value = mid[...] + self.feed(low, w_of, d_of, hidden)
                last[...] = value
                encoded[...] = normed(value, gain[2:3])

        return self.call(
            kernel,
            2,
            [x, self.gain] + self.weight_specs(0, 0, 1, 2),
            [
                ((heads, rows, width), BF),
                ((rows, D), F32),
                ((heads, rows, width), BF),
                ((rows, D), F32),
                ((rows, D), BF),
            ],
            [],
            14,
        )

    def decoder(self, x, encoded):
        heads, each, unit, width = self.heads, self.each, self.unit, self.width
        rows, source = x.shape[0], encoded.shape[0]

        def kernel(order, head, lens, x_ref, enc_ref, gain, w_ref, d_ref, *refs):
            kept, one, kept_q, kept_k, two, hidden, three, final = refs
            step = pl.program_id(0)
            w_of = functools.partial(weights_of, w_ref, order)

            @pl.when(step == 0)
            def _():
                low = normed(x_ref[...], gain[3:4])
                one[...] = x_ref[...] + self.self_attention(
                    low, w_of, kept, lambda n: causal_mask(rows // each)
                )

            @pl.when(step == 1)
            def _():
                low = normed(one[...], gain[4:5])
                total = one[...]
                for j in range(heads):
                    w = w_of(j)
                    query = dot(low, w[:, :unit]).astype(BF)
                    both = dot(enc_ref[...], w[:, unit : 3 * unit]).astype(BF)
                    mixed = attend_heads(
                        query,
                        both[:, :unit],
                        both[:, unit:],
                        each,
                        lambda n: key_mask(lens[n], source // each),
                    )
                    kept_q[j, :, :unit] = query
                    kept_q[j, :, unit:] = mixed
                    kept_k[j] = both
                    total = total + dot_nt(mixed, w[:, 3 * unit :])
                two[...] = total

            @pl.when(step == 2)
            def _():
                low = normed(two[...], gain[5:6])
                d_of = functools.partial(weights_of, d_ref, order)
                value = two[...] + self.feed(low, w_of, d_of, hidden)
                three[...] = value
                final[...] = normed(value, gain[6:7] * D ** (-0.5))

        return self.call(
            kernel,
            3,
            [x, encoded, self.gain] + self.weight_specs(1, 0, 1, 3),
            [
                ((heads, rows, width), BF),
                ((rows, D), F32),
                ((heads, rows, 2 * unit), BF),
                ((heads, source, 2 * unit), BF),
                ((rows, D), F32),
                ((heads, rows, width), BF),
                ((rows, D), F32),
                ((rows, D), BF),
            ],
            [],
            16,
        )

    def feed_back(self, grad, inputs, gain_row, w_of, d_of, hidden, put):
        width = self.width
        low = grad.astype(BF)
        up_t, in_t = low.T, normed(inputs, gain_row).T
        back = None
        for j in range(self.heads):
            up, down, grown = w_of(j), d_of(j), hidden[j]
            grad_pre = jnp.where(grown > 0, dot(low, down), 0.0).astype(BF)
            put(j, 0, dot(in_t, grad_pre))
            put(j, width, dot(up_t, grown))
            part = dot_nt(grad_pre, up)
            back = part if back is None else back + part
        value, slope = norm_back(inputs, gain_row, back)
        return grad + value, slope

    def self_back(self, grad, inputs, gain_row, w_of, kept, mask_of, put):
        unit = self.unit
        low = grad.astype(BF)
        up_t, in_t = low.T, normed(inputs, gain_row).T
        back = None
        for j in range(self.heads):
            w = w_of(j)
            grad_mixed = dot(low, w[:, 3 * unit :]).astype(BF)
            slopes = attend_heads_back(
                kept[j, :, :unit],
                kept[j, :, unit : 2 * unit],
                kept[j, :, 2 * unit : 3 * unit],
                grad_mixed,
                self.each,
                mask_of,
            )
            three = jnp.concatenate(slopes, 1)
            put(j, 0, dot(in_t, three))
            put(j, 3 * unit, dot(up_t, kept[j, :, 3 * unit :]))
            part = dot_nt(three, w[:, : 3 * unit])
            back = part if back is None else back + part
        value, slope = norm_back(inputs, gain_row, back)
        return grad + value, slope

    def absolute_put(self, out_ref, order, head, base):
        def put(j, start, value):
            low = value.astype(BF)
            target = lax.rem(head[0] + j, self.heads)
            for place in range(self.dp):
                out_ref[order[place], target, :, base + start : base + start + value.shape[1]] = low[
                    place * self.deep : (place + 1) * self.deep
                ]

        return put

    def relative_put(self, keep_refs, send_ref):
        quarter = self.dp // 8

        def put(j, start, value):
            stop = start + value.shape[1]
            for place in range(self.dp):
                piece = value[place * self.deep : (place + 1) * self.deep]
                if place < 4 * quarter:
                    keep_refs[place // quarter][place % quarter, j, :, start:stop] = piece
                else:
                    send_ref[place - 4 * quarter, j, :, start:stop] = piece.astype(BF)

        return put

    def relative_outs(self, columns):
        quarter = self.dp // 8
        shape = (self.heads, self.deep, columns)
        return [((quarter,) + shape, F32)] * 4 + [((4 * quarter,) + shape, BF)]

    def flat(self, keeps_send):
        return [array.reshape(-1, array.shape[-1]) for array in keeps_send]

    def decoder_back(self, grad_final, x, encoded, kept_all):
        heads, each, unit, width = self.heads, self.each, self.unit, self.width
        kept, one, kept_q, kept_k, two, hidden, three = kept_all
        rows, source = x.shape[0], encoded.shape[0]

        def kernel(order, head, lens, *refs):
            g_ref, x_ref, enc_ref, gain, one, two, three, kept, kept_q, kept_k, hid = refs[:11]
            w_ref, d_ref, out, gains_out, grad_enc, grad_x, grad_ref = refs[11:]
            step = pl.program_id(0)
            w_of = functools.partial(weights_of, w_ref, order)

            @pl.when(step == 0)
            def _():
                gains_out[...] = jnp.zeros_like(gains_out)
                value, slope = norm_back(three[...], gain[6:7] * D ** (-0.5), g_ref[...])
                gains_out[6:7] = slope * D ** (-0.5)
                d_of = functools.partial(weights_of, d_ref, order)
                grad_ref[...], gains_out[5:6] = self.feed_back(
                    value,
                    two[...],
                    gain[5:6],
                    w_of,
                    d_of,
                    hid,
                    self.absolute_put(out, order, head, 2 * width),
                )

            @pl.when(step == 1)
            def _():
                put = self.absolute_put(out, order, head, width)
                low = grad_ref[...].astype(BF)
                up_t, in_t = low.T, normed(one[...], gain[4:5]).T
                enc_t = enc_ref[...].T
                back, back_enc = None, None
                for j in range(heads):
                    w = w_of(j)
                    grad_mixed = dot(low, w[:, 3 * unit :]).astype(BF)
                    dq, dk, dv = attend_heads_back(
                        kept_q[j, :, :unit],
                        kept_k[j, :, :unit],
                        kept_k[j, :, unit:],
                        grad_mixed,
                        each,
                        lambda n: key_mask(lens[n], source // each),
                    )
                    both = jnp.concatenate([dk, dv], 1)
                    put(j, 0, dot(in_t, dq))
                    put(j, unit, dot(enc_t, both))
                    put(j, 3 * unit, dot(up_t, kept_q[j, :, unit:]))
                    part, part_enc = dot_nt(dq, w[:, :unit]), dot_nt(both, w[:, unit : 3 * unit])
                    back = part if back is None else back + part
                    back_enc = part_enc if back_enc is None else back_enc + part_enc
                grad_enc[...] = back_enc
                value, gains_out[4:5] = norm_back(one[...], gain[4:5], back)
                grad_ref[...] += value

            @pl.when(step == 2)
            def _():
                value, gains_out[3:4] = self.self_back(
                    grad_ref[...],
                    x_ref[...],
                    gain[3:4],
                    w_of,
                    kept,
                    lambda n: causal_mask(rows // each),
                    self.absolute_put(out, order, head, 0),
                )
                grad_x[...] = value.astype(BF)

        return self.call(
            kernel,
            3,
            [grad_final, x, encoded, self.gain, one, two, three, kept, kept_q, kept_k, hidden]
            + self.weight_specs(1, 2, -1, 3),
            [
                ((self.dp, heads, self.deep, 4 * width), BF),
                ((8, D), F32),
                ((source, D), F32),
                ((rows, D), BF),
            ],
            [((rows, D), F32)],
            24,
        )

    def encoder_feed_back(self, grad_encoded, gain_grads, kept_all):
        _, mid, hidden, last = kept_all

        def kernel(order, head, lens, g_ref, more_ref, gain, mid, last, hid, w_ref, d_ref, *refs):
            *outs, grad, gains = refs
            gains[...] = more_ref[...]
            value, gains[2:3] = norm_back(last[...], gain[2:3], g_ref[...])
            grad[...], gains[1:2] = self.feed_back(
                value,
                mid[...],
                gain[1:2],
                functools.partial(weights_of, w_ref, order),
                functools.partial(weights_of, d_ref, order),
                hid,
                self.relative_put(outs[:4], outs[4]),
            )

        *outs, grad, gains = self.call(
            kernel,
            1,
            [grad_encoded, gain_grads, self.gain, mid, last, hidden] + self.weight_specs(0, 1, 0, 2),
            self.relative_outs(2 * self.width) + [(mid.shape, F32), ((8, D), F32)],
            [],
            13,
        )
        return self.flat(outs), grad, gains

    def encoder_self_back(self, grad_mid, gain_grads, x, kept, lanes):
        width = self.width
        rows = x.shape[0]

        def kernel(order, head, lens, g_ref, more_ref, x_ref, gain, kept, w_ref, *refs):
            *outs, grad_x = refs
            put = self.relative_put(outs[:4], outs[4])
            value, slope = self.self_back(
                g_ref[...],
                x_ref[...],
                gain[0:1],
                functools.partial(weights_of, w_ref, order),
                kept,
                lambda n: key_mask(lens[n], rows // self.each),
                put,
            )
            grad_x[...] = value.astype(BF)
            gains = jnp.concatenate(
                [slope, more_ref[1:8], jnp.zeros((lanes - 8, D), F32)], 0
            ).T
            for j in range(self.heads):
                put(j, width, gains)

        *outs, grad_x = self.call(
            kernel,
            1,
            [grad_mid, gain_grads, x, self.gain, kept] + self.weight_specs(0, 0, 0),
            self.relative_outs(width + lanes) + [((rows, D), BF)],
            [],
            16,
        )
        return self.flat(outs), grad_x


def body(
    dp,
    heads,
    source_ids,
    target_ids,
    source_lens,
    target_lens,
    kl_mask,
    teacher,
    *state,
):
    def transposed(group):
        embed, attn_in, attn_out, ff_in, ff_out, gains = group
        swap = functools.partial(jnp.swapaxes, axis1=-1, axis2=-2)
        return (swap(embed), attn_in, swap(attn_out), ff_in, swap(ff_out), gains)

    masters = transposed(state[:6])
    moments = transposed(state[6:12])
    seconds = transposed(state[12:])
    embed_t, attn_in, attn_out_t, ff_in, ff_out_t, gains = masters
    low = embed_t.astype(BF)
    vocab_local = embed_t.shape[1]
    head_pos = lax.axis_index("head")
    lead = (head_pos == 0).astype(F32)
    vocab_start = head_pos * vocab_local
    batch_size, source_len = source_ids.shape
    target_len = target_ids.shape[1]
    token_count = batch_size * target_len
    each = -(-batch_size // heads)
    padded = each * heads

    sides = [
        [attn_in[0, 0], attn_in[0, 1], attn_in[0, 2], attn_out_t[0], ff_in[0], ff_out_t[0]],
        [attn_in[1, 0], attn_in[1, 1], attn_in[1, 2], attn_out_t[1]]
        + [attn_in[2, 0], attn_in[2, 1], attn_in[2, 2], attn_out_t[2], ff_in[1], ff_out_t[1]],
    ]
    widths = [[matrix.shape[-1] for matrix in side] for side in sides]
    lanes = 128
    gain_rows = gains.shape[0]
    counted = jnp.full((1, gains.shape[1]), jnp.sum((target_lens > 0).astype(F32)))
    gain_block = jnp.pad(
        jnp.concatenate([gains, counted], 0).T, ((0, 0), (0, lanes - gain_rows - 1))
    )
    places = [0]
    bit = dp // 2
    while bit:
        places = places + [place ^ bit for place in places]
        bit //= 2
    order = lax.axis_index("dp") ^ jnp.array(places, jnp.int32)
    flat_in = attn_in.reshape((9,) + attn_in.shape[2:])
    arrays = [flat_in, attn_out_t, ff_in, ff_out_t, gain_block]
    enc_plan = [(0, 0), (0, 1), (0, 2), (1, 0), (2, 0), (3, 0), (4, None)]
    dec_plan = [(0, 3), (0, 4), (0, 5), (1, 1), (0, 6), (0, 7), (0, 8), (1, 2), (2, 1), (3, 1)]
    enc_packed = pack(arrays, enc_plan)
    dec_packed = pack(arrays, dec_plan)
    low, enc_packed, dec_packed = tie(low, enc_packed, dec_packed)
    table = GatherDp(low, dp)
    enc_came = gather_head(enc_packed, heads)
    if table.near:
        *table.near, enc_came[0] = tie(*table.near, *enc_came)[:3]
    enc_weights = lax.all_gather(jnp.stack(enc_came), "dp", axis=0)
    table.go_far()
    table_parts = table.parts()
    dec_came = gather_head(after(dec_packed, *enc_came[1:], *table.far), heads)

    def fill(array):
        return jnp.pad(array, ((0, padded - batch_size),) + ((0, 0),) * (array.ndim - 1))

    dec_ids = jnp.concatenate([jnp.zeros((batch_size, 1), jnp.int32), target_ids[:, :-1]], 1)
    enc_ids = jnp.roll(fill(source_ids).reshape(heads, -1), -head_pos, 0) - vocab_start
    dec_ids = jnp.roll(fill(dec_ids).reshape(heads, -1), -head_pos, 0) - vocab_start
    far_looked, table_rows = lookup(enc_ids[1:].reshape(-1), table_parts)
    own_ids = jnp.concatenate([enc_ids[0], dec_ids.reshape(-1)])
    own_looked = pick(own_ids, table_rows, [far_looked])
    dec_came[0] = after(dec_came[0], far_looked)
    dec_weights = lax.all_gather(jnp.stack(dec_came), "dp", axis=0)
    mine = each * source_len
    came = [own_looked[:mine]]
    for j in range(1, heads):
        came.append(head_shift(far_looked[(j - 1) * mine : j * mine], j, heads))
    dec_looked = own_looked[mine:]
    gain = jnp.take(enc_weights[:, 0, :, sum(widths[0]) :], order, axis=0)
    gain = gain[..., :8].astype(F32).reshape(D, 8).T
    real_count = jnp.maximum(jnp.sum(gain[gain_rows].reshape(dp, -1)[:, 0]), 1.0)
    my_lens = lax.dynamic_slice_in_dim(fill(source_lens), head_pos * each, each)
    layers = Layers(order, head_pos, my_lens, enc_weights, dec_weights, gain, each)
    enc_embed = functools.reduce(jnp.add, came).astype(F32)
    looked = after(dec_looked, enc_embed).reshape(heads, -1, D)
    *kept_enc, encoded = layers.encoder(enc_embed)
    dec_came = [looked[0]] + [head_shift(looked[j], j, heads) for j in range(1, heads)]
    dec_came[0] = after(dec_came[0], encoded)
    dec_embed = functools.reduce(jnp.add, dec_came).astype(F32)
    *kept_dec, my_final = layers.decoder(dec_embed, encoded)

    final = jnp.concatenate(gather_head(my_final, heads), 0)
    final = jnp.roll(final, head_pos * each * target_len, 0)[:token_count]
    valid = (jnp.arange(target_len)[None, :] < target_lens[:, None]).astype(F32)
    token_weight = (
        valid / (jnp.maximum(target_lens, 1).astype(F32)[:, None] * real_count)
    ).reshape(token_count)
    divergence_mask = kl_mask.astype(F32).reshape(token_count)
    labels = target_ids.reshape(token_count) - vocab_start
    labels = jnp.where((labels >= 0) & (labels < vocab_local), labels, -1)
    final_t = final.T
    teacher_t = teacher.T
    stats = logits_stats(final_t, labels, teacher_t, table_rows)
    every = jnp.stack(gather_head(stats, heads))
    peak_student = jnp.max(every[:, 0], 0)
    peak_teacher = jnp.max(every[:, 1], 0)
    off_s = every[:, 0] - peak_student
    off_t = jnp.exp((every[:, 1] - peak_teacher) / SOFTEN_FACTOR)
    sum_one = jnp.sum(every[:, 2] * jnp.exp(off_s), 0)
    sum_half = jnp.sum(every[:, 3] * jnp.exp(off_s / SOFTEN_FACTOR), 0)
    sum_teacher = jnp.sum(every[:, 4] * off_t, 0)
    sum_cross = jnp.sum(every[:, 5] * off_t, 0)
    label_logprob = jnp.sum(every[:, 6], 0)
    lse_one = peak_student + jnp.log(sum_one)
    lse_half = peak_student / SOFTEN_FACTOR + jnp.log(sum_half)
    lse_teacher = peak_teacher / SOFTEN_FACTOR + jnp.log(sum_teacher)
    cross_entropy = lse_one - label_logprob
    divergence_value = sum_cross / sum_teacher - lse_teacher + lse_half
    loss_part = lead * jnp.sum(
        token_weight
        * (
            cross_entropy
            + DIVERGENCE_SCALE * SOFTEN_FACTOR * SOFTEN_FACTOR * divergence_value * divergence_mask
        )
    )
    soft_half = DIVERGENCE_SCALE * SOFTEN_FACTOR * divergence_mask * token_weight
    soft_one = token_weight * jnp.exp(SOFTEN_FACTOR * lse_half - lse_one)
    nothing = jnp.zeros_like(lse_half)
    scalars = jnp.stack(
        [lse_half, lse_teacher, soft_one, soft_half, token_weight, nothing, nothing, nothing]
    )
    slope, part = logits_back(final_t, labels, scalars, teacher_t, table_rows, table_parts)
    part = part.T.reshape(batch_size, target_len, D)
    part = jnp.roll(fill(part).reshape(heads, each * target_len, D), -head_pos, 0)
    grad_final = scatter_head([part[j] for j in range(heads)], heads)

    dec_grads, gain_grads, grad_encoded, dec_low = layers.decoder_back(
        grad_final, dec_embed, encoded, kept_dec
    )
    dec_shard = lax.psum_scatter(dec_grads, "dp", scatter_dimension=0)
    dec_done = dec_shard
    dec_shard = lax.psum_scatter(dec_shard, "head", scatter_dimension=0)
    dec_rows = gather_head(dec_low, heads)
    feed_group, grad_mid, gain_grads = layers.encoder_feed_back(grad_encoded, gain_grads, kept_enc)
    grad_mid, *dec_rows = tie(grad_mid, *dec_rows)
    enc_scatter = ScatterDp(dp)
    enc_scatter.add(feed_group[:4], feed_group[4])
    self_group, enc_low = layers.encoder_self_back(
        grad_mid, gain_grads, enc_embed, kept_enc[0], lanes
    )

    enc_scatter.add(self_group[:4], self_group[4])
    enc_scatter.far(None)
    if enc_scatter.pieces:
        enc_low, *enc_scatter.later = tie(enc_low, *enc_scatter.later)
    enc_rows = gather_head(enc_low, heads)
    near_ids = jnp.concatenate([dec_ids.reshape(-1), enc_ids[0]])
    near_rows = jnp.concatenate(dec_rows + [enc_low], 0)
    columns = padded_to(vocab_local)
    (grad_table_t,) = spread(near_ids, near_rows, columns, final_t=final_t, slope=slope)

    def send_heads(shard):
        return [shard[0]] + [head_shift(shard[j], j, heads) for j in range(1, heads)]

    far_ids = enc_ids[1:].reshape(-1)
    far_rows = jnp.concatenate(enc_rows[1:], 0)
    enc_scatter.near(None)
    waits = [dec_done, *enc_scatter.last]
    *keeps, send = spread(far_ids, far_rows, columns, base=grad_table_t, waits=waits)
    scatter = ScatterDp(dp)
    scatter.add(keeps, send)
    (enc_shard,) = enc_scatter.result(None)
    scatter.far(4096, [enc_shard])
    enc_sums = send_heads(enc_shard.astype(BF).reshape(heads, -1, enc_shard.shape[1]))
    enc_sums[0] = enc_shard.reshape(heads, -1, enc_shard.shape[1])[0]
    scatter.near(4096)
    if scatter.last:
        scatter.last[0], dec_shard, *enc_sums = tie(scatter.last[0], dec_shard, *enc_sums)
    g_table, table_squares = scatter.result(4096, vocab_local)
    g_dec = dec_shard.astype(F32)
    g_enc = functools.reduce(jnp.add, [value.astype(F32) for value in enc_sums])

    def squares(array, axes):
        return jnp.sum(array * array, axis=axes).reshape(-1)

    weight_squares = jnp.concatenate(
        [
            squares(embed_t, (0, 1)),
            squares(attn_in, (2, 3)),
            squares(attn_out_t, (1, 2)),
            squares(ff_in, (1, 2)),
            squares(ff_out_t, (1, 2)),
            squares(gains, (1,)) * lead,
        ]
    )
    matrix_count = weight_squares.shape[0]
    gain_at = sum(widths[0])
    unit, wide = widths[0][0], widths[0][4]
    g_gain = g_enc[:, gain_at : gain_at + gain_rows]
    grad_squares = (
        jnp.sum(g_dec * g_dec)
        + jnp.sum(g_enc[:, :gain_at] * g_enc[:, :gain_at])
        + lead * jnp.sum(g_gain * g_gain)
    )
    first_line = jnp.pad(
        jnp.concatenate([weight_squares, loss_part.reshape(1), grad_squares.reshape(1)]),
        (0, lanes - matrix_count - 2),
    ).reshape(1, lanes)
    totals = sum_all(jnp.concatenate([first_line, table_squares], 0), dp, heads)
    grad_norm = jnp.sqrt(totals[0, matrix_count + 1] + jnp.sum(totals[1:]))
    total_loss = totals[0, matrix_count]
    clip = jnp.full((8, 128), jnp.minimum(1.0, CLIP_NORM / grad_norm))
    m_table, v_table, u_table, squares_table = column_call(
        functools.partial(lamb_columns_kernel, vocab_local, 2048),
        [masters[0], moments[0], seconds[0], g_table, clip],
        [(embed_t.shape[0], F32)] * 3,
        2048,
        sums=[(8, 128)],
    )

    def flat9(array):
        return array.reshape((9,) + array.shape[2:])

    def starts(width):
        out = [0]
        for columns in width:
            out.append(out[-1] + columns)
        return out

    at_enc = [2 * wide + k * unit for k in range(4)] + [0, wide]
    at_dec = starts(widths[1])
    places = [
        [(0, at_enc[k]) for k in range(3)]
        + [(1, at_dec[k]) for k in range(3)]
        + [(1, at_dec[k]) for k in range(4, 7)],
        [(0, at_enc[3]), (1, at_dec[3]), (1, at_dec[7])],
        [(0, at_enc[4]), (1, at_dec[8])],
        [(0, at_enc[5]), (1, at_dec[9])],
    ]
    groups = [
        tuple(flat9(stack[1]) if k == 1 else stack[k] for stack in (masters, moments, seconds))
        for k in range(1, 5)
    ]
    *fresh, squares_small = lamb_matrices(clip, [g_enc, g_dec], groups, places)
    m_gain, v_gain, u_gain = lamb(gains, moments[5], seconds[5], g_gain.T, clip[0, 0])
    gain_squares = jnp.pad(squares(u_gain, (1,)) * lead, (0, lanes - gain_rows)).reshape(1, lanes)
    small_count = sum(len(matrices) for matrices in places)
    update_totals = sum_all(
        jnp.concatenate([squares_table, squares_small, gain_squares], 0), dp, heads
    )
    update_squares = jnp.concatenate(
        [
            jnp.sum(update_totals[:8]).reshape(1),
            jnp.sum(update_totals[8 : 8 + small_count], 1),
            update_totals[-1, :gain_rows],
        ]
    )
    rates = LEARN_RATE * jnp.sqrt(totals[0, :matrix_count]) / (jnp.sqrt(update_squares) + 1e-06)
    fresh_m = [m_table] + list(fresh[0::3]) + [m_gain]
    fresh_v = [v_table] + list(fresh[1::3]) + [v_gain]
    updates = [u_table] + list(fresh[2::3]) + [u_gain]
    for stack in (fresh_m, fresh_v, updates):
        stack[1] = stack[1].reshape(attn_in.shape)
    shapes = [(1, 1), (3, 3, 1, 1), (3, 1, 1), (2, 1, 1), (2, 1, 1), (gain_rows, 1)]
    fresh_w, start = [], 0
    for master, update, shape in zip(masters, updates, shapes, strict=True):
        count = 1
        for extent in shape:
            count *= extent
        fresh_w.append(master - rates[start : start + count].reshape(shape) * update)
        start += count
    return (
        total_loss.reshape(1),
        grad_norm.reshape(1),
        *transposed(fresh_w),
        *transposed(fresh_m),
        *transposed(fresh_v),
    )


def solution(mesh):
    params = (
        P("head", "dp"),
        P(None, None, "dp", "head"),
        P(None, "head", "dp"),
        P(None, "dp", "head"),
        P(None, "head", "dp"),
        P(None, "dp"),
    )
    return jax.shard_map(
        functools.partial(body, mesh.shape["dp"], mesh.shape["head"]),
        mesh=mesh,
        in_specs=(
            P("dp", None),
            P("dp", None),
            P("dp"),
            P("dp"),
            P("dp", None),
            P("dp", "head"),
            *params,
            *params,
            *params,
        ),
        out_specs=(P(), P(), *params, *params, *params),
        check_vma=False,
    )
```

```python
import functools

import jax
import jax.numpy as jnp
from jax import lax
from jax.experimental import pallas as pl
from jax.experimental.pallas import tpu as pltpu
from jax.sharding import PartitionSpec as P

D = 512
DH = 64
STEP_NUM = 10

NORM_EPS = 1e-06
SOFTEN_FACTOR = 2.0
DIVERGENCE_SCALE = 1.0
CLIP_NORM = 0.02
BETA_ONE = 0.9
BETA_TWO = 0.999
ADAM_EPS = 1e-08
WEIGHT_DECAY = 0.01
LEARN_RATE = 0.3

BF = jnp.bfloat16
F32 = jnp.float32


def dp_swap(x, bit, dp):
    return lax.ppermute(x, "dp", [(i, i ^ bit) for i in range(dp)])


def head_shift(x, step, heads):
    return lax.ppermute(x, "head", [(i, (i + step) % heads) for i in range(heads)])


def after(x, *earlier):
    return lax.optimization_barrier((x, *earlier))[0]


def tie(chain, *arrived):
    return lax.optimization_barrier((chain, *arrived))


class GatherDp:
    def __init__(self, x, dp):
        self.x, self.dp = x, dp
        self.rows = x.shape[0]
        self.near = (dp_swap(x, 4, dp), dp_swap(x, 2, dp)) if dp == 8 else ()
        self.far = ()

    def go_far(self):
        if self.dp == 8:
            half = self.rows // 2
            part_y, part_x = self.near
            self.far = (dp_swap(part_y[:half], 2, self.dp), dp_swap(part_x[half:], 4, self.dp))

    def parts(self):
        dp = self.dp
        if dp == 8:
            here = [self.x, *self.near, *self.far]
            return here + [dp_swap(part, 1, dp) for part in here]
        whole = self.x
        bit = dp // 2
        while bit:
            whole = jnp.concatenate([whole, dp_swap(whole, bit, dp)], 0)
            bit //= 2
        return [whole]


def gather_head(x, heads):
    return [x] + [head_shift(x, heads - j, heads) for j in range(1, heads)]


def scatter_head(parts, heads):
    total = parts[0].astype(F32)
    for j in range(1, heads):
        total = total + head_shift(parts[j].astype(BF), j, heads).astype(F32)
    return total


def sum_head(x, heads):
    total = x
    for j in range(1, heads):
        total = total + head_shift(x, j, heads)
    return total


def sum_all(x, dp, heads):
    return sum_head(sum_dp(x, dp), heads)


def sum_dp(x, dp):
    bit = 1
    while bit < dp:
        x = x + dp_swap(x, bit, dp)
        bit *= 2
    return x


def ordered(kernel, count, waits):
    if not waits:
        return kernel

    def body(*refs):
        kernel(*refs[:count], *refs[count + len(waits) :])

    return body


ANYWHERE = pl.BlockSpec(memory_space=pl.ANY)


def stacked(refs):
    return refs[0][...] if len(refs) == 1 else jnp.concatenate([ref[...] for ref in refs], 0)


def lookup_kernel(vocab, tile, ids_ref, *refs):
    *table_refs, out_ref, rows_ref, acc_ref = refs
    step = pl.program_id(0)

    @pl.when(step == 0)
    def _():
        acc_ref[...] = jnp.zeros_like(acc_ref)

    place = lax.broadcasted_iota(jnp.int32, (1, tile), 1)
    block = stacked(table_refs)
    block = jnp.where(place < vocab - step * tile, block, jnp.zeros_like(block)).T
    rows_ref[...] = block
    hit = (ids_ref[...] - step * tile == place).astype(BF)
    acc_ref[...] += jnp.dot(hit, block, preferred_element_type=F32)

    @pl.when(step == pl.num_programs(0) - 1)
    def _():
        out_ref[...] = acc_ref[...].astype(BF)


def column_specs(parts, tile):
    return [pl.BlockSpec((part.shape[0], tile), lambda i: (0, i)) for part in parts]


def fixed(shape):
    return pl.BlockSpec(shape, lambda i: (0,) * len(shape))


VMEM_LIMIT = 56 * 2**20


def cost(microseconds):
    return pl.CostEstimate(
        flops=int(1.15e9 * microseconds),
        bytes_accessed=int(3.7e6 * microseconds),
        transcendentals=0,
    )


def padded_to(columns, step=128):
    return -(-columns // step) * step


def lookup(ids, table_parts):
    rows, vocab = ids.shape[0], table_parts[0].shape[1]
    tile = 2048
    return pl.pallas_call(
        functools.partial(lookup_kernel, vocab, tile),
        out_shape=[
            jax.ShapeDtypeStruct((rows, D), BF),
            jax.ShapeDtypeStruct((padded_to(vocab), D), BF),
        ],
        grid=(pl.cdiv(vocab, tile),),
        in_specs=[fixed((rows, 1))] + column_specs(table_parts, tile),
        out_specs=[fixed((rows, D)), pl.BlockSpec((tile, D), lambda i: (i, 0))],
        scratch_shapes=[pltpu.VMEM((rows, D), F32)],
        cost_estimate=cost(26),
        compiler_params=pltpu.CompilerParams(vmem_limit_bytes=VMEM_LIMIT),
    )(ids.reshape(rows, 1), *table_parts)


def pick(ids, table_rows, waits):
    rows, vocab = ids.shape[0], table_rows.shape[0]
    tile = 2048
    return pl.pallas_call(
        ordered(functools.partial(pick_kernel, vocab, tile), 2, waits),
        out_shape=jax.ShapeDtypeStruct((rows, D), BF),
        grid=(pl.cdiv(vocab, tile),),
        in_specs=[fixed((rows, 1)), pl.BlockSpec((tile, D), lambda i: (i, 0))]
        + [ANYWHERE] * len(waits),
        out_specs=fixed((rows, D)),
        scratch_shapes=[pltpu.VMEM((rows, D), F32)],
        cost_estimate=cost(12),
        compiler_params=pltpu.CompilerParams(vmem_limit_bytes=VMEM_LIMIT),
    )(ids.reshape(rows, 1), table_rows, *waits)


def pick_kernel(vocab, tile, ids_ref, rows_ref, out_ref, acc_ref):
    step = pl.program_id(0)

    @pl.when(step == 0)
    def _():
        acc_ref[...] = jnp.zeros_like(acc_ref)

    place = lax.broadcasted_iota(jnp.int32, (1, tile), 1)
    below = lax.broadcasted_iota(jnp.int32, (tile, 1), 0)
    block = rows_ref[...]
    block = jnp.where(below < vocab - step * tile, block, jnp.zeros_like(block))
    hit = (ids_ref[...] - step * tile == place).astype(BF)
    acc_ref[...] += jnp.dot(hit, block, preferred_element_type=F32)

    @pl.when(step == pl.num_programs(0) - 1)
    def _():
        out_ref[...] = acc_ref[...].astype(BF)


def spread_kernel(tile, first, ids_ref, rows_ref, *refs):
    step = pl.program_id(0)
    turned_ref = refs[-1]

    @pl.when(step == 0)
    def _():
        turned_ref[...] = rows_ref[...].T

    place = (first + step) * tile + lax.broadcasted_iota(jnp.int32, (1, tile), 1)
    hit = (ids_ref[...] == place).astype(BF)
    total = jnp.dot(turned_ref[...], hit, preferred_element_type=F32)
    if len(refs) == 4:
        final_ref, slope_ref, out_ref, _ = refs
        out_ref[...] = total + lax.dot_general(
            final_ref[...], slope_ref[...], (((1,), (1,)), ((), ())), preferred_element_type=F32
        )
    else:
        base_ref, *keep_refs, send_ref, _ = refs
        total = base_ref[...] + total
        deep = D // 8
        for number, keep_ref in enumerate(keep_refs):
            keep_ref[...] = total[number * deep : (number + 1) * deep]
        send_ref[...] = total[D // 2 :].astype(BF)


SPREAD_TILE = 1024


def spread(ids, rows_low, columns, final_t=None, slope=None, base=None, first=0, waits=()):
    rows = ids.shape[0]
    tile = SPREAD_TILE
    if base is None:
        shapes = [((D, columns), F32)]
        more = [final_t, slope]
        specs = [fixed(final_t.shape), pl.BlockSpec((tile, slope.shape[1]), lambda i: (i, 0))]
    else:
        shapes = [((D // 8, columns), F32)] * 4 + [((D // 2, columns), BF)]
        more = [base]
        specs = [pl.BlockSpec((D, tile), lambda i: (0, i + first))]
    return pl.pallas_call(
        ordered(functools.partial(spread_kernel, tile, first), 2 + len(more), waits),
        out_shape=[jax.ShapeDtypeStruct(*shape) for shape in shapes],
        grid=(pl.cdiv(columns, tile),),
        in_specs=[fixed((rows, 1)), fixed((rows, D))] + specs + [ANYWHERE] * len(waits),
        out_specs=[pl.BlockSpec((shape[0][0], tile), lambda i: (0, i)) for shape in shapes],
        scratch_shapes=[pltpu.VMEM((D, rows), BF)],
        cost_estimate=cost(18 if base is None else 9),
        compiler_params=pltpu.CompilerParams(vmem_limit_bytes=VMEM_LIMIT),
    )(ids.reshape(rows, 1), rows_low, *more, *waits)


def column_call(kernel, inputs, outputs, tile, sums=(), columns=None, waits=()):
    columns = columns or inputs[0].shape[1]
    out_shape = [jax.ShapeDtypeStruct((rows, columns), dtype) for rows, dtype in outputs]
    out_specs = [pl.BlockSpec((rows, tile), lambda i: (0, i)) for rows, _ in outputs]
    for shape in sums:
        out_shape.append(jax.ShapeDtypeStruct(shape, F32))
        out_specs.append(fixed(shape))
    return pl.pallas_call(
        ordered(kernel, len(inputs), waits),
        out_shape=out_shape,
        grid=(pl.cdiv(columns, tile),),
        in_specs=[
            pl.BlockSpec((array.shape[0], tile), lambda i: (0, i))
            if array.shape[1] >= columns
            else fixed(array.shape)
            for array in inputs
        ]
        + [ANYWHERE] * len(waits),
        out_specs=out_specs,
        cost_estimate=cost(5),
        compiler_params=pltpu.CompilerParams(vmem_limit_bytes=VMEM_LIMIT),
    )(*inputs, *waits)


def first_sums_kernel(groups, *refs):
    d_low, d_high, x_sum, y_sum = refs[4 * groups :]
    start = 0
    for group in range(groups):
        y_ref, x_ref, d_ref, got_ref = refs[4 * group : 4 * group + 4]
        deep, columns = y_ref.shape
        half, stop = deep // 2, start + columns
        y_sum[:, start:stop] = y_ref[...] + got_ref[deep : 2 * deep].astype(F32)
        x_sum[:, start:stop] = x_ref[...] + got_ref[2 * deep : 3 * deep].astype(F32)
        d = (d_ref[...] + got_ref[3 * deep :].astype(F32)).astype(BF)
        d_low[:, start:stop] = d[:half]
        d_high[:, start:stop] = d[half:]
        start = stop


def second_sums_kernel(y_sum, got_a, x_sum, got_b, y_out, x_out):
    half = got_a.shape[0]
    y_out[:half] = (y_sum[:half] + got_a[...].astype(F32)).astype(BF)
    y_out[half:] = y_sum[half:].astype(BF)
    x_out[:half] = x_sum[:half].astype(BF)
    x_out[half:] = (x_sum[half:] + got_b[...].astype(F32)).astype(BF)


def lane_sums(value):
    rows, columns = value.shape
    total = value[:, :128]
    for start in range(128, columns, 128):
        total = total + value[:, start : start + 128]
    out = total[:8]
    for start in range(8, rows, 8):
        out = out + total[start : start + 8]
    return out


def inside(columns, tile, value):
    place = pl.program_id(0) * tile + lax.broadcasted_iota(jnp.int32, (1, tile), 1)
    return jnp.where(place < columns, value, 0.0)


def last_sums_kernel(groups, columns, tile, *refs):
    y_ref, x_ref, out = refs[2 * groups : 2 * groups + 3]
    more = x_ref[...].astype(F32) + y_ref[...].astype(F32)
    start = 0
    for group in range(groups):
        own, got = refs[2 * group : 2 * group + 2]
        deep, stop = own.shape[0], start + own.shape[1]
        out[:, start:stop] = own[...] + got[:deep].astype(F32) + more[:, start:stop]
        start = stop
    if columns is not None:
        squares = refs[-1]

        @pl.when(pl.program_id(0) == 0)
        def _():
            squares[...] = jnp.zeros_like(squares)

        squares[...] += lane_sums(inside(columns, tile, out[...] * out[...]))


class ScatterDp:
    def __init__(self, dp):
        self.dp, self.groups = dp, []

    def add(self, keeps, send):
        self.groups.append((*keeps, dp_swap(send, 1, self.dp)))

    def far(self, tile, waits=()):
        dp = self.dp
        self.pieces = ()
        if dp == 8:
            rows = self.groups[0][0].shape[0]
            inputs, columns = [], 0
            for own, y, x, d, got in self.groups:
                inputs += [y, x, d, got]
                columns += own.shape[1]
            outputs = [(rows // 2, BF)] * 2 + [(rows, F32)] * 2
            kernel = functools.partial(first_sums_kernel, len(self.groups))
            d_low, d_high, *self.later = sums_call(
                kernel, inputs, outputs, columns, tile, waits=waits
            )
            self.pieces = [dp_swap(d_low, 2, dp), dp_swap(d_high, 4, dp)]

    def near(self, tile, waits=()):
        dp = self.dp
        self.last = self.ready = ()
        if dp == 8:
            x_sum, y_sum = self.later
            rows, columns = y_sum.shape
            y_sum, x_sum = sums_call(
                second_sums_kernel,
                [y_sum, self.pieces[0], x_sum, self.pieces[1]],
                [(rows, BF)] * 2,
                columns,
                tile,
                waits=waits,
            )
            self.ready = [y_sum, x_sum]
            self.last = [dp_swap(y_sum, 4, dp), dp_swap(x_sum, 2, dp)]

    def result(self, tile, columns=None, waits=()):
        dp = self.dp
        if dp != 8:
            total = jnp.concatenate(
                [
                    jnp.concatenate(group[:4], 0) + group[4].astype(F32)
                    for group in self.groups
                ],
                1,
            )
            bit = 2
            while bit < dp:
                rows = total.shape[0] // 2
                total = total[:rows] + dp_swap(total[rows:].astype(BF), bit, dp).astype(F32)
                bit *= 2
            total = total[:, :columns]
            if columns is None:
                return [total]
            return [total, jnp.zeros((8, 128), F32).at[0, 0].set(jnp.sum(total * total))]
        inputs, wide = [], 0
        for own, _, _, _, got in self.groups:
            inputs += [own, got]
            wide += own.shape[1]
        inputs += self.last
        kernel = functools.partial(last_sums_kernel, len(self.groups), columns, tile)
        sums = [] if columns is None else [(8, 128)]
        rows = self.groups[0][0].shape[0]
        return sums_call(kernel, inputs, [(rows, F32)], columns or wide, tile, sums, waits)


def sums_call(kernel, inputs, outputs, columns, tile, sums=(), waits=()):
    if tile is not None:
        return column_call(kernel, inputs, outputs, tile, sums, columns, waits)
    everything = pl.BlockSpec(memory_space=pltpu.VMEM)
    return pl.pallas_call(
        ordered(kernel, len(inputs), waits),
        in_specs=[everything] * len(inputs) + [ANYWHERE] * len(waits),
        out_shape=[jax.ShapeDtypeStruct((rows, columns), dtype) for rows, dtype in outputs],
        cost_estimate=cost(5),
        compiler_params=pltpu.CompilerParams(vmem_limit_bytes=VMEM_LIMIT),
    )(*inputs, *waits)


HALF = 0.5 * 1.4426950408889634
CHUNKS = 4
BACK_CHUNKS = 1


def logits_kernel(vocab, tile, final_ref, label_ref, teacher_ref, table_ref, out_ref, *stats):
    top_s, top_t, one, half, teach, cross, label = stats
    step = pl.program_id(0)
    last = pl.num_programs(0) - 1

    @pl.when(step == 0)
    def _():
        top_s[...] = jnp.full_like(top_s, -1e30)
        top_t[...] = jnp.full_like(top_t, -1e30)
        for ref in (one, half, teach, cross, label):
            ref[...] = jnp.zeros_like(ref)

    def work(valid):
        for chunk in range(CHUNKS):
            if chunk * part < valid:
                work_part(chunk * part, min(valid - chunk * part, part))

    part = tile // CHUNKS

    def work_part(start, valid):
        logits = jnp.dot(
            table_ref[start : start + part], final_ref[...], preferred_element_type=F32
        )
        tokens = logits.shape[1]

        def folded(value):
            return (value * HALF).reshape(part // 8, 8, tokens)

        student = folded(logits)
        teacher = folded(teacher_ref[start : start + part].astype(F32))
        place = 8 * lax.broadcasted_iota(jnp.int32, (part // 8, 8, 1), 0)
        place = place + lax.broadcasted_iota(jnp.int32, (part // 8, 8, 1), 1)
        if valid < part:
            student = jnp.where(place < valid, student, -1e30)
            teacher = jnp.where(place < valid, teacher, -1e30)
        old_s, old_t = top_s[...], top_t[...]
        new_s = jnp.maximum(old_s, jnp.max(student, 0))
        new_t = jnp.maximum(old_t, jnp.max(teacher, 0))
        top_s[...] = new_s
        top_t[...] = new_t
        scale_s = jnp.exp2(old_s - new_s)
        scale_t = jnp.exp2(old_t - new_t)
        e = jnp.exp2(student - new_s[None])
        half[...] = half[...] * scale_s + jnp.sum(e, 0)
        one[...] = one[...] * (scale_s * scale_s) + jnp.sum(e * e, 0)
        e = jnp.exp2(teacher - new_t[None])
        teach[...] = teach[...] * scale_t + jnp.sum(e, 0)
        cross[...] = cross[...] * scale_t + jnp.sum(e * (teacher - student), 0)
        labels = (label_ref[...] - (step * tile + start))[None]
        label[...] += jnp.sum(jnp.where(labels == place, student, 0.0), 0)

    rest = vocab - (pl.cdiv(vocab, tile) - 1) * tile
    if rest == tile:
        work(tile)
    else:

        @pl.when(step < last)
        def _():
            work(tile)

        @pl.when(step == last)
        def _():
            work(rest)

    @pl.when(step == last)
    def _():
        peak_s = jnp.max(top_s[...], 0, keepdims=True)
        peak_t = jnp.max(top_t[...], 0, keepdims=True)
        by_s = jnp.exp2(top_s[...] - peak_s)
        by_t = jnp.exp2(top_t[...] - peak_t)

        def total(value):
            return jnp.sum(value, 0, keepdims=True)

        out_ref[0:1] = peak_s * (1.0 / HALF)
        out_ref[1:2] = peak_t * (1.0 / HALF)
        out_ref[2:3] = total(one[...] * (by_s * by_s))
        out_ref[3:4] = total(half[...] * by_s)
        out_ref[4:5] = total(teach[...] * by_t)
        out_ref[5:6] = total(cross[...] * by_t) * (0.5 / HALF)
        out_ref[6:7] = total(label[...]) * (1.0 / HALF)
        out_ref[7:8] = jnp.zeros_like(peak_s)


def logits_stats(final_t, labels, teacher_t, table_rows):
    vocab, tokens = teacher_t.shape
    tile = 1024
    return pl.pallas_call(
        functools.partial(logits_kernel, vocab, tile),
        out_shape=jax.ShapeDtypeStruct((8, tokens), F32),
        grid=(pl.cdiv(vocab, tile),),
        in_specs=[
            fixed(final_t.shape),
            fixed((1, tokens)),
            pl.BlockSpec((tile, tokens), lambda i: (i, 0)),
            pl.BlockSpec((tile, D), lambda i: (i, 0)),
        ],
        out_specs=fixed((8, tokens)),
        scratch_shapes=[pltpu.VMEM((8, tokens), F32)] * 7,
        cost_estimate=cost(17),
        compiler_params=pltpu.CompilerParams(vmem_limit_bytes=VMEM_LIMIT),
    )(final_t, labels.reshape(1, tokens), teacher_t, table_rows)


def logits_back_kernel(vocab, tile, final_ref, label_ref, scalar_ref, teacher_ref, *refs):
    rows_ref, *table_refs, slope_ref, back_ref, acc_ref = refs
    step = pl.program_id(0)
    last = pl.num_programs(0) - 1

    @pl.when(step == 0)
    def _():
        acc_ref[...] = jnp.zeros_like(acc_ref)

    log2e = 2.0 * HALF
    lse_half = scalar_ref[0:1] * log2e
    lse_teacher = scalar_ref[1:2] * log2e
    soft_one = scalar_ref[2:3]
    soft_half = scalar_ref[3:4]
    weight = scalar_ref[4:5]
    part = tile // BACK_CHUNKS
    total = acc_ref[...]
    for start in range(0, tile, part):
        left = vocab - step * tile - start
        good = lax.broadcasted_iota(jnp.int32, (1, part), 1) < left
        block = jnp.concatenate([ref[:, start : start + part] for ref in table_refs], 0)
        block = jnp.where(good, block, jnp.zeros_like(block))
        place = lax.broadcasted_iota(jnp.int32, (part, 1), 0)
        logits = jnp.dot(
            rows_ref[start : start + part], final_ref[...], preferred_element_type=F32
        )
        student = jnp.exp2(logits * HALF - lse_half)
        teacher = teacher_ref[start : start + part].astype(F32)
        teacher = jnp.exp2(teacher * HALF - lse_teacher)
        labels = label_ref[...] - (step * tile + start)
        slope = student * (soft_one * student + soft_half) - soft_half * teacher
        slope = slope - jnp.where(labels == place, weight, 0.0)
        slope = jnp.where(place < left, slope, 0.0).astype(BF)
        slope_ref[start : start + part] = slope
        total = total + jnp.dot(block, slope, preferred_element_type=F32)
    acc_ref[...] = total

    @pl.when(step == last)
    def _():
        back_ref[...] = acc_ref[...].astype(BF)


def logits_back(final_t, labels, scalars, teacher_t, table_rows, table_parts):
    vocab, tokens = teacher_t.shape
    tile = 1024
    return pl.pallas_call(
        functools.partial(logits_back_kernel, vocab, tile),
        out_shape=[
            jax.ShapeDtypeStruct((padded_to(vocab), tokens), BF),
            jax.ShapeDtypeStruct((D, tokens), BF),
        ],
        grid=(pl.cdiv(vocab, tile),),
        in_specs=[
            fixed(final_t.shape),
            fixed((1, tokens)),
            fixed(scalars.shape),
            pl.BlockSpec((tile, tokens), lambda i: (i, 0)),
            pl.BlockSpec((tile, D), lambda i: (i, 0)),
        ]
        + column_specs(table_parts, tile),
        out_specs=[pl.BlockSpec((tile, tokens), lambda i: (i, 0)), fixed((D, tokens))],
        scratch_shapes=[pltpu.VMEM((D, tokens), F32)],
        cost_estimate=cost(22),
        compiler_params=pltpu.CompilerParams(vmem_limit_bytes=VMEM_LIMIT),
    )(final_t, labels.reshape(1, tokens), scalars, teacher_t, table_rows, *table_parts)


BIAS_ONE = 1.0 - BETA_ONE**STEP_NUM
BIAS_TWO = 1.0 - BETA_TWO**STEP_NUM


def lamb(weight, moment, second, grad, clip):
    grad = grad * clip
    moment = BETA_ONE * moment + (1 - BETA_ONE) * grad
    second = BETA_TWO * second + (1 - BETA_TWO) * grad * grad
    update = (
        moment * (1.0 / BIAS_ONE) / (jnp.sqrt(second * (1.0 / BIAS_TWO)) + ADAM_EPS)
        + WEIGHT_DECAY * weight
    )
    return moment, second, update


def lamb_columns_kernel(columns, tile, left, *refs):
    w, m, v, g_left, g_right, clip, m_out, v_out, u_out, squares = refs
    grad = jnp.where(pl.program_id(0) < left, g_left[...], g_right[...])
    moment, second, update = lamb(w[...], m[...], v[...], grad, clip[0:1, 0:1])
    m_out[...] = moment
    v_out[...] = second
    u_out[...] = update

    @pl.when(pl.program_id(0) == 0)
    def _():
        squares[...] = jnp.zeros_like(squares)

    squares[...] += lane_sums(inside(columns, tile, update * update))


def lamb_columns(state, g_left, g_right, clip, tile):
    rows, columns = state[0].shape
    left = g_left.shape[1] // tile
    spec = pl.BlockSpec((rows, tile), lambda i: (0, i))
    return pl.pallas_call(
        functools.partial(lamb_columns_kernel, columns, tile, left),
        out_shape=[jax.ShapeDtypeStruct((rows, columns), F32)] * 3
        + [jax.ShapeDtypeStruct((8, 128), F32)],
        grid=(pl.cdiv(columns, tile),),
        in_specs=[
            spec,
            spec,
            spec,
            pl.BlockSpec((rows, tile), lambda i: (0, jnp.minimum(i, left - 1))),
            pl.BlockSpec((rows, tile), lambda i: (0, jnp.maximum(i - left, 0))),
            fixed(clip.shape),
        ],
        out_specs=[spec, spec, spec, fixed((8, 128))],
        cost_estimate=cost(8),
        compiler_params=pltpu.CompilerParams(vmem_limit_bytes=VMEM_LIMIT),
    )(*state, g_left, g_right, clip)


def step_kernel(counts, rates, *refs):
    groups = len(counts)
    row = 1
    for group, count in enumerate(counts):
        w, u, out = refs[2 * group], refs[2 * group + 1], refs[2 * groups + group]
        for number in range(count):
            out[number] = w[number] - rates[row] * u[number]
            row += 1


def step_matrices(rates, pairs):
    flat = [array for pair in pairs for array in pair]
    return pl.pallas_call(
        functools.partial(step_kernel, [pair[0].shape[0] for pair in pairs]),
        out_shape=[jax.ShapeDtypeStruct(pair[0].shape, F32) for pair in pairs],
        in_specs=[pl.BlockSpec(memory_space=pltpu.SMEM)]
        + [pl.BlockSpec(memory_space=pltpu.VMEM)] * len(flat),
        cost_estimate=cost(3),
        compiler_params=pltpu.CompilerParams(vmem_limit_bytes=VMEM_LIMIT),
    )(rates, *flat)


def lamb_matrices_kernel(places, clip_ref, *refs):
    grads = refs[:2]
    count = len(places)
    states = refs[2 : 2 + 3 * count]
    outs = refs[2 + 3 * count : -1]
    squares = refs[-1]
    squares[...] = jnp.zeros_like(squares)
    clip = clip_ref[0:1, 0:1]
    row = 0
    for group, matrices in enumerate(places):
        w, m, v = states[3 * group : 3 * group + 3]
        m_out, v_out, u_out = outs[3 * group : 3 * group + 3]
        width = w.shape[-1]
        for number, (array, start) in enumerate(matrices):
            grad = grads[array][:, start : start + width]
            moment, second, update = lamb(w[number], m[number], v[number], grad, clip)
            m_out[number] = moment
            v_out[number] = second
            u_out[number] = update
            total = jnp.sum(update * update, 0, keepdims=True)
            lanes = min(128, width)
            line = total[:, :lanes]
            for first in range(lanes, width, lanes):
                line = line + total[:, first : first + lanes]
            squares[row : row + 1, :lanes] = line
            row += 1


def lamb_matrices(clip, grads, groups, places):
    flat = [array for group in groups for array in group]
    shapes = [jax.ShapeDtypeStruct(group[0].shape, F32) for group in groups for _ in range(3)]
    rows = 8 * pl.cdiv(sum(len(matrices) for matrices in places), 8)
    return pl.pallas_call(
        functools.partial(lamb_matrices_kernel, places),
        out_shape=shapes + [jax.ShapeDtypeStruct((rows, 128), F32)],
        cost_estimate=cost(4),
        compiler_params=pltpu.CompilerParams(vmem_limit_bytes=VMEM_LIMIT),
    )(clip, *grads, *flat)


def pack_kernel(heads_of, *refs):
    *in_refs, out_ref = refs
    start = 0
    for number, index in heads_of:
        value = in_refs[number][...] if index is None else in_refs[number][index]
        out_ref[:, start : start + value.shape[1]] = value.astype(BF)
        start += value.shape[1]


def pack(arrays, plan):
    columns = sum(arrays[number].shape[-1] for number, _ in plan)
    return pl.pallas_call(
        functools.partial(pack_kernel, plan),
        out_shape=jax.ShapeDtypeStruct((arrays[0].shape[-2], columns), BF),
        cost_estimate=cost(2),
        compiler_params=pltpu.CompilerParams(vmem_limit_bytes=VMEM_LIMIT),
    )(*arrays)


def dot(a, b):
    return jnp.dot(a, b, preferred_element_type=F32)


def dot_nt(a, b):
    return lax.dot_general(a, b, (((1,), (1,)), ((), ())), preferred_element_type=F32)


def dot_tn(a, b):
    return lax.dot_general(a, b, (((0,), (0,)), ((), ())), preferred_element_type=F32)


def root(inputs):
    return lax.rsqrt(jnp.mean(inputs * inputs, -1, keepdims=True) + NORM_EPS)


def normed(inputs, gain_row):
    return (inputs * root(inputs) * gain_row).astype(BF)


def norm_back(inputs, gain_row, upstream):
    factor = root(inputs)
    scaled = upstream * gain_row
    inner = jnp.mean(scaled * inputs, -1, keepdims=True)
    return (
        factor * (scaled - inputs * factor * factor * inner),
        jnp.sum(upstream * inputs * factor, axis=0, keepdims=True),
    )


def attn_probs(query, keys_all, allowed):
    scores = jnp.where(allowed, dot_nt(query, keys_all) * DH ** (-0.5), -1000000000.0)
    grown = jnp.exp(scores - jnp.max(scores, -1, keepdims=True))
    return grown * (1.0 / jnp.sum(grown, -1, keepdims=True))


def key_mask(count, keys):
    return lax.broadcasted_iota(jnp.int32, (1, keys), 1) < count


def causal_mask(rows):
    return lax.broadcasted_iota(jnp.int32, (rows, rows), 0) >= lax.broadcasted_iota(
        jnp.int32, (rows, rows), 1
    )


def weights_of(ref, order_ref, j):
    return jnp.concatenate([ref[order_ref[place], j] for place in range(ref.shape[0])], 0)


def attend_heads(query, keys_all, values, each, mask_of):
    rows, source = query.shape[0] // each, keys_all.shape[0] // each
    out = []
    for number in range(each):
        a, b = number * rows, number * source
        line = []
        for first in range(0, query.shape[1], DH):
            probs = attn_probs(
                query[a : a + rows, first : first + DH],
                keys_all[b : b + source, first : first + DH],
                mask_of(number),
            ).astype(BF)
            line.append(dot(probs, values[b : b + source, first : first + DH]).astype(BF))
        out.append(jnp.concatenate(line, 1) if len(line) > 1 else line[0])
    return jnp.concatenate(out, 0) if each > 1 else out[0]


def attend_heads_back(query, keys_all, values, grad_mixed, each, mask_of):
    rows, source = query.shape[0] // each, keys_all.shape[0] // each
    outs = ([], [], [])
    for number in range(each):
        a, b = number * rows, number * source
        lines = ([], [], [])
        for first in range(0, query.shape[1], DH):
            q = query[a : a + rows, first : first + DH]
            k = keys_all[b : b + source, first : first + DH]
            v = values[b : b + source, first : first + DH]
            g = grad_mixed[a : a + rows, first : first + DH]
            probs = attn_probs(q, k, mask_of(number))
            grad_probs = dot_nt(g, v)
            slope = probs * (grad_probs - jnp.sum(grad_probs * probs, -1, keepdims=True))
            slope = slope.astype(BF)
            lines[0].append((dot(slope, k) * DH ** (-0.5)).astype(BF))
            lines[1].append((dot_tn(slope, q) * DH ** (-0.5)).astype(BF))
            lines[2].append(dot_tn(probs.astype(BF), g).astype(BF))
        for out, line in zip(outs, lines, strict=True):
            out.append(jnp.concatenate(line, 1) if len(line) > 1 else line[0])
    return [jnp.concatenate(out, 0) if each > 1 else out[0] for out in outs]


class Layers:
    def __init__(self, order, head_pos, lens, enc_weights, dec_weights, gain, each):
        self.prefetch = (order, head_pos.reshape(1), lens)
        self.sides, self.gain, self.each = (enc_weights, dec_weights), gain, each
        self.dp, self.heads, self.deep, _ = enc_weights.shape
        self.width = 4 * D // self.heads
        self.unit = self.width // 4

    def weight_specs(self, side, first, stride, fixed_block=None):
        shape = (self.dp, self.heads, self.deep, self.width)
        weights = self.sides[side]
        out = [
            (
                weights,
                pl.BlockSpec(shape, lambda step, *_: (0, 0, 0, first + stride * step)),
            )
        ]
        if fixed_block is not None:
            out.append(
                (weights, pl.BlockSpec(shape, lambda step, *_: (0, 0, 0, fixed_block)))
            )
        return out

    @staticmethod
    def whole(shape):
        return pl.BlockSpec(shape, lambda *_: (0,) * len(shape))

    def call(self, kernel, phases, arrays, outs, scratch, time):
        arrays = [a if isinstance(a, tuple) else (a, self.whole(a.shape)) for a in arrays]
        return pl.pallas_call(
            kernel,
            out_shape=[jax.ShapeDtypeStruct(shape, dtype) for shape, dtype in outs],
            grid_spec=pltpu.PrefetchScalarGridSpec(
                num_scalar_prefetch=3,
                grid=(phases,),
                in_specs=[spec for _, spec in arrays],
                out_specs=[self.whole(shape) for shape, _ in outs],
                scratch_shapes=[pltpu.VMEM(shape, dtype) for shape, dtype in scratch],
            ),
            cost_estimate=cost(time),
            compiler_params=pltpu.CompilerParams(vmem_limit_bytes=VMEM_LIMIT),
        )(*self.prefetch, *[array for array, _ in arrays])

    def self_attention(self, low, w_of, kept, mask_of):
        unit = self.unit
        total = None
        for j in range(self.heads):
            w = w_of(j)
            qkv = dot(low, w[:, : 3 * unit]).astype(BF)
            mixed = attend_heads(
                qkv[:, :unit], qkv[:, unit : 2 * unit], qkv[:, 2 * unit :], self.each, mask_of
            )
            kept[j, :, : 3 * unit] = qkv
            kept[j, :, 3 * unit :] = mixed
            part = dot_nt(mixed, w[:, 3 * unit :])
            total = part if total is None else total + part
        return total

    def feed(self, low, up_of, down_of, hidden):
        total = None
        for j in range(self.heads):
            grown = jax.nn.relu(dot(low, up_of(j))).astype(BF)
            hidden[j] = grown
            part = dot_nt(grown, down_of(j))
            total = part if total is None else total + part
        return total

    def encoder(self, x):
        heads, each, width = self.heads, self.each, self.width
        rows = x.shape[0]

        def kernel(order, head, lens, x_ref, gain, w_ref, d_ref, kept, mid, hidden, last, encoded):
            step = pl.program_id(0)
            w_of = functools.partial(weights_of, w_ref, order)

            @pl.when(step == 0)
            def _():
                low = normed(x_ref[...], gain[0:1])
                mid[...] = x_ref[...] + self.self_attention(
                    low, w_of, kept, lambda n: key_mask(lens[n], rows // each)
                )

            @pl.when(step == 1)
            def _():
                low = normed(mid[...], gain[1:2])
                d_of = functools.partial(weights_of, d_ref, order)
                value = mid[...] + self.feed(low, w_of, d_of, hidden)
                last[...] = value
                encoded[...] = normed(value, gain[2:3])

        return self.call(
            kernel,
            2,
            [x, self.gain] + self.weight_specs(0, 0, 1, 2),
            [
                ((heads, rows, width), BF),
                ((rows, D), F32),
                ((heads, rows, width), BF),
                ((rows, D), F32),
                ((rows, D), BF),
            ],
            [],
            14,
        )

    def decoder(self, x, encoded):
        heads, each, unit, width = self.heads, self.each, self.unit, self.width
        rows, source = x.shape[0], encoded.shape[0]

        def kernel(order, head, lens, x_ref, enc_ref, gain, w_ref, d_ref, *refs):
            kept, one, kept_q, kept_k, two, hidden, three, final = refs
            step = pl.program_id(0)
            w_of = functools.partial(weights_of, w_ref, order)

            @pl.when(step == 0)
            def _():
                low = normed(x_ref[...], gain[3:4])
                one[...] = x_ref[...] + self.self_attention(
                    low, w_of, kept, lambda n: causal_mask(rows // each)
                )

            @pl.when(step == 1)
            def _():
                low = normed(one[...], gain[4:5])
                total = one[...]
                for j in range(heads):
                    w = w_of(j)
                    query = dot(low, w[:, :unit]).astype(BF)
                    both = dot(enc_ref[...], w[:, unit : 3 * unit]).astype(BF)
                    mixed = attend_heads(
                        query,
                        both[:, :unit],
                        both[:, unit:],
                        each,
                        lambda n: key_mask(lens[n], source // each),
                    )
                    kept_q[j, :, :unit] = query
                    kept_q[j, :, unit:] = mixed
                    kept_k[j] = both
                    total = total + dot_nt(mixed, w[:, 3 * unit :])
                two[...] = total

            @pl.when(step == 2)
            def _():
                low = normed(two[...], gain[5:6])
                d_of = functools.partial(weights_of, d_ref, order)
                value = two[...] + self.feed(low, w_of, d_of, hidden)
                three[...] = value
                final[...] = normed(value, gain[6:7] * D ** (-0.5))

        return self.call(
            kernel,
            3,
            [x, encoded, self.gain] + self.weight_specs(1, 0, 1, 3),
            [
                ((heads, rows, width), BF),
                ((rows, D), F32),
                ((heads, rows, 2 * unit), BF),
                ((heads, source, 2 * unit), BF),
                ((rows, D), F32),
                ((heads, rows, width), BF),
                ((rows, D), F32),
                ((rows, D), BF),
            ],
            [],
            16,
        )

    def feed_back(self, grad, inputs, gain_row, w_of, d_of, hidden, put):
        width = self.width
        low = grad.astype(BF)
        up_t, in_t = low.T, normed(inputs, gain_row).T
        back = None
        for j in range(self.heads):
            up, down, grown = w_of(j), d_of(j), hidden[j]
            grad_pre = jnp.where(grown > 0, dot(low, down), 0.0).astype(BF)
            put(j, 0, dot(in_t, grad_pre))
            put(j, width, dot(up_t, grown))
            part = dot_nt(grad_pre, up)
            back = part if back is None else back + part
        value, slope = norm_back(inputs, gain_row, back)
        return grad + value, slope

    def self_back(self, grad, inputs, gain_row, w_of, kept, mask_of, put):
        unit = self.unit
        low = grad.astype(BF)
        up_t, in_t = low.T, normed(inputs, gain_row).T
        back = None
        for j in range(self.heads):
            w = w_of(j)
            grad_mixed = dot(low, w[:, 3 * unit :]).astype(BF)
            slopes = attend_heads_back(
                kept[j, :, :unit],
                kept[j, :, unit : 2 * unit],
                kept[j, :, 2 * unit : 3 * unit],
                grad_mixed,
                self.each,
                mask_of,
            )
            three = jnp.concatenate(slopes, 1)
            put(j, 0, dot(in_t, three))
            put(j, 3 * unit, dot(up_t, kept[j, :, 3 * unit :]))
            part = dot_nt(three, w[:, : 3 * unit])
            back = part if back is None else back + part
        value, slope = norm_back(inputs, gain_row, back)
        return grad + value, slope

    def absolute_put(self, out_ref, order, head, base):
        def put(j, start, value):
            low = value.astype(BF)
            target = lax.rem(head[0] + j, self.heads)
            for place in range(self.dp):
                out_ref[order[place], target, :, base + start : base + start + value.shape[1]] = low[
                    place * self.deep : (place + 1) * self.deep
                ]

        return put

    def relative_put(self, keep_refs, send_ref):
        quarter = self.dp // 8

        def put(j, start, value):
            stop = start + value.shape[1]
            for place in range(self.dp):
                piece = value[place * self.deep : (place + 1) * self.deep]
                if place < 4 * quarter:
                    keep_refs[place // quarter][place % quarter, j, :, start:stop] = piece
                else:
                    send_ref[place - 4 * quarter, j, :, start:stop] = piece.astype(BF)

        return put

    def relative_outs(self, columns):
        quarter = self.dp // 8
        shape = (self.heads, self.deep, columns)
        return [((quarter,) + shape, F32)] * 4 + [((4 * quarter,) + shape, BF)]

    def flat(self, keeps_send):
        return [array.reshape(-1, array.shape[-1]) for array in keeps_send]

    def decoder_back(self, grad_final, x, encoded, kept_all):
        heads, each, unit, width = self.heads, self.each, self.unit, self.width
        kept, one, kept_q, kept_k, two, hidden, three = kept_all
        rows, source = x.shape[0], encoded.shape[0]

        def kernel(order, head, lens, *refs):
            g_ref, x_ref, enc_ref, gain, one, two, three, kept, kept_q, kept_k, hid = refs[:11]
            w_ref, d_ref, out, gains_out, grad_enc, grad_x, grad_ref = refs[11:]
            step = pl.program_id(0)
            w_of = functools.partial(weights_of, w_ref, order)

            @pl.when(step == 0)
            def _():
                gains_out[...] = jnp.zeros_like(gains_out)
                value, slope = norm_back(three[...], gain[6:7] * D ** (-0.5), g_ref[...])
                gains_out[6:7] = slope * D ** (-0.5)
                d_of = functools.partial(weights_of, d_ref, order)
                grad_ref[...], gains_out[5:6] = self.feed_back(
                    value,
                    two[...],
                    gain[5:6],
                    w_of,
                    d_of,
                    hid,
                    self.absolute_put(out, order, head, 2 * width),
                )

            @pl.when(step == 1)
            def _():
                put = self.absolute_put(out, order, head, width)
                low = grad_ref[...].astype(BF)
                up_t, in_t = low.T, normed(one[...], gain[4:5]).T
                enc_t = enc_ref[...].T
                back, back_enc = None, None
                for j in range(heads):
                    w = w_of(j)
                    grad_mixed = dot(low, w[:, 3 * unit :]).astype(BF)
                    dq, dk, dv = attend_heads_back(
                        kept_q[j, :, :unit],
                        kept_k[j, :, :unit],
                        kept_k[j, :, unit:],
                        grad_mixed,
                        each,
                        lambda n: key_mask(lens[n], source // each),
                    )
                    both = jnp.concatenate([dk, dv], 1)
                    put(j, 0, dot(in_t, dq))
                    put(j, unit, dot(enc_t, both))
                    put(j, 3 * unit, dot(up_t, kept_q[j, :, unit:]))
                    part, part_enc = dot_nt(dq, w[:, :unit]), dot_nt(both, w[:, unit : 3 * unit])
                    back = part if back is None else back + part
                    back_enc = part_enc if back_enc is None else back_enc + part_enc
                grad_enc[...] = back_enc
                value, gains_out[4:5] = norm_back(one[...], gain[4:5], back)
                grad_ref[...] += value

            @pl.when(step == 2)
            def _():
                value, gains_out[3:4] = self.self_back(
                    grad_ref[...],
                    x_ref[...],
                    gain[3:4],
                    w_of,
                    kept,
                    lambda n: causal_mask(rows // each),
                    self.absolute_put(out, order, head, 0),
                )
                grad_x[...] = value.astype(BF)

        return self.call(
            kernel,
            3,
            [grad_final, x, encoded, self.gain, one, two, three, kept, kept_q, kept_k, hidden]
            + self.weight_specs(1, 2, -1, 3),
            [
                ((self.dp, heads, self.deep, 4 * width), BF),
                ((8, D), F32),
                ((source, D), F32),
                ((rows, D), BF),
            ],
            [((rows, D), F32)],
            24,
        )

    def encoder_feed_back(self, grad_encoded, gain_grads, kept_all):
        _, mid, hidden, last = kept_all

        def kernel(order, head, lens, g_ref, more_ref, gain, mid, last, hid, w_ref, d_ref, *refs):
            *outs, grad, gains = refs
            gains[...] = more_ref[...]
            value, gains[2:3] = norm_back(last[...], gain[2:3], g_ref[...])
            grad[...], gains[1:2] = self.feed_back(
                value,
                mid[...],
                gain[1:2],
                functools.partial(weights_of, w_ref, order),
                functools.partial(weights_of, d_ref, order),
                hid,
                self.relative_put(outs[:4], outs[4]),
            )

        *outs, grad, gains = self.call(
            kernel,
            1,
            [grad_encoded, gain_grads, self.gain, mid, last, hidden] + self.weight_specs(0, 1, 0, 2),
            self.relative_outs(2 * self.width) + [(mid.shape, F32), ((8, D), F32)],
            [],
            13,
        )
        return self.flat(outs), grad, gains

    def encoder_self_back(self, grad_mid, gain_grads, x, kept, lanes):
        width = self.width
        rows = x.shape[0]

        def kernel(order, head, lens, g_ref, more_ref, x_ref, gain, kept, w_ref, *refs):
            *outs, grad_x = refs
            put = self.relative_put(outs[:4], outs[4])
            value, slope = self.self_back(
                g_ref[...],
                x_ref[...],
                gain[0:1],
                functools.partial(weights_of, w_ref, order),
                kept,
                lambda n: key_mask(lens[n], rows // self.each),
                put,
            )
            grad_x[...] = value.astype(BF)
            gains = jnp.concatenate(
                [slope, more_ref[1:8], jnp.zeros((lanes - 8, D), F32)], 0
            ).T
            for j in range(self.heads):
                put(j, width, gains)

        *outs, grad_x = self.call(
            kernel,
            1,
            [grad_mid, gain_grads, x, self.gain, kept] + self.weight_specs(0, 0, 0),
            self.relative_outs(width + lanes) + [((rows, D), BF)],
            [],
            16,
        )
        return self.flat(outs), grad_x


def body(
    dp,
    heads,
    source_ids,
    target_ids,
    source_lens,
    target_lens,
    kl_mask,
    teacher,
    *state,
):
    def transposed(group):
        embed, attn_in, attn_out, ff_in, ff_out, gains = group
        swap = functools.partial(jnp.swapaxes, axis1=-1, axis2=-2)
        return (swap(embed), attn_in, swap(attn_out), ff_in, swap(ff_out), gains)

    masters = transposed(state[:6])
    moments = transposed(state[6:12])
    seconds = transposed(state[12:])
    embed_t, attn_in, attn_out_t, ff_in, ff_out_t, gains = masters
    low = embed_t.astype(BF)
    vocab_local = embed_t.shape[1]
    head_pos = lax.axis_index("head")
    lead = (head_pos == 0).astype(F32)
    vocab_start = head_pos * vocab_local
    batch_size, source_len = source_ids.shape
    target_len = target_ids.shape[1]
    token_count = batch_size * target_len
    each = -(-batch_size // heads)
    padded = each * heads

    sides = [
        [attn_in[0, 0], attn_in[0, 1], attn_in[0, 2], attn_out_t[0], ff_in[0], ff_out_t[0]],
        [attn_in[1, 0], attn_in[1, 1], attn_in[1, 2], attn_out_t[1]]
        + [attn_in[2, 0], attn_in[2, 1], attn_in[2, 2], attn_out_t[2], ff_in[1], ff_out_t[1]],
    ]
    widths = [[matrix.shape[-1] for matrix in side] for side in sides]
    lanes = 128
    gain_rows = gains.shape[0]
    counted = jnp.full((1, gains.shape[1]), jnp.sum((target_lens > 0).astype(F32)))
    gain_block = jnp.pad(
        jnp.concatenate([gains, counted], 0).T, ((0, 0), (0, lanes - gain_rows - 1))
    )
    places = [0]
    bit = dp // 2
    while bit:
        places = places + [place ^ bit for place in places]
        bit //= 2
    order = lax.axis_index("dp") ^ jnp.array(places, jnp.int32)
    flat_in = attn_in.reshape((9,) + attn_in.shape[2:])
    arrays = [flat_in, attn_out_t, ff_in, ff_out_t, gain_block]
    enc_plan = [(0, 0), (0, 1), (0, 2), (1, 0), (2, 0), (3, 0), (4, None)]
    dec_plan = [(0, 3), (0, 4), (0, 5), (1, 1), (0, 6), (0, 7), (0, 8), (1, 2), (2, 1), (3, 1)]
    enc_packed = pack(arrays, enc_plan)
    dec_packed = pack(arrays, dec_plan)
    low, enc_packed, dec_packed = tie(low, enc_packed, dec_packed)
    table = GatherDp(low, dp)
    enc_came = gather_head(enc_packed, heads)
    if table.near:
        *table.near, enc_came[0] = tie(*table.near, *enc_came)[:3]
    enc_weights = lax.all_gather(jnp.stack(enc_came), "dp", axis=0)
    table.go_far()
    table_parts = table.parts()
    dec_came = gather_head(after(dec_packed, *enc_came[1:], *table.far), heads)

    def fill(array):
        return jnp.pad(array, ((0, padded - batch_size),) + ((0, 0),) * (array.ndim - 1))

    dec_ids = jnp.concatenate([jnp.zeros((batch_size, 1), jnp.int32), target_ids[:, :-1]], 1)
    enc_ids = jnp.roll(fill(source_ids).reshape(heads, -1), -head_pos, 0) - vocab_start
    dec_ids = jnp.roll(fill(dec_ids).reshape(heads, -1), -head_pos, 0) - vocab_start
    far_looked, table_rows = lookup(enc_ids[1:].reshape(-1), table_parts)
    own_ids = jnp.concatenate([enc_ids[0], dec_ids.reshape(-1)])
    own_looked = pick(own_ids, table_rows, [far_looked])
    dec_came[0] = after(dec_came[0], far_looked)
    dec_weights = lax.all_gather(jnp.stack(dec_came), "dp", axis=0)
    mine = each * source_len
    came = [own_looked[:mine]]
    for j in range(1, heads):
        came.append(head_shift(far_looked[(j - 1) * mine : j * mine], j, heads))
    dec_looked = own_looked[mine:]
    gain = jnp.take(enc_weights[:, 0, :, sum(widths[0]) :], order, axis=0)
    gain = gain[..., :8].astype(F32).reshape(D, 8).T
    real_count = jnp.maximum(jnp.sum(gain[gain_rows].reshape(dp, -1)[:, 0]), 1.0)
    my_lens = lax.dynamic_slice_in_dim(fill(source_lens), head_pos * each, each)
    layers = Layers(order, head_pos, my_lens, enc_weights, dec_weights, gain, each)
    enc_embed = functools.reduce(jnp.add, came).astype(F32)
    looked = after(dec_looked, enc_embed).reshape(heads, -1, D)
    *kept_enc, encoded = layers.encoder(enc_embed)
    dec_came = [looked[0]] + [head_shift(looked[j], j, heads) for j in range(1, heads)]
    dec_came[0] = after(dec_came[0], encoded)
    dec_embed = functools.reduce(jnp.add, dec_came).astype(F32)
    *kept_dec, my_final = layers.decoder(dec_embed, encoded)

    final = jnp.concatenate(gather_head(my_final, heads), 0)
    final = jnp.roll(final, head_pos * each * target_len, 0)[:token_count]
    valid = (jnp.arange(target_len)[None, :] < target_lens[:, None]).astype(F32)
    token_weight = (
        valid / (jnp.maximum(target_lens, 1).astype(F32)[:, None] * real_count)
    ).reshape(token_count)
    divergence_mask = kl_mask.astype(F32).reshape(token_count)
    labels = target_ids.reshape(token_count) - vocab_start
    labels = jnp.where((labels >= 0) & (labels < vocab_local), labels, -1)
    final_t = final.T
    teacher_t = teacher.T
    stats = logits_stats(final_t, labels, teacher_t, table_rows)
    every = jnp.stack(gather_head(stats, heads))
    peak_student = jnp.max(every[:, 0], 0)
    peak_teacher = jnp.max(every[:, 1], 0)
    off_s = every[:, 0] - peak_student
    off_t = jnp.exp((every[:, 1] - peak_teacher) / SOFTEN_FACTOR)
    sum_one = jnp.sum(every[:, 2] * jnp.exp(off_s), 0)
    sum_half = jnp.sum(every[:, 3] * jnp.exp(off_s / SOFTEN_FACTOR), 0)
    sum_teacher = jnp.sum(every[:, 4] * off_t, 0)
    sum_cross = jnp.sum(every[:, 5] * off_t, 0)
    label_logprob = jnp.sum(every[:, 6], 0)
    lse_one = peak_student + jnp.log(sum_one)
    lse_half = peak_student / SOFTEN_FACTOR + jnp.log(sum_half)
    lse_teacher = peak_teacher / SOFTEN_FACTOR + jnp.log(sum_teacher)
    cross_entropy = lse_one - label_logprob
    divergence_value = sum_cross / sum_teacher - lse_teacher + lse_half
    loss_part = lead * jnp.sum(
        token_weight
        * (
            cross_entropy
            + DIVERGENCE_SCALE * SOFTEN_FACTOR * SOFTEN_FACTOR * divergence_value * divergence_mask
        )
    )
    soft_half = DIVERGENCE_SCALE * SOFTEN_FACTOR * divergence_mask * token_weight
    soft_one = token_weight * jnp.exp(SOFTEN_FACTOR * lse_half - lse_one)
    nothing = jnp.zeros_like(lse_half)
    scalars = jnp.stack(
        [lse_half, lse_teacher, soft_one, soft_half, token_weight, nothing, nothing, nothing]
    )
    slope, part = logits_back(final_t, labels, scalars, teacher_t, table_rows, table_parts)
    part = part.T.reshape(batch_size, target_len, D)
    part = jnp.roll(fill(part).reshape(heads, each * target_len, D), -head_pos, 0)
    grad_final = scatter_head([part[j] for j in range(heads)], heads)

    dec_grads, gain_grads, grad_encoded, dec_low = layers.decoder_back(
        grad_final, dec_embed, encoded, kept_dec
    )
    dec_shard = lax.psum_scatter(dec_grads, "dp", scatter_dimension=0)
    dec_done = dec_shard
    dec_shard = lax.psum_scatter(dec_shard, "head", scatter_dimension=0)
    dec_rows = gather_head(dec_low, heads)
    feed_group, grad_mid, gain_grads = layers.encoder_feed_back(grad_encoded, gain_grads, kept_enc)
    grad_mid, *dec_rows = tie(grad_mid, *dec_rows)
    enc_scatter = ScatterDp(dp)
    enc_scatter.add(feed_group[:4], feed_group[4])
    self_group, enc_low = layers.encoder_self_back(
        grad_mid, gain_grads, enc_embed, kept_enc[0], lanes
    )

    enc_scatter.add(self_group[:4], self_group[4])
    enc_scatter.far(None)
    if enc_scatter.pieces:
        enc_low, *enc_scatter.later = tie(enc_low, *enc_scatter.later)
    enc_rows = gather_head(enc_low, heads)
    near_ids = jnp.concatenate([dec_ids.reshape(-1), enc_ids[0]])
    near_rows = jnp.concatenate(dec_rows + [enc_low], 0)
    columns = padded_to(vocab_local)
    (grad_table_t,) = spread(near_ids, near_rows, columns, final_t=final_t, slope=slope)

    def send_heads(shard):
        return [shard[0]] + [head_shift(shard[j], j, heads) for j in range(1, heads)]

    far_ids = enc_ids[1:].reshape(-1)
    far_rows = jnp.concatenate(enc_rows[1:], 0)
    enc_scatter.near(None)
    waits = [dec_done, *enc_scatter.last]
    tiles = pl.cdiv(columns, SPREAD_TILE)
    left = tiles // 4 * 2
    cut = left * SPREAD_TILE
    a, b = ScatterDp(dp), ScatterDp(dp)
    *keeps, send_a = spread(far_ids, far_rows, cut, base=grad_table_t, waits=waits)
    a.add(keeps, send_a)
    *keeps, send_b = spread(
        far_ids, far_rows, columns - cut, base=grad_table_t, first=left, waits=[send_a]
    )
    b.add(keeps, send_b)
    step = 2048
    a.far(step, [send_b])
    b.far(step, a.later[:1] if a.pieces else [])
    a.near(step)
    (enc_shard,) = enc_scatter.result(None, None, [*b.later[:1], *a.ready[:1]] if b.pieces else [])
    b.near(step, a.ready[:1])
    enc_low_shard = after(enc_shard.astype(BF), *a.last)
    enc_sums = send_heads(enc_low_shard.reshape(heads, -1, enc_shard.shape[1]))
    enc_sums[0] = enc_shard.reshape(heads, -1, enc_shard.shape[1])[0]
    g_left, left_squares = a.result(step, cut)
    if b.last:
        b.last[0], dec_shard, *enc_sums = tie(b.last[0], dec_shard, *enc_sums)
    g_right, right_squares = b.result(step, vocab_local - cut, [left_squares])
    table_squares = left_squares + right_squares
    g_dec = dec_shard.astype(F32)
    g_enc = functools.reduce(jnp.add, [value.astype(F32) for value in enc_sums])

    def squares(array, axes):
        return jnp.sum(array * array, axis=axes).reshape(-1)

    weight_squares = jnp.concatenate(
        [
            squares(embed_t, (0, 1)),
            squares(attn_in, (2, 3)),
            squares(attn_out_t, (1, 2)),
            squares(ff_in, (1, 2)),
            squares(ff_out_t, (1, 2)),
            squares(gains, (1,)) * lead,
        ]
    )
    matrix_count = weight_squares.shape[0]
    gain_at = sum(widths[0])
    unit, wide = widths[0][0], widths[0][4]
    g_gain = g_enc[:, gain_at : gain_at + gain_rows]
    grad_squares = (
        jnp.sum(g_dec * g_dec)
        + jnp.sum(g_enc[:, :gain_at] * g_enc[:, :gain_at])
        + lead * jnp.sum(g_gain * g_gain)
    )
    first_line = jnp.pad(
        jnp.concatenate([weight_squares, loss_part.reshape(1), grad_squares.reshape(1)]),
        (0, lanes - matrix_count - 2),
    ).reshape(1, lanes)
    totals = sum_all(jnp.concatenate([first_line, table_squares], 0), dp, heads)
    grad_norm = jnp.sqrt(totals[0, matrix_count + 1] + jnp.sum(totals[1:]))
    total_loss = totals[0, matrix_count]
    clip = jnp.full((8, 128), jnp.minimum(1.0, CLIP_NORM / grad_norm))
    m_table, v_table, u_table, squares_table = lamb_columns(
        (masters[0], moments[0], seconds[0]), g_left, g_right, clip, step
    )

    def flat9(array):
        return array.reshape((9,) + array.shape[2:])

    def starts(width):
        out = [0]
        for columns in width:
            out.append(out[-1] + columns)
        return out

    at_enc = [2 * wide + k * unit for k in range(4)] + [0, wide]
    at_dec = starts(widths[1])
    places = [
        [(0, at_enc[k]) for k in range(3)]
        + [(1, at_dec[k]) for k in range(3)]
        + [(1, at_dec[k]) for k in range(4, 7)],
        [(0, at_enc[3]), (1, at_dec[3]), (1, at_dec[7])],
        [(0, at_enc[4]), (1, at_dec[8])],
        [(0, at_enc[5]), (1, at_dec[9])],
    ]
    groups = [
        tuple(flat9(stack[1]) if k == 1 else stack[k] for stack in (masters, moments, seconds))
        for k in range(1, 5)
    ]
    *fresh, squares_small = lamb_matrices(clip, [g_enc, g_dec], groups, places)
    m_gain, v_gain, u_gain = lamb(gains, moments[5], seconds[5], g_gain.T, clip[0, 0])
    gain_squares = jnp.pad(squares(u_gain, (1,)) * lead, (0, lanes - gain_rows)).reshape(1, lanes)
    small_count = sum(len(matrices) for matrices in places)
    update_totals = sum_all(
        jnp.concatenate([squares_table, squares_small, gain_squares], 0), dp, heads
    )
    update_squares = jnp.concatenate(
        [
            jnp.sum(update_totals[:8]).reshape(1),
            jnp.sum(update_totals[8 : 8 + small_count], 1),
            update_totals[-1, :gain_rows],
        ]
    )
    rates = LEARN_RATE * jnp.sqrt(totals[0, :matrix_count]) / (jnp.sqrt(update_squares) + 1e-06)
    fresh_w = step_matrices(
        rates, [(group[0], update) for group, update in zip(groups, fresh[2::3], strict=True)]
    )
    fresh_w = [
        embed_t - rates[0] * u_table,
        *fresh_w,
        gains - rates[1 + small_count :].reshape(gain_rows, 1) * u_gain,
    ]
    fresh_m = [m_table] + list(fresh[0::3]) + [m_gain]
    fresh_v = [v_table] + list(fresh[1::3]) + [v_gain]
    for stack in (fresh_w, fresh_m, fresh_v):
        stack[1] = stack[1].reshape(attn_in.shape)
    return (
        total_loss.reshape(1),
        grad_norm.reshape(1),
        *transposed(fresh_w),
        *transposed(fresh_m),
        *transposed(fresh_v),
    )


def solution(mesh):
    params = (
        P("head", "dp"),
        P(None, None, "dp", "head"),
        P(None, "head", "dp"),
        P(None, "dp", "head"),
        P(None, "head", "dp"),
        P(None, "dp"),
    )
    return jax.shard_map(
        functools.partial(body, mesh.shape["dp"], mesh.shape["head"]),
        mesh=mesh,
        in_specs=(
            P("dp", None),
            P("dp", None),
            P("dp"),
            P("dp"),
            P("dp", None),
            P("dp", "head"),
            *params,
            *params,
            *params,
        ),
        out_specs=(P(), P(), *params, *params, *params),
        check_vma=False,
    )
```
